32 devices in a mesh: ctx: 8 (over y, x, core), fsdp: 4 (over z).
Axes of the slice: x: 2, y: 2, z: 4, core: 2. Of those that a mesh axis runs over, the one named last changes fastest.
Arguments:
- tokens: bfloat16 [4, 4096, 2048], P('fsdp', 'ctx'), may hold values from -6 to 6
- cotangent: bfloat16 [4, 4096, 2048], P('fsdp', 'ctx'), may hold values from -6 to 6
- kv_cotangent: bfloat16 [4, 4096, 256], P('fsdp', 'ctx'), may hold values from -6 to 6
- lengths: int32 [4], P('fsdp'), may hold values from 1024 to 4096, as said below
- block_order: int32 [4, 16], P('fsdp'), may hold values from 0 to 15, each once within a row
- w_query: bfloat16 [2048, 2048], P('fsdp'), may hold values from -0.125 to 0.125
- w_kv: bfloat16 [2048, 256], P('fsdp'), may hold values from -0.25 to 0.25
- w_out: bfloat16 [2048, 2048], P('fsdp'), may hold values from -0.375 to 0.375
- gain_attn: bfloat16 [2048], P('fsdp'), may hold values from 0.5 to 1.5
- gain_ffn: bfloat16 [2048], P('fsdp'), may hold values from 0.5 to 1.5
- w_gate: bfloat16 [2048, 5632], P(None, 'fsdp'), may hold values from -0.125 to 0.125
- w_up: bfloat16 [2048, 5632], P(None, 'fsdp'), may hold values from -0.125 to 0.125
- w_down: bfloat16 [2048, 5632], P(None, 'fsdp'), may hold values from -0.078125 to 0.078125
Outputs:
- output: bfloat16 [4, 4096, 2048], P('fsdp', 'ctx')
- input_grad: bfloat16 [4, 4096, 2048], P('fsdp', 'ctx')
- grad_w_query: float32 [2048, 2048], P(('ctx', 'fsdp'))
- grad_w_kv: float32 [2048, 256], P(('ctx', 'fsdp'))
- grad_w_out: float32 [2048, 2048], P(('ctx', 'fsdp'))
- grad_gain_attn: float32 [2048], P(('ctx', 'fsdp'))
- grad_gain_ffn: float32 [2048], P(('ctx', 'fsdp'))
- grad_w_gate: float32 [2048, 5632], P('ctx', 'fsdp')
- grad_w_up: float32 [2048, 5632], P('ctx', 'fsdp')
- grad_w_down: float32 [2048, 5632], P('ctx', 'fsdp')
The draws below stay inside these ranges and needn't reach their ends.
Inputs may be any that keep to these rules, and one draw needn't show every extreme that they name: Slot s holds one sequence of lengths[s] tokens; in every draw some slot is full. Each row is a permutation: stored block j of slot s, its tokens j * 256 to (j + 1) * 256 - 1, holds positions block_order[s, j] * 256 onward.
All inputs are finite; a program needn't handle non-finite values.
Results may differ from the reference program's by a relative error of at most 0.025.
Values may be sent and summed in bfloat16 or wider, within the bound.
No kernel may reach another device: no remote copies, remote signals or barrier semaphores. Data moves between devices by JAX's collectives and lax.ppermute only.
A program may use at most 448 MiB of HBM per device.

```python
import jax
import jax.numpy as jnp
from jax import lax

D = 2048
H = 16
HD = 128
FF = 5632
SLOT = 4096
MINLEN = 1024
SLOTS = 4
BLK = 256
N_CTX = 8


def draw_lengths(key, part):
    first_key, second_key = jax.random.split(key)
    drawn = jax.random.randint(first_key, (SLOTS,), MINLEN, SLOT + 1)
    full_slot = jax.random.randint(second_key, (), 0, SLOTS)
    return jnp.where(jnp.arange(SLOTS) == full_slot, SLOT, drawn).astype(jnp.int32)


def steps_of(stream_key, shape, pieces, least, top_value):
    loudness, own = 1.0, jax.random.fold_in(stream_key, 6)
    for axis_at, shards_of in pieces:
        heights = jnp.exp(jax.random.uniform(jax.random.fold_in(own, axis_at), (shards_of,), jnp.float32, least / len(pieces), top_value / len(pieces)))
        loudness = loudness * jnp.repeat(heights, shape[axis_at] // shards_of).reshape([-1 if axis == axis_at else 1 for axis in range(len(shape))])
    return loudness


def noise(rng, dims, spread, most, cuts=(), kind=jnp.bfloat16):
    loudness = steps_of(rng, dims, cuts, -0.22, 0.18) if cuts else 1.0
    values = jax.random.normal(rng, dims, jnp.float32) * spread * loudness
    return jnp.minimum(jnp.maximum(values, -most), most).astype(kind)


def setup_inputs(seed: int = 0) -> dict:
    keys = jax.random.split(jax.random.key(seed), 14)
    return {
        "tokens": noise(keys[0], (SLOTS, SLOT, D), 1.0, 6.0, ((0, 4), (1, 8))),
        "cotangent": noise(keys[1], (SLOTS, SLOT, D), 1.0, 6.0, ((0, 4), (1, 8))),
        "kv_cotangent": noise(keys[2], (SLOTS, SLOT, 2 * HD), 1.0, 6.0, ((0, 4), (1, 8))),
        "lengths": draw_lengths(jax.random.fold_in(keys[13], 71), 0),
        "block_order": jax.vmap(lambda own: jax.random.permutation(own, 2 * N_CTX))(jax.random.split(keys[4], SLOTS)).reshape((SLOTS, 2 * N_CTX)).astype(jnp.int32),
        "w_query": noise(keys[5], (D, H * HD), D ** -0.5, 0.125, ((0, 4),)),
        "w_kv": noise(keys[6], (D, 2 * HD), (D // 4) ** -0.5, 0.25, ((0, 4),)),
        "w_out": noise(keys[7], (H * HD, D), (H * HD // 8) ** -0.5, 0.375, ((0, 4),)),
        "gain_attn": jnp.clip(1.0 + 0.1 * jax.random.normal(keys[8], (D,), jnp.float32), 0.5, 1.5).astype(jnp.bfloat16),
        "gain_ffn": jnp.clip(1.0 + 0.1 * jax.random.normal(keys[9], (D,), jnp.float32), 0.5, 1.5).astype(jnp.bfloat16),
        "w_gate": noise(keys[10], (D, FF), D ** -0.5, 0.125, ((1, 4),)),
        "w_up": noise(keys[11], (D, FF), D ** -0.5, 0.125, ((1, 4),)),
        "w_down": noise(keys[12], (D, FF), FF ** -0.5, 0.078125, ((1, 4),)),
    }


EPSILON = 1e-05
ROPE_BASE = 10000.0
MASKED = -1e+30

@jax.custom_vjp
def low(v):
    return lax.optimization_barrier(v.astype(jnp.bfloat16)).astype(jnp.float32)

@jax.custom_vjp
def low_back(v):
    return v

def low_keep(v):
    return (low(v), None)

def low_pass(kept, grad):
    return (grad,)

def back_keep(v):
    return (v, None)

def back_low(kept, grad):
    return (low(grad),)
low.defvjp(low_keep, low_pass)
low_back.defvjp(back_keep, back_low)

def matmul(left, right):
    return jnp.dot(left, right, precision=lax.Precision.HIGHEST, preferred_element_type=jnp.float32)

def angles(positions):
    half_dim = HD // 2
    frequency = ROPE_BASE ** (-2.0 * jnp.arange(half_dim, dtype=jnp.float32) / HD)
    phase_angle = positions.astype(jnp.float32)[:, None] * frequency[None, :]
    return (jnp.cos(phase_angle), jnp.sin(phase_angle))

def rotate(vectors, cosine, sine_vals):
    half_dim = cosine.shape[-1]
    first_half = vectors[..., :half_dim]
    second_half = vectors[..., half_dim:]
    return jnp.concatenate([first_half * cosine - second_half * sine_vals, second_half * cosine + first_half * sine_vals], axis=-1)

def attend(query_rot, key_rot, values, positions, length):
    block_rows = min(512, SLOT)

    def query_block(inputs):
        query_part, query_pos = inputs
        scores = low_back(jnp.einsum('qhd,kd->qhk', query_part, key_rot, precision=lax.Precision.HIGHEST))
        allowed = (positions[None, :] <= query_pos[:, None]) & (positions[None, :] < length)
        scores = jnp.where(allowed[:, None, :], scores, MASKED)
        probability = jax.nn.softmax(scores, axis=-1)
        return jnp.einsum('qhk,kd->qhd', low(probability), values, precision=lax.Precision.HIGHEST)
    result = lax.map(jax.checkpoint(query_block), (query_rot.reshape(SLOT // block_rows, block_rows, H, HD), positions.reshape(SLOT // block_rows, block_rows)))
    return result.reshape(SLOT, H * HD)

def block_layer(slot_tokens, w_query, w_kv, w_out, gain_attn, gain_ffn, w_gate, w_up, w_down, positions, length):
    live_rows = (positions < length)[:, None]
    inverse_one = lax.rsqrt(lax.optimization_barrier(jnp.mean(slot_tokens * slot_tokens, axis=-1, keepdims=True)) + EPSILON)
    normed_attn = low(slot_tokens * inverse_one * gain_attn)
    queries = low_back(matmul(normed_attn, w_query)).reshape(SLOT, H, HD)
    key_value = low_back(matmul(normed_attn, w_kv))
    cosine, sine_vals = angles(positions)
    query_rot = low_back(low(rotate(queries, cosine[:, None, :], sine_vals[:, None, :]) * HD ** (-0.5)))
    key_rot = low_back(low(rotate(key_value[:, :HD], cosine, sine_vals)))
    values = low_back(low(key_value[:, HD:]))
    attention = low_back(low(attend(query_rot, key_rot, values, positions, length)))
    residual = slot_tokens + low_back(matmul(attention, w_out))
    inverse_two = lax.rsqrt(lax.optimization_barrier(jnp.mean(residual * residual, axis=-1, keepdims=True)) + EPSILON)
    normed_ffn = low(residual * inverse_two * gain_ffn)
    gate_proj = low_back(matmul(normed_ffn, w_gate))
    up_proj = low_back(matmul(normed_ffn, w_up))
    hidden = low_back(low(jax.nn.silu(gate_proj) * up_proj))
    ffn_out = low_back(matmul(hidden, w_down.T))
    output = jnp.where(live_rows, residual + ffn_out, 0.0)
    shared = jnp.where(live_rows, jnp.concatenate([key_rot, values], axis=-1), 0.0)
    return (output, shared)

def reference(tokens, cotangent, kv_cotangent, lengths, block_order, w_query, w_kv, w_out, gain_attn, gain_ffn, w_gate, w_up, w_down):
    weights = tuple((weight.astype(jnp.float32) for weight in (w_query, w_kv, w_out, gain_attn, gain_ffn, w_gate, w_up, w_down)))
    offsets = jnp.arange(SLOT, dtype=jnp.int32) % BLK
    positions = (jnp.repeat(block_order, BLK, axis=1) * BLK + offsets[None, :]).astype(jnp.int32)
    initial = tuple((jnp.zeros(weight.shape, jnp.float32) for weight in weights))

    def per_slot(carried, inputs):
        slot_tokens, slot_cot, slot_kv_cot, slot_pos, length = inputs

        def forward(tokens_in, *params):
            return block_layer(tokens_in, *params, slot_pos, length)
        outputs, pullback = jax.vjp(forward, slot_tokens.astype(jnp.float32), *weights)
        gradients = pullback((slot_cot.astype(jnp.float32), slot_kv_cot.astype(jnp.float32)))
        summed = tuple((running + gradient for running, gradient in zip(carried, gradients[1:])))
        return (summed, (outputs[0].astype(jnp.bfloat16), gradients[0].astype(jnp.bfloat16)))
    totals, (output, input_grad) = lax.scan(per_slot, initial, (tokens, cotangent, kv_cotangent, positions, lengths))
    return (output, input_grad, totals[0], totals[1], totals[2], totals[3], totals[4], totals[5], totals[6], totals[7])
```

```python
import functools
import jax
import jax.numpy as jnp
from jax import lax
from jax.experimental import pallas as pl
from jax.experimental.pallas import tpu as pltpu
from jax.sharding import Mesh
from jax.sharding import PartitionSpec as P

H = 16
HD = 128
MASKED = -1e30
LN2 = 0.6931471805599453

def block_places(order_ref, place_ref, own, count):
    for stored in range(count):
        relative = ((stored // 2) ^ own) * 2 + stored % 2
        place_ref[order_ref[stored]] = relative


def attend_forward(group, blk, scal_ref, order_ref, q_ref, kv_ref, out_ref, lse_ref, place_ref, qt_ref, vt_ref, acc_ref, max_ref, sum_ref):
    row_block, head_group = pl.program_id(0), pl.program_id(1)
    own, length = scal_ref[0], scal_ref[1]
    count = order_ref.shape[0]

    @pl.when((row_block == 0) & (head_group == 0))
    def _():
        block_places(order_ref, place_ref, own, count)
        for piece in range(count):
            vt_ref[:, piece * blk:(piece + 1) * blk] = kv_ref[piece * blk:(piece + 1) * blk, HD:].T

    mine = order_ref[2 * (own ^ (row_block // 2)) + row_block % 2]
    for head in range(group):
        qt_ref[:, head * blk:(head + 1) * blk] = q_ref[:, head * HD:(head + 1) * HD].T
    max_ref[...] = jnp.full(max_ref.shape, MASKED, jnp.float32)
    sum_ref[...] = jnp.zeros(sum_ref.shape, jnp.float32)
    acc_ref[...] = jnp.zeros(acc_ref.shape, jnp.float32)

    def step(place, masked):
        start = pl.multiple_of(place * blk, blk)
        scores = jnp.dot(kv_ref[pl.ds(start, blk), :HD], qt_ref[...], preferred_element_type=jnp.float32)
        if masked:
            keys = lax.broadcasted_iota(jnp.int32, (blk, blk), 0)
            rows = lax.broadcasted_iota(jnp.int32, (blk, blk), 1)
            scores = jnp.where(jnp.concatenate([keys <= rows] * group, axis=1), scores, MASKED)
        old = max_ref[...]
        new = jnp.maximum(old, jnp.max(scores, axis=0, keepdims=True))
        weights = jnp.exp2(scores - new)
        scale = jnp.exp2(old - new)
        max_ref[...] = new
        sum_ref[...] = sum_ref[...] * scale + jnp.sum(weights, axis=0, keepdims=True)
        acc_ref[...] = acc_ref[...] * scale + jnp.dot(
            vt_ref[:, pl.ds(start, blk)], weights.astype(jnp.bfloat16), preferred_element_type=jnp.float32)

    @pl.when(mine * blk < length)
    def _():
        step(place_ref[mine], True)

        def body(j, carried):
            step(place_ref[j], False)
            return carried
        lax.fori_loop(0, mine, body, 0)
        total = sum_ref[...]
        result = acc_ref[...] * (1.0 / total)
        for head in range(group):
            out_ref[:, head * HD:(head + 1) * HD] = result[:, head * blk:(head + 1) * blk].T.astype(jnp.bfloat16)
        lse_ref[0] = max_ref[...] + jnp.log2(total)

    @pl.when(mine * blk >= length)
    def _():
        out_ref[...] = jnp.zeros(out_ref.shape, jnp.bfloat16)
        lse_ref[...] = jnp.zeros(lse_ref.shape, jnp.float32)


def attention_forward(scalars, order, queries, keys_values, group, blk):
    rows, width = queries.shape
    span = keys_values.shape[0]
    row_blocks, head_groups = rows // blk, width // (group * HD)
    return pl.pallas_call(
        functools.partial(attend_forward, group, blk),
        grid_spec=pltpu.PrefetchScalarGridSpec(
            num_scalar_prefetch=2,
            grid=(row_blocks, head_groups),
            in_specs=[
                pl.BlockSpec((blk, group * HD), lambda i, g, *_: (i, g)),
                pl.BlockSpec((span, 2 * HD), lambda i, g, *_: (0, 0)),
            ],
            out_specs=[
                pl.BlockSpec((blk, group * HD), lambda i, g, *_: (i, g)),
                pl.BlockSpec((1, 1, group * blk), lambda i, g, *_: (i * head_groups + g, 0, 0)),
            ],
            scratch_shapes=[
                pltpu.SMEM((order.shape[0],), jnp.int32),
                pltpu.VMEM((HD, group * blk), jnp.bfloat16),
                pltpu.VMEM((HD, span), jnp.bfloat16),
                pltpu.VMEM((HD, group * blk), jnp.float32),
                pltpu.VMEM((1, group * blk), jnp.float32),
                pltpu.VMEM((1, group * blk), jnp.float32),
            ],
        ),
        out_shape=[
            jax.ShapeDtypeStruct((rows, width), jnp.bfloat16),
            jax.ShapeDtypeStruct((row_blocks * head_groups, 1, group * blk), jnp.float32),
        ],
        compiler_params=pltpu.CompilerParams(vmem_limit_bytes=40 * 2**20),
        cost_estimate=pl.CostEstimate(flops=3 * rows * width * span, bytes_accessed=4 * rows * width + 4 * span * HD, transcendentals=rows * span * width // HD),
        name="attend_forward",
    )(scalars, order, queries, keys_values)


def attend_backward(group, blk, scal_ref, order_ref, q_ref, g_ref, a_ref, lse_ref, kv_ref, dq_ref, dkv_ref, place_ref, qt_ref, gt_ref, qs_ref, gs_ref, kt_ref, acc_ref, delta_ref):
    row_block, head_group = pl.program_id(0), pl.program_id(1)
    own, length = scal_ref[0], scal_ref[1]
    count = order_ref.shape[0]

    @pl.when((row_block == 0) & (head_group == 0))
    def _():
        block_places(order_ref, place_ref, own, count)
        for piece in range(count):
            kt_ref[:, piece * blk:(piece + 1) * blk] = kv_ref[piece * blk:(piece + 1) * blk, :HD].T
        dkv_ref[...] = jnp.zeros(dkv_ref.shape, jnp.float32)

    mine = order_ref[2 * (own ^ (row_block // 2)) + row_block % 2]

    def step(place, masked):
        start = pl.multiple_of(place * blk, blk)
        scores = jnp.dot(kv_ref[pl.ds(start, blk), :HD], qt_ref[...], preferred_element_type=jnp.float32)
        weights = jnp.exp2(scores - lse_ref[0])
        if masked:
            keys = lax.broadcasted_iota(jnp.int32, (blk, blk), 0)
            rows = lax.broadcasted_iota(jnp.int32, (blk, blk), 1)
            weights = jnp.where(jnp.concatenate([keys <= rows] * group, axis=1), weights, 0.0)
        grads = jnp.dot(kv_ref[pl.ds(start, blk), HD:], gt_ref[...], preferred_element_type=jnp.float32)
        dscores = (weights * (grads - delta_ref[...])).astype(jnp.bfloat16)
        dkv_ref[pl.ds(start, blk), HD:] += jnp.dot(weights.astype(jnp.bfloat16), gs_ref[...], preferred_element_type=jnp.float32)
        dkv_ref[pl.ds(start, blk), :HD] += jnp.dot(dscores, qs_ref[...], preferred_element_type=jnp.float32)
        acc_ref[...] += jnp.dot(kt_ref[:, pl.ds(start, blk)], dscores, preferred_element_type=jnp.float32)

    @pl.when(mine * blk < length)
    def _():
        for head in range(group):
            lanes = slice(head * HD, (head + 1) * HD)
            cells = slice(head * blk, (head + 1) * blk)
            query, grad = q_ref[:, lanes], g_ref[:, lanes]
            qt_ref[:, cells] = query.T
            gt_ref[:, cells] = grad.T
            qs_ref[cells, :] = query
            gs_ref[cells, :] = grad
            product = grad.astype(jnp.float32) * a_ref[:, lanes].astype(jnp.float32)
            delta_ref[:, cells] = jnp.sum(product.T, axis=0, keepdims=True)
        acc_ref[...] = jnp.zeros(acc_ref.shape, jnp.float32)
        step(place_ref[mine], True)

        def body(j, carried):
            step(place_ref[j], False)
            return carried
        lax.fori_loop(0, mine, body, 0)
        for head in range(group):
            dq_ref[:, head * HD:(head + 1) * HD] = acc_ref[:, head * blk:(head + 1) * blk].T.astype(jnp.bfloat16)

    @pl.when(mine * blk >= length)
    def _():
        dq_ref[...] = jnp.zeros(dq_ref.shape, jnp.bfloat16)


def attention_backward(scalars, order, queries, grads, attended, lse, keys_values, group, blk):
    rows, width = queries.shape
    span = keys_values.shape[0]
    row_blocks, head_groups = rows // blk, width // (group * HD)
    rowspec = pl.BlockSpec((blk, group * HD), lambda i, g, *_: (i, g))
    return pl.pallas_call(
        functools.partial(attend_backward, group, blk),
        grid_spec=pltpu.PrefetchScalarGridSpec(
            num_scalar_prefetch=2,
            grid=(row_blocks, head_groups),
            in_specs=[
                rowspec, rowspec, rowspec,
                pl.BlockSpec((1, 1, group * blk), lambda i, g, *_: (i * head_groups + g, 0, 0)),
                pl.BlockSpec((span, 2 * HD), lambda i, g, *_: (0, 0)),
            ],
            out_specs=[rowspec, pl.BlockSpec((span, 2 * HD), lambda i, g, *_: (0, 0))],
            scratch_shapes=[
                pltpu.SMEM((order.shape[0],), jnp.int32),
                pltpu.VMEM((HD, group * blk), jnp.bfloat16),
                pltpu.VMEM((HD, group * blk), jnp.bfloat16),
                pltpu.VMEM((group * blk, HD), jnp.bfloat16),
                pltpu.VMEM((group * blk, HD), jnp.bfloat16),
                pltpu.VMEM((HD, span), jnp.bfloat16),
                pltpu.VMEM((HD, group * blk), jnp.float32),
                pltpu.VMEM((1, group * blk), jnp.float32),
            ],
        ),
        out_shape=[
            jax.ShapeDtypeStruct((rows, width), jnp.bfloat16),
            jax.ShapeDtypeStruct((span, 2 * HD), jnp.float32),
        ],
        compiler_params=pltpu.CompilerParams(vmem_limit_bytes=48 * 2**20),
        cost_estimate=pl.CostEstimate(flops=7 * rows * width * span, bytes_accessed=8 * rows * width + 12 * span * HD, transcendentals=rows * span * width // HD),
        name="attend_backward",
    )(scalars, order, queries, grads, attended, lse, keys_values)


EPSILON = 1e-05
ROPE_BASE = 10000.0
LOG2E = 1.4426950408889634
BF16 = jnp.bfloat16
F32 = jnp.float32


def angles(positions):
    half_dim = HD // 2
    frequency = ROPE_BASE ** (-2.0 * jnp.arange(half_dim, dtype=F32) / HD)
    phase_angle = positions.astype(F32)[:, None] * frequency[None, :]
    return (jnp.cos(phase_angle), jnp.sin(phase_angle))


def rotate(vectors, cosine, sine_vals):
    half_dim = cosine.shape[-1]
    first_half = vectors[..., :half_dim]
    second_half = vectors[..., half_dim:]
    return jnp.concatenate(
        [
            first_half * cosine - second_half * sine_vals,
            second_half * cosine + first_half * sine_vals,
        ],
        axis=-1,
    )


def matmul(left, right):
    return jnp.dot(left, right, preferred_element_type=F32)


def contract_rows(left, right):
    return lax.dot_general(left, right, (((0,), (0,)), ((), ())), preferred_element_type=F32)


def contract_cols(left, right):
    return lax.dot_general(left, right, (((1,), (1,)), ((), ())), preferred_element_type=F32)


def exchange(value, axis, distance):
    size = lax.axis_size(axis)
    return lax.ppermute(value, axis, [(i, i ^ distance) for i in range(size)])


def swap_core(value):
    return exchange(value, "core", 1)


def gather_chips(value):
    chips = lax.axis_size("chip")
    if chips != 4:
        return [value] + [exchange(value, "chip", k) for k in range(1, chips)]
    half = value.shape[0] // 2
    first, second = exchange(value, "chip", 1), exchange(value, "chip", 2)
    far = jnp.concatenate(
        [exchange(first[:half], "chip", 2), exchange(second[half:], "chip", 1)], axis=0
    )
    return [value, first, second, far]


def gather_ctx(value):
    return [piece for chunk in gather_chips(value) for piece in (chunk, swap_core(chunk))]


def reduce_chips(parts):
    chips = lax.axis_size("chip")
    if chips != 4:
        total = parts[0].astype(F32)
        for k in range(1, chips):
            total = total + exchange(parts[k].astype(BF16), "chip", k).astype(F32)
        return total
    half = parts[0].shape[0] // 2
    far = parts[3].astype(BF16)
    for_second = exchange(far[:half], "chip", 1).astype(F32)
    for_first = exchange(far[half:], "chip", 2).astype(F32)
    first = jnp.concatenate(
        [parts[1][:half].astype(F32), parts[1][half:].astype(F32) + for_first], axis=0
    ).astype(BF16)
    second = jnp.concatenate(
        [parts[2][:half].astype(F32) + for_second, parts[2][half:].astype(F32)], axis=0
    ).astype(BF16)
    return (
        parts[0].astype(F32)
        + exchange(first, "chip", 1).astype(F32)
        + exchange(second, "chip", 2).astype(F32)
    )


def reduce_depth(pieces_of):
    total = pieces_of(0).astype(F32)
    for k in range(1, lax.axis_size("fsdp")):
        total = total + exchange(pieces_of(k).astype(BF16), "fsdp", k).astype(F32)
    return total


def reduce_ctx(term_of, chips):
    order = [3, 1, 2, 0] if chips == 4 else list(range(chips))
    parts = [None] * chips
    for k in order:
        other = swap_core(term_of(2 * k + 1).astype(BF16))
        parts[k] = (term_of(2 * k) + other.astype(F32)).astype(BF16)
    return reduce_chips(parts)


def at(value, index):
    return lax.dynamic_index_in_dim(value, index, 0, keepdims=False)


def lay_columns(chunks, chip, width):
    rows = chunks[0].shape[0]
    whole = jnp.zeros((rows, width * len(chunks)), chunks[0].dtype)
    for k, chunk in enumerate(chunks):
        whole = lax.dynamic_update_slice(whole, chunk, (0, (chip ^ k) * width))
    return whole


def shards(
    tokens,
    cotangent,
    kv_cotangent,
    lengths,
    block_order,
    w_query,
    w_kv,
    w_out,
    gain_attn,
    gain_ffn,
    w_gate,
    w_up,
    w_down,
):
    local_len, model_dim = tokens.shape[1:]
    chips, planes = lax.axis_size("chip"), lax.axis_size("fsdp")
    chip, core, plane = lax.axis_index("chip"), lax.axis_index("core"), lax.axis_index("fsdp")
    own = chip * 2 + core
    places = chips * 2
    blk = local_len // 2
    order, length = block_order[0], lengths[0]
    depth = w_query.shape[0]

    kv_rows = depth // chips
    small = jnp.concatenate(
        [
            lax.dynamic_slice_in_dim(w_kv, chip * kv_rows, kv_rows, 0),
            jnp.concatenate([gain_attn, gain_ffn]).reshape(-1, 2 * HD),
        ],
        axis=0,
    )
    gain_rows = depth // (2 * HD)
    small_all = lax.all_gather(small, "fsdp", axis=0)
    gain_one = small_all[:, kv_rows : kv_rows + gain_rows].reshape(model_dim).astype(F32)
    gain_two = small_all[:, kv_rows + gain_rows :].reshape(model_dim).astype(F32)
    kv_chunks = gather_chips(small_all[:, :kv_rows])
    kv_full = jnp.zeros((planes, chips, kv_rows, 2 * HD), BF16)
    for k, chunk in enumerate(kv_chunks):
        kv_full = lax.dynamic_update_slice(kv_full, chunk[:, None], (0, chip ^ k, 0, 0))
    kv_full = kv_full.reshape(model_dim, 2 * HD)

    part = depth // 2
    wide = part * planes
    query_piece = lax.dynamic_slice(w_query, (0, chip * 2 * part + core * part), (depth, part))
    query_half = lay_columns(
        gather_chips(lax.all_gather(query_piece, "fsdp", axis=0, tiled=True)), chip, part
    )
    out_cols = model_dim // chips
    out_piece = lax.dynamic_slice(w_out, (core * part, chip * out_cols), (part, out_cols))
    out_half = lay_columns(
        gather_chips(lax.all_gather(out_piece, "fsdp", axis=0, tiled=True)), chip, out_cols
    )

    offsets = jnp.arange(blk, dtype=jnp.int32)
    mine = lax.dynamic_slice_in_dim(order, own * 2, 2, 0)
    theirs = lax.dynamic_slice_in_dim(order, (own ^ 1) * 2, 2, 0)
    both_pos = (jnp.concatenate([mine, theirs])[:, None] * blk + offsets[None, :]).reshape(-1)
    live_rows = (both_pos[:local_len] < length)[:, None]
    cosine, sine_vals = angles(both_pos)

    tokens_low = tokens[0]
    tokens_flat = tokens_low.astype(F32)
    both_tokens = jnp.concatenate([tokens_low, swap_core(tokens_low)], axis=0).astype(F32)
    both_inverse = lax.rsqrt(jnp.mean(both_tokens * both_tokens, axis=1, keepdims=True) + EPSILON)
    both_normed = (both_tokens * both_inverse * gain_one).astype(BF16)
    inverse_one = both_inverse[:local_len]

    key_value = matmul(both_normed[:local_len], kv_full)
    key_rot = rotate(key_value[:, :HD], cosine[:local_len], sine_vals[:local_len])
    local_kv = jnp.concatenate([key_rot, key_value[:, HD:]], axis=1).astype(BF16)
    slot_kv = jnp.concatenate(gather_ctx(local_kv), axis=0)

    heads = wide // HD
    queries = matmul(both_normed, query_half).reshape(2 * local_len, heads, HD)
    query_rot = rotate(queries, cosine[:, None, :], sine_vals[:, None, :]) * (
        LOG2E * HD ** (-0.5)
    )
    query_rot = query_rot.astype(BF16).reshape(2 * local_len, wide)

    scalars = jnp.stack([own, length]).astype(jnp.int32)
    attended, lse = attention_forward(scalars, order, query_rot, slot_kv, heads, blk)

    branch_other = swap_core(matmul(attended[local_len:], out_half).astype(BF16))
    residual = tokens_flat + matmul(attended[:local_len], out_half) + branch_other.astype(F32)
    inverse_two = lax.rsqrt(jnp.mean(residual * residual, axis=1, keepdims=True) + EPSILON)
    unit_two = residual * inverse_two
    normed_ffn = (unit_two * gain_two).astype(BF16)
    grad_out = jnp.where(live_rows, cotangent[0], jnp.zeros((), BF16))

    share = w_gate.shape[1] // places

    def hidden_rows(weight):
        piece = lax.dynamic_slice(weight, (0, own * share), (model_dim, share)).T
        return lax.all_gather(piece, "fsdp", axis=0, tiled=True)

    gate_rows, up_rows, down_rows = hidden_rows(w_gate), hidden_rows(w_up), hidden_rows(w_down)
    grad_chunks = gather_ctx(grad_out)
    normed_chunks = gather_ctx(normed_ffn)
    hidden_chunks, gate_chunks, up_chunks = [], [], []
    for normed, grad in zip(normed_chunks, grad_chunks):
        grad_hidden = contract_cols(grad, down_rows).astype(BF16).astype(F32)
        gate_proj = contract_cols(normed, gate_rows)
        up_proj = contract_cols(normed, up_rows)
        sigmoid_gate = jax.nn.sigmoid(gate_proj)
        silu_gate = gate_proj * sigmoid_gate
        hidden_chunks.append((silu_gate * up_proj).astype(BF16))
        gate_chunks.append(
            (grad_hidden * up_proj * sigmoid_gate * (1.0 + gate_proj * (1.0 - sigmoid_gate))).astype(BF16)
        )
        up_chunks.append((grad_hidden * silu_gate).astype(BF16))

    grad_normed = reduce_ctx(
        lambda i: matmul(gate_chunks[i], gate_rows) + matmul(up_chunks[i], up_rows), chips
    )
    ffn_out = reduce_ctx(lambda i: matmul(hidden_chunks[i], down_rows), chips)
    output = jnp.where(live_rows, residual + ffn_out, 0.0).astype(BF16)

    normed_all = jnp.concatenate(normed_chunks, axis=0)
    grad_all = jnp.concatenate(grad_chunks, axis=0)

    def ffn_gradient(left_chunks, right):
        term = contract_rows(jnp.concatenate(left_chunks, axis=0), right).astype(BF16)
        return lax.psum_scatter(term, "fsdp", scatter_dimension=0, tiled=True)

    ffn_terms = jnp.stack(
        [
            ffn_gradient(gate_chunks, normed_all),
            ffn_gradient(up_chunks, normed_all),
            ffn_gradient(hidden_chunks, grad_all),
        ]
    )
    ffn_terms = ffn_terms.reshape(3, share, places, model_dim // places)
    ffn_terms = lax.all_to_all(ffn_terms, ("chip", "core"), 2, 0, tiled=False)
    ffn_grads = ffn_terms.transpose(1, 3, 0, 2).reshape(3, model_dim // places, places * share)
    ffn_grads = ffn_grads.astype(F32)

    grad_gain_two = jnp.sum(grad_normed * unit_two, axis=0)
    scaled_two = grad_normed * gain_two
    grad_residual = grad_out.astype(F32) + inverse_two * (
        scaled_two - unit_two * jnp.mean(scaled_two * unit_two, axis=1, keepdims=True)
    )
    grad_branch = grad_residual.astype(BF16)
    both_branch = jnp.concatenate([grad_branch, swap_core(grad_branch)], axis=0)
    grad_attn = contract_cols(both_branch, out_half).astype(BF16)
    grad_query_rot, kv_terms = attention_backward(
        scalars, order, query_rot, grad_attn, attended, lse, slot_kv, heads, blk
    )

    out_terms = contract_rows(attended, both_branch).astype(BF16).reshape(planes, part, model_dim)
    out_sum = reduce_chips([at(out_terms, chip ^ k) for k in range(chips)])
    out_sum = out_sum.reshape(planes, part // planes, model_dim)
    grad_w_out = reduce_depth(lambda k: at(out_sum, plane ^ k))

    kv_terms = jnp.concatenate([kv_terms[:, :HD] * LN2, kv_terms[:, HD:]], axis=1)
    kv_terms = kv_terms.reshape(places, local_len, 2 * HD)
    kv_total = reduce_ctx(lambda i: kv_terms[i], chips) + jnp.where(
        live_rows, kv_cotangent[0].astype(F32), 0.0
    )
    kv_low = kv_total.astype(BF16).astype(F32)
    grad_key = rotate(kv_low[:, :HD], cosine[:local_len], -sine_vals[:local_len])
    grad_kv = jnp.concatenate([grad_key, kv_low[:, HD:]], axis=1).astype(BF16)
    both_grad_kv = jnp.concatenate([grad_kv, swap_core(grad_kv)], axis=0)
    kv_half = lax.dynamic_slice_in_dim(both_grad_kv, core * HD, HD, 1)
    grad_qrot = grad_query_rot.astype(F32).reshape(2 * local_len, heads, HD)
    grad_query = rotate(grad_qrot, cosine[:, None, :], -sine_vals[:, None, :]) * HD ** (-0.5)
    grad_query = grad_query.reshape(2 * local_len, wide).astype(BF16)

    kv_weight_half = lax.dynamic_slice_in_dim(kv_full, core * HD, HD, 1)

    def normed_one_term(rows):
        return contract_cols(grad_query[rows], query_half) + contract_cols(kv_half[rows], kv_weight_half)

    other_one = swap_core(normed_one_term(slice(local_len, None)).astype(BF16))
    grad_normed_one = normed_one_term(slice(0, local_len)) + other_one.astype(F32)
    unit_one = tokens_flat * inverse_one
    grad_gain_one = jnp.sum(grad_normed_one * unit_one, axis=0)
    scaled_one = grad_normed_one * gain_one
    grad_tokens = grad_residual + inverse_one * (
        scaled_one - unit_one * jnp.mean(scaled_one * unit_one, axis=1, keepdims=True)
    )

    def attn_gradient(terms):
        terms = terms.astype(BF16).reshape(chips, places * planes // chips * (depth // places), -1)
        total = reduce_chips([at(terms, chip ^ k) for k in range(chips)])
        total = total.reshape(2, planes, depth // places, -1)
        total = reduce_depth(lambda k: lax.dynamic_index_in_dim(total, plane ^ k, 1, keepdims=False))
        return at(total, core), swap_core(at(total, core ^ 1))

    def by_core(kept, other):
        return jnp.where(core == 0, jnp.stack([kept, other], -2), jnp.stack([other, kept], -2))

    kept, other = attn_gradient(contract_rows(both_normed, grad_query))
    rows = kept.shape[0]
    grad_w_query = by_core(
        kept.reshape(rows, planes, part), other.reshape(rows, planes, part)
    ).reshape(rows, model_dim)
    gains = jnp.stack([grad_gain_one, grad_gain_two], axis=1)
    kept, other = attn_gradient(
        jnp.concatenate(
            [contract_rows(both_normed, kv_half), jnp.pad(gains, ((0, 0), (0, HD - 2)))], axis=1
        )
    )
    grad_w_kv = by_core(kept[:, :HD], other[:, :HD]).reshape(rows, 2 * HD)
    gain_sums = kept[:, HD : HD + 2] + other[:, HD : HD + 2]
    return (
        output[None],
        grad_tokens.astype(BF16)[None],
        grad_w_query,
        grad_w_kv,
        grad_w_out,
        gain_sums[:, 0],
        gain_sums[:, 1],
        ffn_grads[0],
        ffn_grads[1],
        ffn_grads[2],
    )


def solution(mesh):
    ctx, planes = mesh.shape["ctx"], mesh.shape["fsdp"]
    split = Mesh(mesh.devices.reshape(ctx // 2, 2, planes), ("chip", "core", "fsdp"))
    ctx_axes = ("chip", "core")
    return jax.shard_map(
        shards,
        mesh=split,
        in_specs=(
            P("fsdp", ctx_axes, None),
            P("fsdp", ctx_axes, None),
            P("fsdp", ctx_axes, None),
            P("fsdp"),
            P("fsdp", None),
            P("fsdp", None),
            P("fsdp", None),
            P("fsdp", None),
            P("fsdp"),
            P("fsdp"),
            P(None, "fsdp"),
            P(None, "fsdp"),
            P(None, "fsdp"),
        ),
        out_specs=(
            P("fsdp", ctx_axes, None),
            P("fsdp", ctx_axes, None),
            P(("chip", "core", "fsdp"), None),
            P(("chip", "core", "fsdp"), None),
            P(("chip", "core", "fsdp"), None),
            P(("chip", "core", "fsdp")),
            P(("chip", "core", "fsdp")),
            P(ctx_axes, "fsdp"),
            P(ctx_axes, "fsdp"),
            P(ctx_axes, "fsdp"),
        ),
        check_vma=False,
    )
```

```python
import functools

import jax
import jax.numpy as jnp
from jax import lax
from jax.experimental import pallas as pl
from jax.experimental.layout import Layout, with_layout_constraint
from jax.experimental.pallas import tpu as pltpu
from jax.sharding import Mesh
from jax.sharding import PartitionSpec as P

H = 16
HD = 128
HALF = HD // 2
MASKED = -1e30
LN2 = 0.6931471805599453
LOG2E = 1.4426950408889634
EPSILON = 1e-05
ROPE_BASE = 10000.0
BF16 = jnp.bfloat16
F32 = jnp.float32


def block_places(order_ref, place_ref, own):
    count = order_ref.shape[0]
    for stored in range(count):
        relative = (stored // 2) ^ own
        place_ref[order_ref[stored]] = (relative % 2 * (count // 4) + relative // 2) * 2 + stored % 2


def causal(blk, group):
    keys = lax.broadcasted_iota(jnp.int32, (blk, blk), 0)
    rows = lax.broadcasted_iota(jnp.int32, (blk, blk), 1)
    return jnp.concatenate([keys <= rows] * group, axis=1)


def row_position(order_ref, own, row_block):
    return order_ref[2 * (own ^ (row_block // 2)) + row_block % 2]


def attend_forward(group, blk, scal_ref, order_ref, q_ref, cos_ref, sin_ref, kv_ref, out_ref, lse_ref, qt_ref, place_ref, vt_ref, acc_ref, max_ref, sum_ref):
    row_block = pl.program_id(0)
    own, length = scal_ref[0], scal_ref[1]

    @pl.when(row_block == 0)
    def _():
        block_places(order_ref, place_ref, own)
        for piece in range(order_ref.shape[0]):
            cells = slice(piece * blk, (piece + 1) * blk)
            vt_ref[:, cells] = kv_ref[cells, HD:].T

    mine = row_position(order_ref, own, row_block)

    def step(place, masked):
        start = pl.multiple_of(place * blk, blk)
        scores = jnp.dot(kv_ref[pl.ds(start, blk), :HD], qt_ref[0], preferred_element_type=F32)
        if masked:
            scores = jnp.where(causal(blk, group), scores, MASKED)
        old = max_ref[...]
        new = jnp.maximum(old, jnp.max(scores, axis=0, keepdims=True))
        weights = jnp.exp2(scores - new)
        scale = jnp.exp2(old - new)
        max_ref[...] = new
        sum_ref[...] = sum_ref[...] * scale + jnp.sum(weights, axis=0, keepdims=True)
        acc_ref[...] = acc_ref[...] * scale + jnp.dot(
            vt_ref[:, pl.ds(start, blk)], weights.astype(BF16), preferred_element_type=F32
        )

    @pl.when(mine * blk < length)
    def _():
        cosine, sine = cos_ref[...], sin_ref[...]
        for head in range(group):
            query = q_ref[:, head * HD : (head + 1) * HD].T
            first, second = query[:HALF], query[HALF:]
            turned = jnp.concatenate(
                [first * cosine - second * sine, second * cosine + first * sine], axis=0
            )
            qt_ref[0, :, head * blk : (head + 1) * blk] = (turned * (LOG2E * HD**-0.5)).astype(BF16)
        max_ref[...] = jnp.full(max_ref.shape, MASKED, F32)
        sum_ref[...] = jnp.zeros(sum_ref.shape, F32)
        acc_ref[...] = jnp.zeros(acc_ref.shape, F32)
        step(place_ref[mine], True)

        def body(j, carried):
            step(place_ref[j], False)
            return carried

        lax.fori_loop(0, mine, body, 0)
        total = sum_ref[...]
        result = acc_ref[...] * (1.0 / total)
        for head in range(group):
            out_ref[:, head * HD : (head + 1) * HD] = (
                result[:, head * blk : (head + 1) * blk].T.astype(BF16)
            )
        lse_ref[0] = max_ref[...] + jnp.log2(total)

    @pl.when(mine * blk >= length)
    def _():
        out_ref[...] = jnp.zeros(out_ref.shape, BF16)
        lse_ref[...] = jnp.zeros(lse_ref.shape, F32)
        qt_ref[...] = jnp.zeros(qt_ref.shape, BF16)


def attention_forward(scalars, order, queries, cosine, sine, keys_values, blk):
    rows, width = queries.shape
    span = keys_values.shape[0]
    row_blocks, heads = rows // blk, width // HD
    table = pl.BlockSpec((HALF, blk), lambda i, *_: (0, i))
    per_block = lambda *dims: pl.BlockSpec((1,) + dims, lambda i, *_: (i, 0, 0))
    return pl.pallas_call(
        functools.partial(attend_forward, heads, blk),
        grid_spec=pltpu.PrefetchScalarGridSpec(
            num_scalar_prefetch=2,
            grid=(row_blocks,),
            in_specs=[
                pl.BlockSpec((blk, width), lambda i, *_: (i, 0)),
                table,
                table,
                pl.BlockSpec((span, 2 * HD), lambda i, *_: (0, 0)),
            ],
            out_specs=[
                pl.BlockSpec((blk, width), lambda i, *_: (i, 0)),
                per_block(1, heads * blk),
                per_block(HD, heads * blk),
            ],
            scratch_shapes=[
                pltpu.SMEM((order.shape[0],), jnp.int32),
                pltpu.VMEM((HD, span), BF16),
                pltpu.VMEM((HD, heads * blk), F32),
                pltpu.VMEM((1, heads * blk), F32),
                pltpu.VMEM((1, heads * blk), F32),
            ],
        ),
        out_shape=[
            jax.ShapeDtypeStruct((rows, width), BF16),
            jax.ShapeDtypeStruct((row_blocks, 1, heads * blk), F32),
            jax.ShapeDtypeStruct((row_blocks, HD, heads * blk), BF16),
        ],
        compiler_params=pltpu.CompilerParams(vmem_limit_bytes=40 * 2**20),
        cost_estimate=pl.CostEstimate(flops=2**20, bytes_accessed=2**16, transcendentals=0),
        name="attend_forward",
    )(scalars, order, queries, cosine, sine, keys_values)


def attend_backward(group, blk, scal_ref, order_ref, qt_ref, g_ref, a_ref, lse_ref, cos_ref, sin_ref, kv_ref, dq_ref, dkv_ref, place_ref, gt_ref, qs_ref, gs_ref, kt_ref, acc_ref, delta_ref):
    row_block = pl.program_id(0)
    own, length = scal_ref[0], scal_ref[1]

    @pl.when(row_block == 0)
    def _():
        block_places(order_ref, place_ref, own)
        for piece in range(order_ref.shape[0]):
            cells = slice(piece * blk, (piece + 1) * blk)
            kt_ref[:, cells] = kv_ref[cells, :HD].T
        dkv_ref[...] = jnp.zeros(dkv_ref.shape, F32)

    mine = row_position(order_ref, own, row_block)

    def step(place, masked):
        start = pl.multiple_of(place * blk, blk)
        scores = jnp.dot(kv_ref[pl.ds(start, blk), :HD], qt_ref[0], preferred_element_type=F32)
        weights = jnp.exp2(scores - lse_ref[0])
        if masked:
            weights = jnp.where(causal(blk, group), weights, 0.0)
        grads = jnp.dot(kv_ref[pl.ds(start, blk), HD:], gt_ref[...], preferred_element_type=F32)
        dscores = (weights * (grads - delta_ref[...])).astype(BF16)
        dkv_ref[pl.ds(start, blk), HD:] += jnp.dot(
            weights.astype(BF16), gs_ref[...], preferred_element_type=F32
        )
        dkv_ref[pl.ds(start, blk), :HD] += jnp.dot(dscores, qs_ref[...], preferred_element_type=F32)
        acc_ref[...] += jnp.dot(kt_ref[:, pl.ds(start, blk)], dscores, preferred_element_type=F32)

    @pl.when(mine * blk < length)
    def _():
        for head in range(group):
            lanes = slice(head * HD, (head + 1) * HD)
            cells = slice(head * blk, (head + 1) * blk)
            grad = g_ref[:, lanes]
            gt_ref[:, cells] = grad.T
            qs_ref[cells, :] = qt_ref[0, :, cells].T
            gs_ref[cells, :] = grad
            product = grad.astype(F32) * a_ref[:, lanes].astype(F32)
            delta_ref[:, cells] = jnp.sum(product.T, axis=0, keepdims=True)
        acc_ref[...] = jnp.zeros(acc_ref.shape, F32)
        step(place_ref[mine], True)

        def body(j, carried):
            step(place_ref[j], False)
            return carried

        lax.fori_loop(0, mine, body, 0)
        cosine, sine = cos_ref[...], sin_ref[...]
        for head in range(group):
            turned = acc_ref[:, head * blk : (head + 1) * blk].astype(BF16).astype(F32)
            first, second = turned[:HALF], turned[HALF:]
            grad = jnp.concatenate(
                [first * cosine + second * sine, second * cosine - first * sine], axis=0
            )
            dq_ref[:, head * HD : (head + 1) * HD] = (grad * HD**-0.5).T.astype(BF16)

    @pl.when(mine * blk >= length)
    def _():
        dq_ref[...] = jnp.zeros(dq_ref.shape, BF16)


def attention_backward(scalars, order, turned, grads, attended, lse, cosine, sine, keys_values, blk, group, which):
    rows = grads.shape[0]
    span = keys_values.shape[0]
    row_blocks = rows // blk
    table = pl.BlockSpec((HALF, blk), lambda i, *_: (0, i))
    rowspec = pl.BlockSpec((blk, group * HD), lambda i, *_: (i, which))
    per_block = lambda *dims: pl.BlockSpec((1,) + dims, lambda i, *_: (i, 0, which))
    return pl.pallas_call(
        functools.partial(attend_backward, group, blk),
        grid_spec=pltpu.PrefetchScalarGridSpec(
            num_scalar_prefetch=2,
            grid=(row_blocks,),
            in_specs=[
                per_block(HD, group * blk),
                rowspec,
                rowspec,
                per_block(1, group * blk),
                table,
                table,
                pl.BlockSpec((span, 2 * HD), lambda i, *_: (0, 0)),
            ],
            out_specs=[
                pl.BlockSpec((blk, group * HD), lambda i, *_: (i, 0)),
                pl.BlockSpec((span, 2 * HD), lambda i, *_: (0, 0)),
            ],
            scratch_shapes=[
                pltpu.SMEM((order.shape[0],), jnp.int32),
                pltpu.VMEM((HD, group * blk), BF16),
                pltpu.VMEM((group * blk, HD), BF16),
                pltpu.VMEM((group * blk, HD), BF16),
                pltpu.VMEM((HD, span), BF16),
                pltpu.VMEM((HD, group * blk), F32),
                pltpu.VMEM((1, group * blk), F32),
            ],
        ),
        out_shape=[
            jax.ShapeDtypeStruct((rows, group * HD), BF16),
            jax.ShapeDtypeStruct((span, 2 * HD), F32),
        ],
        compiler_params=pltpu.CompilerParams(vmem_limit_bytes=48 * 2**20),
        cost_estimate=pl.CostEstimate(flops=2**20, bytes_accessed=2**16, transcendentals=0),
        name="attend_backward",
    )(scalars, order, turned, grads, attended, lse, cosine, sine, keys_values)


def ffn_rows(count, tiles, place_ref, xa_ref, xb_ref, ga_ref, gb_ref, gate_ref, up_ref, down_ref, *rest):
    back_a, back_b, out_a, out_b, x_all, g_all, hidden_all, dgate_all, dup_all = rest[count:]
    units = gate_ref.shape[0] * gate_ref.shape[2]
    gate_rows, up_rows, down_rows = (ref[...].reshape(units, -1) for ref in (gate_ref, up_ref, down_ref))
    nt = (((1,), (1,)), ((), ()))
    early = pl.program_id(0) < tiles
    x = jnp.where(early, xa_ref[...], xb_ref[...])
    grad = jnp.where(early, ga_ref[...], gb_ref[...])
    gate = lax.dot_general(x, gate_rows, nt, preferred_element_type=F32)
    up = lax.dot_general(x, up_rows, nt, preferred_element_type=F32)
    dhidden = lax.dot_general(grad, down_rows, nt, preferred_element_type=F32)
    dhidden = dhidden.astype(BF16).astype(F32)
    sigmoid = jax.nn.sigmoid(gate)
    silu = gate * sigmoid
    hidden = (silu * up).astype(BF16)
    dgate = (dhidden * up * sigmoid * (1.0 + gate * (1.0 - sigmoid))).astype(BF16)
    dup = (dhidden * silu).astype(BF16)
    back = (
        jnp.dot(dgate, gate_rows, preferred_element_type=F32)
        + jnp.dot(dup, up_rows, preferred_element_type=F32)
    ).astype(BF16)
    out = jnp.dot(hidden, down_rows, preferred_element_type=F32).astype(BF16)
    x_all[...] = x
    g_all[...] = grad
    hidden_all[...] = hidden
    dgate_all[...] = dgate
    dup_all[...] = dup

    @pl.when(early)
    def _():
        back_a[...] = back
        out_a[...] = out

    @pl.when(jnp.logical_not(early))
    def _():
        back_b[...] = back
        out_b[...] = out


def ffn_pair(place, pairs, xa, xb, ga, gb, weights, kept):
    rows, model_dim = xa.shape
    planes, _, share, _ = weights.shape
    units = planes * share
    tile = min(256, rows)
    tiles = rows // tile
    weight = lambda which: pl.BlockSpec(
        (planes, 1, share, model_dim), lambda i, *_: (0, which, 0, 0), pipeline_mode=pl.Buffered(1)
    )
    turn_a = lambda i: jnp.minimum(i, tiles - 1)
    turn_b = lambda i: jnp.maximum(i - tiles, 0)
    block = lambda index: pl.BlockSpec((tile, model_dim), index)
    here_a, here_b = block(lambda i, *_: (turn_a(i), 0)), block(lambda i, *_: (turn_b(i), 0))
    out_a = block(lambda i, place_ref: (place_ref[0] * tiles + turn_a(i), 0))
    out_b = block(lambda i, place_ref: (place_ref[0] * tiles + turn_b(i), 0))
    there = lambda wide: pl.BlockSpec((tile, wide), lambda i, place_ref: (place_ref[0] * 2 * tiles + i, 0))
    count = len(kept)
    shape = lambda tall, wide: jax.ShapeDtypeStruct((tall, wide), BF16)
    return pl.pallas_call(
        functools.partial(ffn_rows, count, tiles),
        grid_spec=pltpu.PrefetchScalarGridSpec(
            num_scalar_prefetch=1,
            grid=(2 * tiles,),
            in_specs=[here_a, here_b, out_a, out_b, weight(0), weight(1), weight(2)]
            + [pl.BlockSpec(memory_space=pl.ANY)] * count,
            out_specs=[here_a, here_b, out_a, out_b] + [there(model_dim)] * 2 + [there(units)] * 3,
        ),
        out_shape=[shape(rows, model_dim)] * 2
        + [shape(pairs * rows, model_dim)] * 2
        + [shape(pairs * 2 * rows, model_dim)] * 2
        + [shape(pairs * 2 * rows, units)] * 3,
        input_output_aliases={8 + i: 2 + i for i in range(count)},
        compiler_params=pltpu.CompilerParams(vmem_limit_bytes=52 * 2**20),
        cost_estimate=pl.CostEstimate(flops=2**20, bytes_accessed=2**16, transcendentals=0),
        name="ffn_pair",
    )(place, xa, xb, ga, gb, weights, weights, weights, *kept)


def angles(positions):
    frequency = ROPE_BASE ** (-2.0 * jnp.arange(HALF, dtype=F32) / HD)
    phase_angle = frequency[:, None] * positions.astype(F32)[None, :]
    return (jnp.cos(phase_angle), jnp.sin(phase_angle))


def rotate(vectors, cosine, sine_vals):
    first_half = vectors[..., :HALF]
    second_half = vectors[..., HALF:]
    return jnp.concatenate(
        [
            first_half * cosine - second_half * sine_vals,
            second_half * cosine + first_half * sine_vals,
        ],
        axis=-1,
    )


def matmul(left, right):
    return jnp.dot(left, right, preferred_element_type=F32)


def contract_rows(left, right):
    return lax.dot_general(left, right, (((0,), (0,)), ((), ())), preferred_element_type=F32)


def contract_cols(left, right):
    return lax.dot_general(left, right, (((1,), (1,)), ((), ())), preferred_element_type=F32)


def after(value, *earlier):
    return lax.optimization_barrier((value, earlier))[0]


def exchange(value, axis, distance):
    size = lax.axis_size(axis)
    return lax.ppermute(value, axis, [(i, i ^ distance) for i in range(size)])


def swap_core(value):
    return exchange(value, "core", 1)


def spread_chips(value):
    return [value] + [exchange(value, "chip", k) for k in range(1, lax.axis_size("chip"))]


def gather_near(value):
    if lax.axis_size("chip") != 4:
        return spread_chips(value)
    return [value, exchange(value, "chip", 1), exchange(value, "chip", 2)]


def send_far(near):
    if lax.axis_size("chip") != 4:
        return ()
    value, first, second = near
    half = value.shape[0] // 2
    return exchange(first[:half], "chip", 2), exchange(second[half:], "chip", 1)


def gather_far(near):
    halves = send_far(near)
    return near + [jnp.concatenate(halves, axis=0)] if halves else near


def gather_chips(value):
    return gather_far(gather_near(value))


def add_cores(terms, terms_of_other):
    return (terms.astype(F32) + swap_core(terms_of_other.astype(BF16)).astype(F32)).astype(BF16)


def deal(terms, axis):
    dealt = lax.all_to_all(terms.astype(BF16), axis, 0, 0, tiled=False)
    return jnp.sum(dealt.astype(F32), axis=0)


def at(value, index, axis=0):
    return lax.dynamic_index_in_dim(value, index, axis, keepdims=False)


def sum_planes(terms, plane):
    total = at(terms, plane).astype(F32)
    for k in range(1, lax.axis_size("fsdp")):
        total = total + exchange(at(terms, plane ^ k).astype(BF16), "fsdp", k).astype(F32)
    return total


def reduce_far(last):
    half = last.shape[0] // 2
    return exchange(last[:half], "chip", 1), exchange(last[half:], "chip", 2)


def add_half(term, passing, which):
    half = passing.shape[0]
    first, second = term[:half].astype(F32), term[half:].astype(F32)
    if which == 0:
        first = first + passing.astype(F32)
    else:
        second = second + passing.astype(F32)
    return jnp.concatenate([first, second], axis=0).astype(BF16)


def lay_columns(chunks, chip):
    rows, width = chunks[0].shape
    whole = jnp.zeros((rows, width * len(chunks)), chunks[0].dtype)
    for k, chunk in enumerate(chunks):
        whole = lax.dynamic_update_slice(whole, chunk, (0, (chip ^ k) * width))
    return whole


def shards(
    tokens,
    cotangent,
    kv_cotangent,
    lengths,
    block_order,
    w_query,
    w_kv,
    w_out,
    gain_attn,
    gain_ffn,
    w_gate,
    w_up,
    w_down,
):
    local_len, model_dim = tokens.shape[1:]
    chips, planes = lax.axis_size("chip"), lax.axis_size("fsdp")
    chip, core, plane = lax.axis_index("chip"), lax.axis_index("core"), lax.axis_index("fsdp")
    own = chip * 2 + core
    places = chips * 2
    blk = local_len // 2
    order, length = block_order[0], lengths[0]
    depth = w_query.shape[0]

    part = depth // 2
    wide = part * planes
    out_cols = model_dim // chips
    kv_rows = depth // chips
    gain_rows = depth // (2 * HD)
    narrow = lambda value: value.reshape(-1, 2 * HD)
    pieces = [
        lax.dynamic_slice(w_query, (0, chip * 2 * part + core * part), (depth, part)),
        lax.dynamic_slice(w_out, (core * part, chip * out_cols), (part, out_cols)),
        lax.dynamic_slice_in_dim(w_kv, chip * kv_rows, kv_rows, 0),
        gain_attn,
        gain_ffn,
    ]
    heights = [piece.size // (2 * HD) for piece in pieces]
    packed = jnp.concatenate([narrow(piece) for piece in pieces], axis=0)
    packed = lax.all_gather(packed, "fsdp", axis=0)
    bounds = [sum(heights[: i + 1]) for i in range(4)]
    query_piece, out_piece, kv_piece, gain_one, gain_two = jnp.split(packed, bounds, axis=1)
    share = w_gate.shape[1] // places
    pieces = jnp.stack(
        [
            lax.dynamic_slice(weight, (0, own * share), (model_dim, share)).T
            for weight in (w_gate, w_up, w_down)
        ]
    )
    ffn_weights = lax.all_gather(pieces, "fsdp", axis=0)
    query_piece = query_piece.reshape(model_dim, part)
    out_piece = out_piece.reshape(wide, out_cols)
    gain_one = gain_one.reshape(model_dim).astype(F32)
    gain_two = gain_two.reshape(model_dim).astype(F32)
    kv_full = jnp.zeros((planes, chips, kv_rows, 2 * HD), BF16)
    kv_chunks = gather_chips(kv_piece)
    for k, chunk in enumerate(kv_chunks):
        kv_full = lax.dynamic_update_slice(kv_full, chunk[:, None], (0, chip ^ k, 0, 0))
    kv_full = with_layout_constraint(kv_full.reshape(model_dim, 2 * HD), Layout((0, 1)))

    own_pos = jnp.repeat(lax.dynamic_slice_in_dim(order, own * 2, 2, 0) * blk, blk) + (
        jnp.arange(local_len, dtype=jnp.int32) % blk
    )
    live_rows = (own_pos < length)[:, None]
    grad_out = jnp.where(live_rows, cotangent[0], jnp.zeros((), BF16))
    grad_near = after(gather_near(grad_out), pieces)
    query_piece = after(query_piece, kv_chunks, grad_near)
    query_half = lay_columns(gather_chips(query_piece), chip)
    out_chunks = spread_chips(after(out_piece, query_half))
    grad_far = send_far(after(grad_near, query_half))

    offsets = jnp.arange(blk, dtype=jnp.int32)
    mine = lax.dynamic_slice_in_dim(order, own * 2, 2, 0)
    theirs = lax.dynamic_slice_in_dim(order, (own ^ 1) * 2, 2, 0)
    both_pos = (jnp.concatenate([mine, theirs])[:, None] * blk + offsets[None, :]).reshape(-1)
    cosine, sine_vals = angles(both_pos)
    own_cosine, own_sine = cosine[:, :local_len].T, sine_vals[:, :local_len].T

    tokens_low = tokens[0]
    tokens_flat = tokens_low.astype(F32)
    both_tokens = jnp.concatenate([tokens_low, swap_core(tokens_low)], axis=0).astype(F32)
    both_inverse = lax.rsqrt(jnp.mean(both_tokens * both_tokens, axis=1, keepdims=True) + EPSILON)
    both_normed = (both_tokens * both_inverse * gain_one).astype(BF16)
    inverse_one = both_inverse[:local_len]

    key_value = matmul(both_normed[:local_len], kv_full)
    key_rot = rotate(key_value[:, :HD], own_cosine, own_sine)
    local_kv = jnp.concatenate([key_rot, key_value[:, HD:]], axis=1).astype(BF16)
    slot_kv = jnp.concatenate(gather_chips(local_kv), axis=0)
    slot_kv = jnp.concatenate([slot_kv, swap_core(slot_kv)], axis=0)

    heads = wide // HD
    queries = matmul(both_normed, query_half)
    scalars = jnp.stack([own, length]).astype(jnp.int32)
    attended, lse, turned = attention_forward(
        scalars, order, queries, cosine, sine_vals, slot_kv, blk
    )

    attended, lse, turned, out_chunks, grad_far = lax.optimization_barrier(
        (attended, lse, turned, out_chunks, grad_far)
    )
    grad_mine = jnp.concatenate(list(grad_near) + ([jnp.concatenate(grad_far, axis=0)] if grad_far else []), axis=0)
    grad_other = swap_core(grad_mine)
    out_half = lay_columns(out_chunks, chip)
    branch_other = swap_core(matmul(attended[local_len:], out_half).astype(BF16))
    residual = tokens_flat + matmul(attended[:local_len], out_half) + branch_other.astype(F32)
    inverse_two = lax.rsqrt(jnp.mean(residual * residual, axis=1, keepdims=True) + EPSILON)
    unit_two = residual * inverse_two
    normed_ffn = (unit_two * gain_two).astype(BF16)
    def pair(at_place, chunk, kept):
        result = ffn_pair(
            jnp.full((1,), at_place, jnp.int32),
            chips,
            chunk,
            swap_core(chunk),
            grad_mine,
            grad_other,
            ffn_weights,
            kept,
        )
        return result[0], result[1], tuple(result[2:])

    normed_near = gather_near(normed_ffn)
    back_own, back_other, kept = pair(0, normed_near[0], ())
    back_other = swap_core(back_other)
    if chips == 4:
        normed_near = after(normed_near, back_own)
        normed_far = send_far(normed_near)
        own_first, other_first, kept = pair(1, normed_near[1], kept)
        normed_far = after(normed_far, own_first)
        own_last, other_last, kept = pair(3, jnp.concatenate(normed_far, axis=0), kept)
        last = add_cores(own_last, other_last)
        first = add_cores(own_first, other_first)
        kept = after(kept, last, first)
        passing = reduce_far(last)
        own_second, other_second, kept = pair(2, normed_near[2], kept)
        passing, own_second, other_second, kept = lax.optimization_barrier(
            (passing, own_second, other_second, kept)
        )
        first = add_half(first, passing[1], 1)
        second = add_half(add_cores(own_second, other_second), passing[0], 0)
        kept = after(kept, first, second)
        arrived = [exchange(first, "chip", 1), exchange(second, "chip", 2), back_other]
    else:
        normed_chunks = gather_far(after(normed_near, back_own))
        arrived = [back_other]
        for k in range(1, chips):
            own_term, other_term, kept = pair(k, normed_chunks[k], kept)
            arrived.append(exchange(add_cores(own_term, other_term), "chip", k))

    out_own, out_other, normed_all, grad_all, hidden_all, dgate_all, dup_all = kept
    down_term = contract_rows(hidden_all, grad_all).astype(BF16)
    out_parts = add_cores(out_own, out_other).reshape(chips, local_len, model_dim)
    gate_term = contract_rows(dgate_all, normed_all).astype(BF16)
    arrived = after(arrived, down_term, out_parts, gate_term)
    grad_normed = back_own.astype(F32)
    for term in arrived:
        grad_normed = grad_normed + term.astype(F32)
    out_parts = after(out_parts, arrived)

    def over_planes(term):
        return lax.psum_scatter(term, "fsdp", scatter_dimension=0, tiled=True)

    gate_term, down_term = over_planes(gate_term), over_planes(down_term)

    grad_gain_two = jnp.sum(grad_normed * unit_two, axis=0)
    scaled_two = grad_normed * gain_two
    grad_residual = grad_out.astype(F32) + inverse_two * (
        scaled_two - unit_two * jnp.mean(scaled_two * unit_two, axis=1, keepdims=True)
    )
    grad_branch = grad_residual.astype(BF16)
    both_branch = jnp.concatenate([grad_branch, swap_core(grad_branch)], axis=0)
    grad_attn = contract_cols(both_branch, out_half).astype(BF16)
    branch_terms = contract_rows(attended, both_branch).astype(BF16)
    branch_terms = branch_terms.reshape(planes, part, model_dim)
    grad_attn = after(grad_attn, branch_terms)
    group = heads // 2

    def backward(grads, which):
        return attention_backward(
            scalars, order, turned, grads, attended, lse, cosine, sine_vals, slot_kv, blk, group, which
        )

    def deal_rows(terms):
        terms = terms.reshape(chips, 2 * planes * (depth // places), -1)
        return lax.all_to_all(terms, "chip", 0, 0, tiled=False)

    def by_plane(dealt):
        total = jnp.sum(dealt.astype(F32), axis=0)
        return total.reshape(2, planes, depth // places, -1).swapaxes(0, 1)

    branch_dealt = lax.all_to_all(branch_terms, "chip", 0, 0, tiled=False)
    up_term = contract_rows(*after((dup_all, normed_all), branch_terms)).astype(BF16)
    if chips == 4:
        out_passing = reduce_far(out_parts[3])
    else:
        out_passing = ()
    grad_query_a, kv_terms_a = backward(after(grad_attn, up_term), 0)
    grad_query_a, kv_terms_a, out_passing, branch_dealt = lax.optimization_barrier(
        (grad_query_a, kv_terms_a, out_passing, branch_dealt)
    )
    branch_sum = jnp.sum(branch_dealt.astype(F32), axis=0)
    query_terms_a = contract_rows(both_normed, grad_query_a).astype(BF16)
    if chips == 4:
        out_near = (add_half(out_parts[1], out_passing[1], 1), add_half(out_parts[2], out_passing[0], 0))
    else:
        out_near = tuple(out_parts[k] for k in range(1, chips))
    branch_sum = branch_sum.reshape(planes, part // planes, model_dim)
    grad_query_b, kv_terms_b = backward(after(grad_attn, out_near, query_terms_a, branch_sum), 1)
    out_arrived = [exchange(term, "chip", k + 1) for k, term in enumerate(out_near)]
    grad_w_out = sum_planes(branch_sum, plane)
    query_sums_a = deal_rows(query_terms_a)
    ffn_terms = [gate_term, over_planes(up_term), down_term]
    grad_query_b, kv_terms_b, out_arrived, grad_w_out, query_sums_a, ffn_terms = lax.optimization_barrier(
        (grad_query_b, kv_terms_b, out_arrived, grad_w_out, query_sums_a, ffn_terms)
    )
    kv_terms = kv_terms_a + kv_terms_b
    kv_terms = jnp.concatenate([kv_terms[:, :HD] * LN2, kv_terms[:, HD:]], axis=1)
    kv_terms = kv_terms.reshape(2, chips * local_len, 2 * HD)
    kv_parts = add_cores(kv_terms[0], kv_terms[1]).reshape(chips, local_len, 2 * HD)
    kv_arrived = [exchange(kv_parts[k], "chip", k) for k in range(1, chips)]
    query_terms_b = contract_rows(*after((both_normed, grad_query_b), kv_parts)).astype(BF16)
    kv_arrived = after(kv_arrived, query_terms_b)
    ffn_terms = jnp.stack(ffn_terms).reshape(3, share, places, model_dim // places)
    ffn_terms = lax.all_to_all(ffn_terms, ("chip", "core"), 2, 0, tiled=False)
    kv_arrived, ffn_terms = lax.optimization_barrier((kv_arrived, ffn_terms))
    query_sums_b = deal_rows(after(query_terms_b, kv_arrived))
    kv_total = kv_parts[0].astype(F32)
    for term in kv_arrived:
        kv_total = kv_total + term.astype(F32)
    kv_total = kv_total + jnp.where(live_rows, kv_cotangent[0].astype(F32), 0.0)
    kv_low = kv_total.astype(BF16).astype(F32)
    grad_key = rotate(kv_low[:, :HD], own_cosine, -own_sine)
    grad_kv = jnp.concatenate([grad_key, kv_low[:, HD:]], axis=1).astype(BF16)
    both_grad_kv = jnp.concatenate([grad_kv, swap_core(grad_kv)], axis=0)
    kv_half = lax.dynamic_slice_in_dim(both_grad_kv, core * HD, HD, 1)
    kv_weight_half = lax.dynamic_slice_in_dim(kv_full, core * HD, HD, 1)
    both_query = jnp.concatenate([grad_query_a, grad_query_b], axis=1)

    def normed_one_term(rows):
        return contract_cols(both_query[rows], query_half) + contract_cols(kv_half[rows], kv_weight_half)

    other_one = swap_core(normed_one_term(slice(local_len, None)).astype(BF16))
    gains = jnp.pad(grad_gain_two[:, None], ((0, 0), (0, HD - 1)))
    kv_grads = jnp.concatenate([contract_rows(both_normed, kv_half), gains], axis=1).astype(BF16)
    kv_grads = kv_grads.reshape(chips, 2 * planes * (depth // places), 2 * HD)
    kv_sent = [exchange(at(kv_grads, chip ^ k), "chip", k) for k in range(1, chips)]

    query_sums_b = after(query_sums_b, kv_grads)
    query_sums = jnp.concatenate([by_plane(query_sums_a), by_plane(query_sums_b)], axis=3)
    query_sums = sum_planes(query_sums, plane)

    grad_normed_one = normed_one_term(slice(0, local_len)) + other_one.astype(F32)
    unit_one = tokens_flat * inverse_one
    scaled_one = grad_normed_one * gain_one
    grad_tokens = grad_residual + inverse_one * (
        scaled_one - unit_one * jnp.mean(scaled_one * unit_one, axis=1, keepdims=True)
    )
    grad_tokens = grad_tokens.astype(BF16)
    ffn_out = out_parts[0].astype(F32)
    for term in out_arrived:
        ffn_out = ffn_out + term.astype(F32)
    output = jnp.where(live_rows, residual + ffn_out, 0.0).astype(BF16)

    kv_sent = after(kv_sent, grad_tokens)
    kv_sums = at(kv_grads, chip).astype(F32)
    for term in kv_sent:
        kv_sums = kv_sums + term.astype(F32)
    kv_sums = kv_sums.reshape(2, planes, depth // places, 2 * HD).swapaxes(0, 1)
    kv_sums = sum_planes(kv_sums, plane)

    rows = depth // places
    own_rows = [((chip * 2 + j) * planes + plane) * rows for j in range(2)]
    gain_sums = jnp.stack(
        [
            jnp.sum(lax.dynamic_slice_in_dim(query_half, row, rows, 0).astype(F32) * query_sums[j], axis=1)
            + jnp.sum(
                lax.dynamic_slice_in_dim(kv_weight_half, row, rows, 0).astype(F32) * kv_sums[j, :, :HD],
                axis=1,
            )
            for j, row in enumerate(own_rows)
        ]
    )
    kv_sums = lax.dynamic_update_slice(kv_sums, gain_sums[:, :, None], (0, 0, HD + 1))

    def by_core(sums):
        kept, other = at(sums, core), swap_core(at(sums, core ^ 1))
        return jnp.where(core == 0, kept, other), jnp.where(core == 0, other, kept)

    first, second = by_core(query_sums)
    grad_w_query = jnp.stack(
        [first.reshape(rows, planes, part), second.reshape(rows, planes, part)], axis=2
    ).reshape(rows, model_dim)
    first, second = by_core(kv_sums)
    grad_w_kv = jnp.concatenate([first[:, :HD], second[:, :HD]], axis=1)
    gain_sums = first[:, HD : HD + 2] + second[:, HD : HD + 2]
    grad_gain_two = gain_sums[:, 0]
    grad_gain_one = gain_sums[:, 1] / lax.dynamic_slice_in_dim(gain_one, (own * planes + plane) * rows, rows, 0)
    ffn_grads = ffn_terms.transpose(1, 3, 0, 2).reshape(3, model_dim // places, places * share)
    ffn_grads = ffn_grads.astype(F32)
    return (
        output[None],
        grad_tokens.astype(BF16)[None],
        grad_w_query,
        grad_w_kv,
        grad_w_out,
        grad_gain_one,
        grad_gain_two,
        ffn_grads[0],
        ffn_grads[1],
        ffn_grads[2],
    )


def solution(mesh):
    ctx, planes = mesh.shape["ctx"], mesh.shape["fsdp"]
    split = Mesh(mesh.devices.reshape(ctx // 2, 2, planes), ("chip", "core", "fsdp"))
    ctx_axes = ("chip", "core")
    return jax.shard_map(
        shards,
        mesh=split,
        in_specs=(
            P("fsdp", ctx_axes, None),
            P("fsdp", ctx_axes, None),
            P("fsdp", ctx_axes, None),
            P("fsdp"),
            P("fsdp", None),
            P("fsdp", None),
            P("fsdp", None),
            P("fsdp", None),
            P("fsdp"),
            P("fsdp"),
            P(None, "fsdp"),
            P(None, "fsdp"),
            P(None, "fsdp"),
        ),
        out_specs=(
            P("fsdp", ctx_axes, None),
            P("fsdp", ctx_axes, None),
            P(("chip", "core", "fsdp"), None),
            P(("chip", "core", "fsdp"), None),
            P(("chip", "core", "fsdp"), None),
            P(("chip", "core", "fsdp")),
            P(("chip", "core", "fsdp")),
            P(ctx_axes, "fsdp"),
            P(ctx_axes, "fsdp"),
            P(ctx_axes, "fsdp"),
        ),
        check_vma=False,
    )
```

```python
import functools

import jax
import jax.numpy as jnp
from jax import lax
from jax.experimental import pallas as pl
from jax.experimental.layout import Layout, with_layout_constraint
from jax.experimental.pallas import tpu as pltpu
from jax.sharding import Mesh
from jax.sharding import PartitionSpec as P

H = 16
HD = 128
HALF = HD // 2
MASKED = -1e30
LN2 = 0.6931471805599453
LOG2E = 1.4426950408889634
EPSILON = 1e-05
ROPE_BASE = 10000.0
BF16 = jnp.bfloat16
F32 = jnp.float32


def block_places(order_ref, place_ref, own):
    count = order_ref.shape[0]
    for stored in range(count):
        device = stored // 2
        place_ref[order_ref[stored]] = ((device ^ own) % 2 * (count // 4) + device // 2) * 2 + stored % 2


def causal(blk, group):
    keys = lax.broadcasted_iota(jnp.int32, (blk, blk), 0)
    rows = lax.broadcasted_iota(jnp.int32, (blk, blk), 1)
    return jnp.concatenate([keys <= rows] * group, axis=1)


def row_position(order_ref, own, row_block):
    return order_ref[2 * (own ^ (row_block // 2)) + row_block % 2]


def attend_forward(group, blk, scal_ref, order_ref, q_ref, cos_ref, sin_ref, kv_ref, out_ref, lse_ref, qt_ref, place_ref, vt_ref, acc_ref, max_ref, sum_ref):
    row_block = pl.program_id(0)
    own, length = scal_ref[0], scal_ref[1]

    @pl.when(row_block == 0)
    def _():
        block_places(order_ref, place_ref, own)
        for piece in range(order_ref.shape[0]):
            cells = slice(piece * blk, (piece + 1) * blk)
            vt_ref[:, cells] = kv_ref[cells, HD:].T

    mine = row_position(order_ref, own, row_block)

    def step(place, masked):
        start = pl.multiple_of(place * blk, blk)
        scores = jnp.dot(kv_ref[pl.ds(start, blk), :HD], qt_ref[0], preferred_element_type=F32)
        if masked:
            scores = jnp.where(causal(blk, group), scores, MASKED)
        old = max_ref[...]
        new = jnp.maximum(old, jnp.max(scores, axis=0, keepdims=True))
        weights = jnp.exp2(scores - new)
        scale = jnp.exp2(old - new)
        max_ref[...] = new
        sum_ref[...] = sum_ref[...] * scale + jnp.sum(weights, axis=0, keepdims=True)
        acc_ref[...] = acc_ref[...] * scale + jnp.dot(
            vt_ref[:, pl.ds(start, blk)], weights.astype(BF16), preferred_element_type=F32
        )

    @pl.when(mine * blk < length)
    def _():
        cosine, sine = cos_ref[...], sin_ref[...]
        for head in range(group):
            query = q_ref[:, head * HD : (head + 1) * HD].T
            first, second = query[:HALF], query[HALF:]
            turned = jnp.concatenate(
                [first * cosine - second * sine, second * cosine + first * sine], axis=0
            )
            qt_ref[0, :, head * blk : (head + 1) * blk] = (turned * (LOG2E * HD**-0.5)).astype(BF16)
        max_ref[...] = jnp.full(max_ref.shape, MASKED, F32)
        sum_ref[...] = jnp.zeros(sum_ref.shape, F32)
        acc_ref[...] = jnp.zeros(acc_ref.shape, F32)
        step(place_ref[mine], True)

        def body(j, carried):
            step(place_ref[j], False)
            return carried

        lax.fori_loop(0, mine, body, 0)
        total = sum_ref[...]
        result = acc_ref[...] * (1.0 / total)
        for head in range(group):
            out_ref[:, head * HD : (head + 1) * HD] = (
                result[:, head * blk : (head + 1) * blk].T.astype(BF16)
            )
        lse_ref[0] = max_ref[...] + jnp.log2(total)

    @pl.when(mine * blk >= length)
    def _():
        out_ref[...] = jnp.zeros(out_ref.shape, BF16)
        lse_ref[...] = jnp.zeros(lse_ref.shape, F32)
        qt_ref[...] = jnp.zeros(qt_ref.shape, BF16)


def attention_forward(scalars, order, queries, cosine, sine, keys_values, blk):
    rows, width = queries.shape
    span = keys_values.shape[0]
    row_blocks, heads = rows // blk, width // HD
    table = pl.BlockSpec((HALF, blk), lambda i, *_: (0, i))
    per_block = lambda *dims: pl.BlockSpec((1,) + dims, lambda i, *_: (i, 0, 0))
    return pl.pallas_call(
        functools.partial(attend_forward, heads, blk),
        grid_spec=pltpu.PrefetchScalarGridSpec(
            num_scalar_prefetch=2,
            grid=(row_blocks,),
            in_specs=[
                pl.BlockSpec((blk, width), lambda i, *_: (i, 0)),
                table,
                table,
                pl.BlockSpec((span, 2 * HD), lambda i, *_: (0, 0)),
            ],
            out_specs=[
                pl.BlockSpec((blk, width), lambda i, *_: (i, 0)),
                per_block(1, heads * blk),
                per_block(HD, heads * blk),
            ],
            scratch_shapes=[
                pltpu.SMEM((order.shape[0],), jnp.int32),
                pltpu.VMEM((HD, span), BF16),
                pltpu.VMEM((HD, heads * blk), F32),
                pltpu.VMEM((1, heads * blk), F32),
                pltpu.VMEM((1, heads * blk), F32),
            ],
        ),
        out_shape=[
            jax.ShapeDtypeStruct((rows, width), BF16),
            jax.ShapeDtypeStruct((row_blocks, 1, heads * blk), F32),
            jax.ShapeDtypeStruct((row_blocks, HD, heads * blk), BF16),
        ],
        compiler_params=pltpu.CompilerParams(vmem_limit_bytes=40 * 2**20),
        cost_estimate=pl.CostEstimate(flops=2**20, bytes_accessed=2**16, transcendentals=0),
        name="attend_forward",
    )(scalars, order, queries, cosine, sine, keys_values)


def attend_backward(group, blk, last, scal_ref, order_ref, qt_ref, g_ref, a_ref, lse_ref, cos_ref, sin_ref, kv_ref, *rest):
    if last:
        before_ref, dq_ref, mine_ref, other_ref, place_ref, gt_ref, qs_ref, gs_ref, kt_ref, acc_ref, delta_ref, dkv_ref = rest
    else:
        dq_ref, dkv_ref, place_ref, gt_ref, qs_ref, gs_ref, kt_ref, acc_ref, delta_ref = rest
    row_block = pl.program_id(0)
    own, length = scal_ref[0], scal_ref[1]

    @pl.when(row_block == 0)
    def _():
        block_places(order_ref, place_ref, own)
        for piece in range(order_ref.shape[0]):
            cells = slice(piece * blk, (piece + 1) * blk)
            kt_ref[:, cells] = kv_ref[cells, :HD].T
        dkv_ref[...] = before_ref[...] if last else jnp.zeros(dkv_ref.shape, F32)

    mine = row_position(order_ref, own, row_block)

    def step(place, masked):
        start = pl.multiple_of(place * blk, blk)
        scores = jnp.dot(kv_ref[pl.ds(start, blk), :HD], qt_ref[0], preferred_element_type=F32)
        weights = jnp.exp2(scores - lse_ref[0])
        if masked:
            weights = jnp.where(causal(blk, group), weights, 0.0)
        grads = jnp.dot(kv_ref[pl.ds(start, blk), HD:], gt_ref[...], preferred_element_type=F32)
        dscores = (weights * (grads - delta_ref[...])).astype(BF16)
        dkv_ref[pl.ds(start, blk), HD:] += jnp.dot(
            weights.astype(BF16), gs_ref[...], preferred_element_type=F32
        )
        dkv_ref[pl.ds(start, blk), :HD] += jnp.dot(dscores, qs_ref[...], preferred_element_type=F32)
        acc_ref[...] += jnp.dot(kt_ref[:, pl.ds(start, blk)], dscores, preferred_element_type=F32)

    @pl.when(mine * blk < length)
    def _():
        for head in range(group):
            lanes = slice(head * HD, (head + 1) * HD)
            cells = slice(head * blk, (head + 1) * blk)
            grad = g_ref[:, lanes]
            gt_ref[:, cells] = grad.T
            qs_ref[cells, :] = qt_ref[0, :, cells].T
            gs_ref[cells, :] = grad
            product = grad.astype(F32) * a_ref[:, lanes].astype(F32)
            delta_ref[:, cells] = jnp.sum(product.T, axis=0, keepdims=True)
        acc_ref[...] = jnp.zeros(acc_ref.shape, F32)
        step(place_ref[mine], True)

        def body(j, carried):
            step(place_ref[j], False)
            return carried

        lax.fori_loop(0, mine, body, 0)
        cosine, sine = cos_ref[...], sin_ref[...]
        for head in range(group):
            turned = acc_ref[:, head * blk : (head + 1) * blk].astype(BF16).astype(F32)
            first, second = turned[:HALF], turned[HALF:]
            grad = jnp.concatenate(
                [first * cosine + second * sine, second * cosine - first * sine], axis=0
            )
            dq_ref[:, head * HD : (head + 1) * HD] = (grad * HD**-0.5).T.astype(BF16)

    @pl.when(mine * blk >= length)
    def _():
        dq_ref[...] = jnp.zeros(dq_ref.shape, BF16)

    if last:

        @pl.when(row_block == pl.num_programs(0) - 1)
        def _():
            half = mine_ref.shape[0]
            for total_ref, rows in ((mine_ref, slice(0, half)), (other_ref, slice(half, 2 * half))):
                total_ref[:, :HD] = (dkv_ref[rows, :HD] * LN2).astype(BF16)
                total_ref[:, HD:] = dkv_ref[rows, HD:].astype(BF16)


def attention_backward(scalars, order, turned, grads, attended, lse, cosine, sine, keys_values, blk, group, which, before=None):
    last = before is not None
    rows = grads.shape[0]
    span = keys_values.shape[0]
    row_blocks = rows // blk
    whole = pl.BlockSpec((span, 2 * HD), lambda i, *_: (0, 0))
    table = pl.BlockSpec((HALF, blk), lambda i, *_: (0, i))
    rowspec = pl.BlockSpec((blk, group * HD), lambda i, *_: (i, which))
    per_block = lambda *dims: pl.BlockSpec((1,) + dims, lambda i, *_: (i, 0, which))
    return pl.pallas_call(
        functools.partial(attend_backward, group, blk, last),
        grid_spec=pltpu.PrefetchScalarGridSpec(
            num_scalar_prefetch=2,
            grid=(row_blocks,),
            in_specs=[
                per_block(HD, group * blk),
                rowspec,
                rowspec,
                per_block(1, group * blk),
                table,
                table,
                whole,
            ]
            + [whole] * last,
            out_specs=[
                pl.BlockSpec((blk, group * HD), lambda i, *_: (i, 0)),
            ]
            + ([pl.BlockSpec((span // 2, 2 * HD), lambda i, *_: (0, 0))] * 2 if last else [whole]),
            scratch_shapes=[
                pltpu.SMEM((order.shape[0],), jnp.int32),
                pltpu.VMEM((HD, group * blk), BF16),
                pltpu.VMEM((group * blk, HD), BF16),
                pltpu.VMEM((group * blk, HD), BF16),
                pltpu.VMEM((HD, span), BF16),
                pltpu.VMEM((HD, group * blk), F32),
                pltpu.VMEM((1, group * blk), F32),
            ]
            + [pltpu.VMEM((span, 2 * HD), F32)] * last,
        ),
        out_shape=[
            jax.ShapeDtypeStruct((rows, group * HD), BF16),
        ]
        + (
            [jax.ShapeDtypeStruct((span // 2, 2 * HD), BF16)] * 2
            if last
            else [jax.ShapeDtypeStruct((span, 2 * HD), F32)]
        ),
        compiler_params=pltpu.CompilerParams(vmem_limit_bytes=48 * 2**20),
        cost_estimate=pl.CostEstimate(flops=2**20, bytes_accessed=2**16, transcendentals=0),
        name="attend_backward",
    )(scalars, order, turned, grads, attended, lse, cosine, sine, keys_values, *([before] if last else []))


def ffn_rows(count, tiles, place_ref, xa_ref, xb_ref, ga_ref, gb_ref, gate_ref, up_ref, down_ref, *rest):
    back_a, back_b, out_a, out_b, x_all, g_all, hidden_all, dgate_all, dup_all = rest[count:]
    units = gate_ref.shape[0] * gate_ref.shape[2]
    gate_rows, up_rows, down_rows = (ref[...].reshape(units, -1) for ref in (gate_ref, up_ref, down_ref))
    nt = (((1,), (1,)), ((), ()))
    early = pl.program_id(0) < tiles
    x = jnp.where(early, xa_ref[...], xb_ref[...])
    grad = jnp.where(early, ga_ref[...], gb_ref[...])
    gate = lax.dot_general(x, gate_rows, nt, preferred_element_type=F32)
    up = lax.dot_general(x, up_rows, nt, preferred_element_type=F32)
    dhidden = lax.dot_general(grad, down_rows, nt, preferred_element_type=F32)
    dhidden = dhidden.astype(BF16).astype(F32)
    sigmoid = jax.nn.sigmoid(gate)
    silu = gate * sigmoid
    hidden = (silu * up).astype(BF16)
    dgate = (dhidden * up * sigmoid * (1.0 + gate * (1.0 - sigmoid))).astype(BF16)
    dup = (dhidden * silu).astype(BF16)
    out = jnp.dot(hidden, down_rows, preferred_element_type=F32).astype(BF16)
    step = 512 if x.shape[1] % 512 == 0 else x.shape[1]
    back = jnp.concatenate(
        [
            (
                jnp.dot(dgate, gate_rows[:, at_col : at_col + step], preferred_element_type=F32)
                + jnp.dot(dup, up_rows[:, at_col : at_col + step], preferred_element_type=F32)
            ).astype(BF16)
            for at_col in range(0, x.shape[1], step)
        ],
        axis=1,
    )
    x_all[...] = x
    g_all[...] = grad
    hidden_all[...] = hidden
    dgate_all[...] = dgate
    dup_all[...] = dup

    @pl.when(early)
    def _():
        back_a[...] = back
        out_a[...] = out

    @pl.when(jnp.logical_not(early))
    def _():
        back_b[...] = back
        out_b[...] = out


def ffn_pair(place, pairs, xa, xb, ga, gb, weights, kept):
    rows, model_dim = xa.shape
    planes, _, share, _ = weights.shape
    units = planes * share
    tile = min(256, rows)
    tiles = rows // tile
    weight = lambda which: pl.BlockSpec(
        (planes, 1, share, model_dim), lambda i, *_: (0, which, 0, 0), pipeline_mode=pl.Buffered(1)
    )
    turn_a = lambda i: jnp.minimum(i, tiles - 1)
    turn_b = lambda i: jnp.maximum(i - tiles, 0)
    block = lambda index: pl.BlockSpec((tile, model_dim), index)
    here_a, here_b = block(lambda i, *_: (turn_a(i), 0)), block(lambda i, *_: (turn_b(i), 0))
    out_a = block(lambda i, place_ref: (place_ref[0] * tiles + turn_a(i), 0))
    out_b = block(lambda i, place_ref: (place_ref[0] * tiles + turn_b(i), 0))
    there = lambda wide: pl.BlockSpec((tile, wide), lambda i, place_ref: (place_ref[0] * 2 * tiles + i, 0))
    count = len(kept)
    shape = lambda tall, wide: jax.ShapeDtypeStruct((tall, wide), BF16)
    return pl.pallas_call(
        functools.partial(ffn_rows, count, tiles),
        grid_spec=pltpu.PrefetchScalarGridSpec(
            num_scalar_prefetch=1,
            grid=(2 * tiles,),
            in_specs=[here_a, here_b, here_a, here_b, weight(0), weight(1), weight(2)]
            + [pl.BlockSpec(memory_space=pl.ANY)] * count,
            out_specs=[here_a, here_b, out_a, out_b] + [there(model_dim)] * 2 + [there(units)] * 3,
        ),
        out_shape=[shape(rows, model_dim)] * 2
        + [shape(pairs * rows, model_dim)] * 2
        + [shape(pairs * 2 * rows, model_dim)] * 2
        + [shape(pairs * 2 * rows, units)] * 3,
        input_output_aliases={8 + i: 2 + i for i in range(count)},
        compiler_params=pltpu.CompilerParams(vmem_limit_bytes=52 * 2**20),
        cost_estimate=pl.CostEstimate(flops=2**20, bytes_accessed=2**16, transcendentals=0),
        name="ffn_pair",
    )(place, xa, xb, ga, gb, weights, weights, weights, *kept)


def pack_columns(*refs):
    out_ref = refs[-1]
    columns = out_ref.shape[3]
    for which, in_ref in enumerate(refs[:-1]):
        for place in range(out_ref.shape[0]):
            out_ref[place, which] = in_ref[:, place * columns : (place + 1) * columns]


def pack_units(terms, places):
    share, columns = terms[0].shape
    if share % 16:
        return jnp.stack(terms).reshape(len(terms), share, places, columns // places).transpose(2, 0, 1, 3)
    return pl.pallas_call(
        pack_columns,
        out_shape=jax.ShapeDtypeStruct((places, len(terms), share, columns // places), BF16),
        compiler_params=pltpu.CompilerParams(vmem_limit_bytes=32 * 2**20),
        cost_estimate=pl.CostEstimate(flops=2**16, bytes_accessed=len(terms) * terms[0].size * 4, transcendentals=0),
        name="pack_units",
    )(*terms)


def turn_rows(in_ref, *out_refs):
    for which, out_ref in enumerate(out_refs):
        out_ref[...] = in_ref[:, which].reshape(out_ref.shape[1], out_ref.shape[0]).T.astype(F32)


def turn_units(terms):
    places, count, share, columns = terms.shape
    if share % 16:
        turned = terms.transpose(1, 3, 0, 2).reshape(count, columns, places * share).astype(F32)
        return [turned[which] for which in range(count)]
    return pl.pallas_call(
        turn_rows,
        out_shape=[jax.ShapeDtypeStruct((columns, places * share), F32)] * count,
        compiler_params=pltpu.CompilerParams(vmem_limit_bytes=32 * 2**20),
        cost_estimate=pl.CostEstimate(flops=2**20, bytes_accessed=terms.size * 6, transcendentals=0),
        name="turn_units",
    )(terms)


def alternate_columns(part, first_ref, second_ref, out_ref):
    for at_col in range(0, first_ref.shape[1], part):
        out_ref[:, 2 * at_col : 2 * at_col + part] = first_ref[:, at_col : at_col + part]
        out_ref[:, 2 * at_col + part : 2 * at_col + 2 * part] = second_ref[:, at_col : at_col + part]


def alternate(first, second, part):
    rows, width = first.shape
    return pl.pallas_call(
        functools.partial(alternate_columns, part),
        out_shape=jax.ShapeDtypeStruct((rows, 2 * width), F32),
        cost_estimate=pl.CostEstimate(flops=2**16, bytes_accessed=first.size * 16, transcendentals=0),
        name="alternate",
    )(first, second)


def angles(positions):
    frequency = ROPE_BASE ** (-2.0 * jnp.arange(HALF, dtype=F32) / HD)
    phase_angle = frequency[:, None] * positions.astype(F32)[None, :]
    return (jnp.cos(phase_angle), jnp.sin(phase_angle))


def rotate(vectors, cosine, sine_vals):
    first_half = vectors[..., :HALF]
    second_half = vectors[..., HALF:]
    return jnp.concatenate(
        [
            first_half * cosine - second_half * sine_vals,
            second_half * cosine + first_half * sine_vals,
        ],
        axis=-1,
    )


def matmul(left, right):
    return jnp.dot(left, right, preferred_element_type=F32)


def contract_rows(left, right):
    return lax.dot_general(left, right, (((0,), (0,)), ((), ())), preferred_element_type=F32)


def contract_cols(left, right):
    return lax.dot_general(left, right, (((1,), (1,)), ((), ())), preferred_element_type=F32)


def after(value, *earlier):
    return lax.optimization_barrier((value, earlier))[0]


def exchange(value, axis, distance):
    size = lax.axis_size(axis)
    return lax.ppermute(value, axis, [(i, i ^ distance) for i in range(size)])


def swap_core(value):
    return exchange(value, "core", 1)


def spread_chips(value):
    chips = lax.axis_size("chip")
    copies = jnp.broadcast_to(value[None], (chips,) + value.shape)
    return lax.all_to_all(copies, "chip", 0, 0, tiled=False)


def gather_near(value):
    if lax.axis_size("chip") != 4:
        return [value] + [exchange(value, "chip", k) for k in range(1, lax.axis_size("chip"))]
    return [value, exchange(value, "chip", 1), exchange(value, "chip", 2)]


def send_far(near):
    if lax.axis_size("chip") != 4:
        return ()
    value, first, second = lax.optimization_barrier(near)
    half = value.shape[0] // 2
    return exchange(first[:half], "chip", 2), exchange(second[half:], "chip", 1)


def gather_far(near):
    halves = send_far(near)
    return near + [jnp.concatenate(halves, axis=0)] if halves else near


def gather_chips(value):
    return gather_far(gather_near(value))


def add_cores(terms, terms_of_other):
    return (terms.astype(F32) + swap_core(terms_of_other.astype(BF16)).astype(F32)).astype(BF16)


def deal(terms, axis):
    dealt = lax.all_to_all(terms.astype(BF16), axis, 0, 0, tiled=False)
    return jnp.sum(dealt.astype(F32), axis=0)


def at(value, index, axis=0):
    return lax.dynamic_index_in_dim(value, index, axis, keepdims=False)


def sum_planes(terms, plane):
    total = at(terms, plane).astype(F32)
    for k in range(1, lax.axis_size("fsdp")):
        total = total + exchange(at(terms, plane ^ k).astype(BF16), "fsdp", k).astype(F32)
    return total


def reduce_far(last):
    half = last.shape[0] // 2
    return exchange(last[:half], "chip", 1), exchange(last[half:], "chip", 2)


def add_half(term, passing, which):
    start = which * passing.shape[0]
    half = term[start : start + passing.shape[0]].astype(F32) + passing.astype(F32)
    return lax.dynamic_update_slice(term, half.astype(BF16), (start, 0))


def lay_columns(chunks, chip):
    rows, width = chunks[0].shape
    whole = jnp.zeros((rows, width * len(chunks)), chunks[0].dtype)
    for k, chunk in enumerate(chunks):
        whole = lax.dynamic_update_slice(whole, chunk, (0, (chip ^ k) * width))
    return whole


def shards(
    tokens,
    cotangent,
    kv_cotangent,
    lengths,
    block_order,
    w_query,
    w_kv,
    w_out,
    gain_attn,
    gain_ffn,
    w_gate,
    w_up,
    w_down,
):
    local_len, model_dim = tokens.shape[1:]
    chips, planes = lax.axis_size("chip"), lax.axis_size("fsdp")
    chip, core, plane = lax.axis_index("chip"), lax.axis_index("core"), lax.axis_index("fsdp")
    own = chip * 2 + core
    places = chips * 2
    blk = local_len // 2
    order, length = block_order[0], lengths[0]
    depth = w_query.shape[0]

    part = depth // 2
    wide = part * planes
    out_cols = model_dim // chips
    kv_rows = depth // chips
    gain_rows = depth // (2 * HD)
    narrow = lambda value: value.reshape(-1, 2 * HD)
    pieces = [
        lax.dynamic_slice(w_query, (0, chip * 2 * part + core * part), (depth, part)),
        lax.dynamic_slice(w_out, (core * part, chip * out_cols), (part, out_cols)),
        lax.dynamic_slice_in_dim(w_kv, chip * kv_rows, kv_rows, 0),
        gain_attn,
        gain_ffn,
    ]
    heights = [piece.size // (2 * HD) for piece in pieces]
    packed = jnp.concatenate([narrow(piece) for piece in pieces], axis=0)
    packed = lax.all_gather(packed, "fsdp", axis=0)
    bounds = [sum(heights[: i + 1]) for i in range(4)]
    query_piece, out_piece, kv_piece, gain_one, gain_two = jnp.split(packed, bounds, axis=1)
    out_piece = out_piece.reshape(wide, out_cols)
    gain_one = gain_one.reshape(model_dim).astype(F32)
    gain_two = gain_two.reshape(model_dim).astype(F32)
    share = w_gate.shape[1] // places
    pieces = jnp.stack(
        [
            lax.dynamic_slice(weight, (0, own * share), (model_dim, share)).T
            for weight in (w_gate, w_up, w_down)
        ]
    )
    query_piece = query_piece.reshape(model_dim, part)
    own_pos = jnp.repeat(lax.dynamic_slice_in_dim(order, own * 2, 2, 0) * blk, blk) + (
        jnp.arange(local_len, dtype=jnp.int32) % blk
    )
    live_rows = (own_pos < length)[:, None]
    grad_out = jnp.where(live_rows, cotangent[0], jnp.zeros((), BF16))
    grad_near = after(gather_near(grad_out), pieces)
    grad_far = send_far(grad_near)
    kv_full = spread_chips(after(kv_piece, grad_near)).swapaxes(0, 1).reshape(model_dim, 2 * HD)
    kv_full = with_layout_constraint(kv_full, Layout((0, 1)))
    query_near = gather_near(after(query_piece, grad_far))
    query_half = lay_columns(gather_far(query_near), chip)
    grad_others = [swap_core(chunk) for chunk in after(grad_near, query_near)]
    out_piece = after(out_piece, query_half)
    out_chunks = [out_piece] + [exchange(out_piece, "chip", k) for k in range(1, chips)]
    ffn_weights = lax.all_gather(pieces, "fsdp", axis=0)

    offsets = jnp.arange(blk, dtype=jnp.int32)
    mine = lax.dynamic_slice_in_dim(order, own * 2, 2, 0)
    theirs = lax.dynamic_slice_in_dim(order, (own ^ 1) * 2, 2, 0)
    both_pos = (jnp.concatenate([mine, theirs])[:, None] * blk + offsets[None, :]).reshape(-1)
    cosine, sine_vals = angles(both_pos)
    own_cosine, own_sine = cosine[:, :local_len].T, sine_vals[:, :local_len].T

    tokens_low = tokens[0]
    tokens_flat = tokens_low.astype(F32)
    both_tokens = jnp.concatenate([tokens_low, swap_core(tokens_low)], axis=0).astype(F32)
    both_inverse = lax.rsqrt(jnp.mean(both_tokens * both_tokens, axis=1, keepdims=True) + EPSILON)
    both_normed = (both_tokens * both_inverse * gain_one).astype(BF16)
    inverse_one = both_inverse[:local_len]

    key_value = matmul(both_normed[:local_len], kv_full)
    key_rot = rotate(key_value[:, :HD], own_cosine, own_sine)
    local_kv = jnp.concatenate([key_rot, key_value[:, HD:]], axis=1).astype(BF16)
    slot_kv = spread_chips(local_kv).reshape(-1, 2 * HD)
    slot_kv = jnp.concatenate([slot_kv, swap_core(slot_kv)], axis=0)

    heads = wide // HD
    queries = matmul(both_normed, query_half)
    scalars = after(jnp.stack([own, length]).astype(jnp.int32), grad_others)
    attended, lse, turned = attention_forward(
        scalars, order, queries, cosine, sine_vals, slot_kv, blk
    )

    attended, lse, turned, out_chunks = lax.optimization_barrier((attended, lse, turned, out_chunks))
    grad_mine = list(grad_near)
    if grad_far:
        grad_mine.append(jnp.concatenate(grad_far, axis=0))
        grad_others.append(swap_core(grad_mine[3]))
    out_half = lay_columns(out_chunks, chip)
    branch_other = swap_core(matmul(attended[local_len:], out_half).astype(BF16))
    residual = tokens_flat + matmul(attended[:local_len], out_half) + branch_other.astype(F32)
    inverse_two = lax.rsqrt(jnp.mean(residual * residual, axis=1, keepdims=True) + EPSILON)
    unit_two = residual * inverse_two
    normed_ffn = (unit_two * gain_two).astype(BF16)
    def pair(at_place, chunk, kept):
        result = ffn_pair(
            jnp.full((1,), at_place, jnp.int32),
            chips,
            chunk,
            swap_core(chunk),
            grad_mine[at_place],
            grad_others[at_place],
            ffn_weights,
            kept,
        )
        return result[0], result[1], tuple(result[2:])

    normed_near = gather_near(normed_ffn)
    back_own, back_other, kept = pair(0, normed_near[0], ())
    back_other = swap_core(back_other)
    if chips == 4:
        normed_near = after(normed_near, back_own)
        normed_far = send_far(normed_near)
        own_first, other_first, kept = pair(1, normed_near[1], kept)
        normed_far = after(normed_far, own_first)
        own_last, other_last, kept = pair(3, jnp.concatenate(normed_far, axis=0), kept)
        last = add_cores(own_last, other_last)
        first = add_cores(own_first, other_first)
        kept = after(kept, last, first)
        passing = reduce_far(last)
        own_second, other_second, kept = pair(2, normed_near[2], kept)
        passing, own_second, other_second, kept = lax.optimization_barrier(
            (passing, own_second, other_second, kept)
        )
        first = add_half(first, passing[1], 1)
        second = add_half(add_cores(own_second, other_second), passing[0], 0)
        kept = after(kept, first, second)
        arrived = [exchange(first, "chip", 1), exchange(second, "chip", 2), back_other]
    else:
        normed_chunks = gather_far(after(normed_near, back_own))
        arrived = [back_other]
        for k in range(1, chips):
            own_term, other_term, kept = pair(k, normed_chunks[k], kept)
            arrived.append(exchange(add_cores(own_term, other_term), "chip", k))

    out_own, out_other, normed_all, grad_all, hidden_all, dgate_all, dup_all = kept
    down_term = contract_rows(hidden_all, grad_all).astype(BF16)
    out_other = swap_core(out_other)
    cuts = [0, 1, 2, 3, 3.5, 4] if chips == 4 else range(chips + 1)
    out_parts = [
        (out_own[int(a * local_len) : int(b * local_len)].astype(F32) + out_other[int(a * local_len) : int(b * local_len)].astype(F32)).astype(BF16)
        for a, b in zip(cuts[:-1], cuts[1:])
    ]
    gate_term = contract_rows(dgate_all, normed_all).astype(BF16)
    arrived = after(arrived, down_term, out_parts, gate_term)
    grad_normed = back_own.astype(F32)
    for term in arrived:
        grad_normed = grad_normed + term.astype(F32)
    out_parts = after(out_parts, arrived)

    def over_planes(term):
        return lax.psum_scatter(term, "fsdp", scatter_dimension=0, tiled=True)

    gate_term, down_term = over_planes(gate_term), over_planes(down_term)

    grad_gain_two = jnp.sum(grad_normed * unit_two, axis=0)
    scaled_two = grad_normed * gain_two
    grad_residual = grad_out.astype(F32) + inverse_two * (
        scaled_two - unit_two * jnp.mean(scaled_two * unit_two, axis=1, keepdims=True)
    )
    grad_branch = grad_residual.astype(BF16)
    both_branch = jnp.concatenate([grad_branch, swap_core(grad_branch)], axis=0)
    grad_attn = contract_cols(both_branch, out_half).astype(BF16)
    branch_terms = contract_rows(attended, both_branch).astype(BF16)
    branch_terms = branch_terms.reshape(planes, part, model_dim)
    grad_attn = after(grad_attn, branch_terms)
    group = heads // 2

    def backward(grads, which, before=None):
        return attention_backward(
            scalars, order, turned, grads, attended, lse, cosine, sine_vals, slot_kv, blk, group, which, before
        )

    def deal_rows(terms):
        return lax.all_to_all(terms.reshape(places, planes * (depth // places), -1), ("chip", "core"), 0, 0, tiled=False)

    def by_plane(dealt):
        total = jnp.sum(dealt.astype(F32).reshape(chips, 2, planes, depth // places, -1), axis=0)
        return total.swapaxes(0, 1).astype(BF16)

    branch_dealt = lax.all_to_all(branch_terms, "chip", 0, 0, tiled=False)
    up_term = contract_rows(*after((dup_all, normed_all), branch_terms)).astype(BF16)
    if chips == 4:
        out_passing = exchange(out_parts[3], "chip", 1), exchange(out_parts[4], "chip", 2)
    else:
        out_passing = ()
    grad_query_a, kv_terms_a = backward(after(grad_attn, up_term), 0)
    grad_query_a, kv_terms_a, out_passing, branch_dealt = lax.optimization_barrier(
        (grad_query_a, kv_terms_a, out_passing, branch_dealt)
    )
    branch_sum = jnp.sum(branch_dealt.astype(F32), axis=0)
    query_terms_a = contract_rows(both_normed, grad_query_a).astype(BF16)
    if chips == 4:
        out_near = (add_half(out_parts[1], out_passing[1], 1), add_half(out_parts[2], out_passing[0], 0))
    else:
        out_near = tuple(out_parts[k] for k in range(1, chips))
    branch_sum = branch_sum.reshape(planes, part // planes, model_dim)
    grad_query_b, kv_mine, kv_other = backward(
        after(grad_attn, out_near, query_terms_a, branch_sum), 1, kv_terms_a
    )
    out_arrived = [exchange(term, "chip", k + 1) for k, term in enumerate(out_near)]
    grad_w_out = sum_planes(branch_sum, plane)
    query_sums_a = deal_rows(query_terms_a)
    ffn_terms = [gate_term, over_planes(up_term), down_term]
    grad_query_b, kv_mine, kv_other, out_arrived, grad_w_out, ffn_terms, query_sums_a = lax.optimization_barrier(
        (grad_query_b, kv_mine, kv_other, out_arrived, grad_w_out, ffn_terms, query_sums_a)
    )
    kv_parts = with_layout_constraint(add_cores(kv_mine, kv_other), Layout((0, 1)))
    kv_parts = kv_parts.reshape(chips, local_len, 2 * HD)
    kv_parts = [at(kv_parts, chip ^ k) for k in range(chips)]
    kv_arrived = [exchange(kv_parts[k], "chip", k) for k in range(1, chips)]
    out_arrived, ffn_terms, grad_query_b, query_sums_a = after(
        (out_arrived, ffn_terms, grad_query_b, query_sums_a), kv_parts
    )
    query_terms_b = contract_rows(both_normed, grad_query_b).astype(BF16)
    kv_arrived = after(kv_arrived, query_terms_b)
    ffn_terms = pack_units(after(ffn_terms, query_sums_a), places)
    ffn_terms = lax.all_to_all(ffn_terms, ("chip", "core"), 0, 0, tiled=False)
    kv_total = kv_parts[0].astype(F32)
    for term in kv_arrived:
        kv_total = kv_total + term.astype(F32)
    kv_total = kv_total + jnp.where(live_rows, kv_cotangent[0].astype(F32), 0.0)
    kv_low = kv_total.astype(BF16).astype(F32)
    grad_key = rotate(kv_low[:, :HD], own_cosine, -own_sine)
    grad_kv = jnp.concatenate([grad_key, kv_low[:, HD:]], axis=1).astype(BF16)
    both_grad_kv = jnp.concatenate([grad_kv, swap_core(grad_kv)], axis=0)
    kv_half = lax.dynamic_slice_in_dim(both_grad_kv, core * HD, HD, 1)
    kv_weight_half = lax.dynamic_slice_in_dim(kv_full, core * HD, HD, 1)
    rows = depth // places
    first_row = (own * planes + plane) * rows
    other_row = ((own ^ 1) * planes + plane) * rows
    kept_rows = lax.dynamic_slice_in_dim(query_half, first_row, rows, 0)
    sent_rows = swap_core(lax.dynamic_slice_in_dim(query_half, other_row, rows, 0))
    own_query_rows = jnp.where(
        core == 0, jnp.stack([kept_rows, sent_rows]), jnp.stack([sent_rows, kept_rows])
    )
    own_kv_rows = lax.dynamic_slice_in_dim(kv_full, first_row, rows, 0)
    both_query = jnp.concatenate([grad_query_a, grad_query_b], axis=1)

    def normed_one_term(rows):
        return contract_cols(both_query[rows], query_half) + contract_cols(kv_half[rows], kv_weight_half)

    gains = jnp.pad(grad_gain_two[:, None], ((0, 0), (0, HD - 1)))
    kv_grads = jnp.concatenate([contract_rows(both_normed, kv_half), gains], axis=1).astype(BF16)
    last_terms = jnp.concatenate([query_terms_b, kv_grads], axis=1)
    last_terms = with_layout_constraint(last_terms, Layout((0, 1)))
    last_dealt = deal_rows(after(last_terms, ffn_terms))
    query_sums_a = sum_planes(by_plane(after(query_sums_a, last_terms)), plane)
    both_query = after(both_query, last_terms)
    other_one = swap_core(normed_one_term(slice(local_len, None)).astype(BF16))

    grad_normed_one = normed_one_term(slice(0, local_len)) + other_one.astype(F32)
    unit_one = tokens_flat * inverse_one
    scaled_one = grad_normed_one * gain_one
    grad_tokens = grad_residual + inverse_one * (
        scaled_one - unit_one * jnp.mean(scaled_one * unit_one, axis=1, keepdims=True)
    )
    grad_tokens = grad_tokens.astype(BF16)
    out_arrived = after(out_arrived, last_terms)
    ffn_out = out_parts[0].astype(F32)
    for term in out_arrived:
        ffn_out = ffn_out + term.astype(F32)
    output = jnp.where(live_rows, residual + ffn_out, 0.0).astype(BF16)

    ffn_grads = turn_units(after(ffn_terms, last_terms))
    last_dealt = after(last_dealt, grad_tokens, output, query_sums_a, ffn_grads)
    last_planes = by_plane(last_dealt)
    last_arrived = [exchange(at(last_planes, plane ^ k), "fsdp", k) for k in range(1, planes)]
    last_sums = at(last_planes, plane).astype(F32)
    for term in last_arrived:
        last_sums = last_sums + term.astype(F32)
    query_sums = jnp.concatenate([query_sums_a, last_sums[:, :, : -2 * HD]], axis=2)
    kv_sums = last_sums[:, :, -2 * HD :]

    own_gain = lax.dynamic_slice_in_dim(gain_one, first_row, rows, 0)
    grad_gain_one = (
        jnp.sum(own_query_rows.astype(F32) * query_sums, axis=(0, 2))
        + jnp.sum(own_kv_rows.astype(F32) * jnp.concatenate([kv_sums[0, :, :HD], kv_sums[1, :, :HD]], axis=1), axis=1)
    ) / own_gain
    grad_gain_two = kv_sums[0, :, HD] + kv_sums[1, :, HD]
    grad_w_query = alternate(query_sums[0], query_sums[1], part)
    grad_w_kv = jnp.concatenate([kv_sums[0, :, :HD], kv_sums[1, :, :HD]], axis=1)
    return (
        output[None],
        grad_tokens.astype(BF16)[None],
        grad_w_query,
        grad_w_kv,
        grad_w_out,
        grad_gain_one,
        grad_gain_two,
        ffn_grads[0],
        ffn_grads[1],
        ffn_grads[2],
    )


def solution(mesh):
    ctx, planes = mesh.shape["ctx"], mesh.shape["fsdp"]
    split = Mesh(mesh.devices.reshape(ctx // 2, 2, planes), ("chip", "core", "fsdp"))
    ctx_axes = ("chip", "core")
    return jax.shard_map(
        shards,
        mesh=split,
        in_specs=(
            P("fsdp", ctx_axes, None),
            P("fsdp", ctx_axes, None),
            P("fsdp", ctx_axes, None),
            P("fsdp"),
            P("fsdp", None),
            P("fsdp", None),
            P("fsdp", None),
            P("fsdp", None),
            P("fsdp"),
            P("fsdp"),
            P(None, "fsdp"),
            P(None, "fsdp"),
            P(None, "fsdp"),
        ),
        out_specs=(
            P("fsdp", ctx_axes, None),
            P("fsdp", ctx_axes, None),
            P(("chip", "core", "fsdp"), None),
            P(("chip", "core", "fsdp"), None),
            P(("chip", "core", "fsdp"), None),
            P(("chip", "core", "fsdp")),
            P(("chip", "core", "fsdp")),
            P(ctx_axes, "fsdp"),
            P(ctx_axes, "fsdp"),
            P(ctx_axes, "fsdp"),
        ),
        check_vma=False,
    )
```

```python
import functools

import jax
import jax.numpy as jnp
from jax import lax
from jax.experimental import pallas as pl
from jax.experimental.layout import Layout, with_layout_constraint
from jax.experimental.pallas import tpu as pltpu
from jax.sharding import Mesh
from jax.sharding import PartitionSpec as P

H = 16
HD = 128
HALF = HD // 2
MASKED = -1e30
LN2 = 0.6931471805599453
LOG2E = 1.4426950408889634
EPSILON = 1e-05
ROPE_BASE = 10000.0
BF16 = jnp.bfloat16
F32 = jnp.float32


def block_places(order_ref, place_ref, own):
    count = order_ref.shape[0]
    for stored in range(count):
        device = stored // 2
        place_ref[order_ref[stored]] = ((device ^ own) % 2 * (count // 4) + device // 2) * 2 + stored % 2


def causal(blk, group):
    keys = lax.broadcasted_iota(jnp.int32, (blk, blk), 0)
    rows = lax.broadcasted_iota(jnp.int32, (blk, blk), 1)
    return jnp.concatenate([keys <= rows] * group, axis=1)


def row_position(order_ref, own, row_block):
    return order_ref[2 * (own ^ (row_block // 2)) + row_block % 2]


def attend_forward(group, blk, scal_ref, order_ref, q_ref, cos_ref, sin_ref, kv_ref, out_ref, lse_ref, qt_ref, place_ref, vt_ref, acc_ref, max_ref, sum_ref):
    row_block = pl.program_id(0)
    own, length = scal_ref[0], scal_ref[1]

    @pl.when(row_block == 0)
    def _():
        block_places(order_ref, place_ref, own)
        for piece in range(order_ref.shape[0]):
            cells = slice(piece * blk, (piece + 1) * blk)
            vt_ref[:, cells] = kv_ref[cells, HD:].T

    mine = row_position(order_ref, own, row_block)

    def step(place, masked):
        start = pl.multiple_of(place * blk, blk)
        scores = jnp.dot(kv_ref[pl.ds(start, blk), :HD], qt_ref[0], preferred_element_type=F32)
        if masked:
            scores = jnp.where(causal(blk, group), scores, MASKED)
        old = max_ref[...]
        new = jnp.maximum(old, jnp.max(scores, axis=0, keepdims=True))
        weights = jnp.exp2(scores - new)
        scale = jnp.exp2(old - new)
        max_ref[...] = new
        sum_ref[...] = sum_ref[...] * scale + jnp.sum(weights, axis=0, keepdims=True)
        acc_ref[...] = acc_ref[...] * scale + jnp.dot(
            vt_ref[:, pl.ds(start, blk)], weights.astype(BF16), preferred_element_type=F32
        )

    @pl.when(mine * blk < length)
    def _():
        cosine, sine = cos_ref[...], sin_ref[...]
        for head in range(group):
            query = q_ref[:, head * HD : (head + 1) * HD].T
            first, second = query[:HALF], query[HALF:]
            turned = jnp.concatenate(
                [first * cosine - second * sine, second * cosine + first * sine], axis=0
            )
            qt_ref[0, :, head * blk : (head + 1) * blk] = (turned * (LOG2E * HD**-0.5)).astype(BF16)
        max_ref[...] = jnp.full(max_ref.shape, MASKED, F32)
        sum_ref[...] = jnp.zeros(sum_ref.shape, F32)
        acc_ref[...] = jnp.zeros(acc_ref.shape, F32)
        step(place_ref[mine], True)

        def body(j, carried):
            step(place_ref[j], False)
            return carried

        lax.fori_loop(0, mine, body, 0)
        total = sum_ref[...]
        result = acc_ref[...] * (1.0 / total)
        for head in range(group):
            out_ref[:, head * HD : (head + 1) * HD] = (
                result[:, head * blk : (head + 1) * blk].T.astype(BF16)
            )
        lse_ref[0] = max_ref[...] + jnp.log2(total)

    @pl.when(mine * blk >= length)
    def _():
        out_ref[...] = jnp.zeros(out_ref.shape, BF16)
        lse_ref[...] = jnp.zeros(lse_ref.shape, F32)
        qt_ref[...] = jnp.zeros(qt_ref.shape, BF16)


def attention_forward(scalars, order, queries, cosine, sine, keys_values, blk):
    rows, width = queries.shape
    span = keys_values.shape[0]
    row_blocks, heads = rows // blk, width // HD
    table = pl.BlockSpec((HALF, blk), lambda i, *_: (0, i))
    per_block = lambda *dims: pl.BlockSpec((1,) + dims, lambda i, *_: (i, 0, 0))
    return pl.pallas_call(
        functools.partial(attend_forward, heads, blk),
        grid_spec=pltpu.PrefetchScalarGridSpec(
            num_scalar_prefetch=2,
            grid=(row_blocks,),
            in_specs=[
                pl.BlockSpec((blk, width), lambda i, *_: (i, 0)),
                table,
                table,
                pl.BlockSpec((span, 2 * HD), lambda i, *_: (0, 0)),
            ],
            out_specs=[
                pl.BlockSpec((blk, width), lambda i, *_: (i, 0)),
                per_block(1, heads * blk),
                per_block(HD, heads * blk),
            ],
            scratch_shapes=[
                pltpu.SMEM((order.shape[0],), jnp.int32),
                pltpu.VMEM((HD, span), BF16),
                pltpu.VMEM((HD, heads * blk), F32),
                pltpu.VMEM((1, heads * blk), F32),
                pltpu.VMEM((1, heads * blk), F32),
            ],
        ),
        out_shape=[
            jax.ShapeDtypeStruct((rows, width), BF16),
            jax.ShapeDtypeStruct((row_blocks, 1, heads * blk), F32),
            jax.ShapeDtypeStruct((row_blocks, HD, heads * blk), BF16),
        ],
        compiler_params=pltpu.CompilerParams(vmem_limit_bytes=40 * 2**20),
        cost_estimate=pl.CostEstimate(flops=2**20, bytes_accessed=2**16, transcendentals=0),
        name="attend_forward",
    )(scalars, order, queries, cosine, sine, keys_values)


def attend_backward(group, blk, last, scal_ref, order_ref, qt_ref, g_ref, a_ref, lse_ref, cos_ref, sin_ref, kv_ref, *rest):
    if last:
        before_ref, dq_ref, mine_ref, other_ref, place_ref, gt_ref, qs_ref, gs_ref, kt_ref, acc_ref, delta_ref, dkv_ref = rest
    else:
        dq_ref, dkv_ref, place_ref, gt_ref, qs_ref, gs_ref, kt_ref, acc_ref, delta_ref = rest
    row_block = pl.program_id(0)
    own, length = scal_ref[0], scal_ref[1]

    @pl.when(row_block == 0)
    def _():
        block_places(order_ref, place_ref, own)
        for piece in range(order_ref.shape[0]):
            cells = slice(piece * blk, (piece + 1) * blk)
            kt_ref[:, cells] = kv_ref[cells, :HD].T
        dkv_ref[...] = before_ref[...] if last else jnp.zeros(dkv_ref.shape, F32)

    mine = row_position(order_ref, own, row_block)

    def step(place, masked):
        start = pl.multiple_of(place * blk, blk)
        scores = jnp.dot(kv_ref[pl.ds(start, blk), :HD], qt_ref[0], preferred_element_type=F32)
        weights = jnp.exp2(scores - lse_ref[0])
        if masked:
            weights = jnp.where(causal(blk, group), weights, 0.0)
        grads = jnp.dot(kv_ref[pl.ds(start, blk), HD:], gt_ref[...], preferred_element_type=F32)
        dscores = (weights * (grads - delta_ref[...])).astype(BF16)
        dkv_ref[pl.ds(start, blk), HD:] += jnp.dot(
            weights.astype(BF16), gs_ref[...], preferred_element_type=F32
        )
        dkv_ref[pl.ds(start, blk), :HD] += jnp.dot(dscores, qs_ref[...], preferred_element_type=F32)
        acc_ref[...] += jnp.dot(kt_ref[:, pl.ds(start, blk)], dscores, preferred_element_type=F32)

    @pl.when(mine * blk < length)
    def _():
        for head in range(group):
            lanes = slice(head * HD, (head + 1) * HD)
            cells = slice(head * blk, (head + 1) * blk)
            grad = g_ref[:, lanes]
            gt_ref[:, cells] = grad.T
            qs_ref[cells, :] = qt_ref[0, :, cells].T
            gs_ref[cells, :] = grad
            product = grad.astype(F32) * a_ref[:, lanes].astype(F32)
            delta_ref[:, cells] = jnp.sum(product.T, axis=0, keepdims=True)
        acc_ref[...] = jnp.zeros(acc_ref.shape, F32)
        step(place_ref[mine], True)

        def body(j, carried):
            step(place_ref[j], False)
            return carried

        lax.fori_loop(0, mine, body, 0)
        cosine, sine = cos_ref[...], sin_ref[...]
        for head in range(group):
            turned = acc_ref[:, head * blk : (head + 1) * blk].astype(BF16).astype(F32)
            first, second = turned[:HALF], turned[HALF:]
            grad = jnp.concatenate(
                [first * cosine + second * sine, second * cosine - first * sine], axis=0
            )
            dq_ref[:, head * HD : (head + 1) * HD] = (grad * HD**-0.5).T.astype(BF16)

    @pl.when(mine * blk >= length)
    def _():
        dq_ref[...] = jnp.zeros(dq_ref.shape, BF16)

    if last:

        @pl.when(row_block == pl.num_programs(0) - 1)
        def _():
            half = mine_ref.shape[0]
            for total_ref, rows in ((mine_ref, slice(0, half)), (other_ref, slice(half, 2 * half))):
                total_ref[:, :HD] = (dkv_ref[rows, :HD] * LN2).astype(BF16)
                total_ref[:, HD:] = dkv_ref[rows, HD:].astype(BF16)


def attention_backward(scalars, order, turned, grads, attended, lse, cosine, sine, keys_values, blk, group, which, before=None):
    last = before is not None
    rows = grads.shape[0]
    span = keys_values.shape[0]
    row_blocks = rows // blk
    whole = pl.BlockSpec((span, 2 * HD), lambda i, *_: (0, 0))
    table = pl.BlockSpec((HALF, blk), lambda i, *_: (0, i))
    rowspec = pl.BlockSpec((blk, group * HD), lambda i, *_: (i, which))
    per_block = lambda *dims: pl.BlockSpec((1,) + dims, lambda i, *_: (i, 0, which))
    return pl.pallas_call(
        functools.partial(attend_backward, group, blk, last),
        grid_spec=pltpu.PrefetchScalarGridSpec(
            num_scalar_prefetch=2,
            grid=(row_blocks,),
            in_specs=[
                per_block(HD, group * blk),
                rowspec,
                rowspec,
                per_block(1, group * blk),
                table,
                table,
                whole,
            ]
            + [whole] * last,
            out_specs=[
                pl.BlockSpec((blk, group * HD), lambda i, *_: (i, 0)),
            ]
            + ([pl.BlockSpec((span // 2, 2 * HD), lambda i, *_: (0, 0))] * 2 if last else [whole]),
            scratch_shapes=[
                pltpu.SMEM((order.shape[0],), jnp.int32),
                pltpu.VMEM((HD, group * blk), BF16),
                pltpu.VMEM((group * blk, HD), BF16),
                pltpu.VMEM((group * blk, HD), BF16),
                pltpu.VMEM((HD, span), BF16),
                pltpu.VMEM((HD, group * blk), F32),
                pltpu.VMEM((1, group * blk), F32),
            ]
            + [pltpu.VMEM((span, 2 * HD), F32)] * last,
        ),
        out_shape=[
            jax.ShapeDtypeStruct((rows, group * HD), BF16),
        ]
        + (
            [jax.ShapeDtypeStruct((span // 2, 2 * HD), BF16)] * 2
            if last
            else [jax.ShapeDtypeStruct((span, 2 * HD), F32)]
        ),
        compiler_params=pltpu.CompilerParams(vmem_limit_bytes=48 * 2**20),
        cost_estimate=pl.CostEstimate(flops=2**20, bytes_accessed=2**16, transcendentals=0),
        name="attend_backward",
    )(scalars, order, turned, grads, attended, lse, cosine, sine, keys_values, *([before] if last else []))


def ffn_rows(count, tiles, place_ref, xa_ref, xb_ref, ga_ref, gb_ref, gate_ref, up_ref, down_ref, *rest):
    back_a, back_b, out_a, out_b, x_all, g_all, hidden_all, dgate_all, dup_all = rest[count:]
    units = gate_ref.shape[0] * gate_ref.shape[2]
    gate_rows, up_rows, down_rows = (ref[...].reshape(units, -1) for ref in (gate_ref, up_ref, down_ref))
    nt = (((1,), (1,)), ((), ()))
    early = pl.program_id(0) < tiles
    x = jnp.where(early, xa_ref[...], xb_ref[...])
    grad = jnp.where(early, ga_ref[...], gb_ref[...])
    gate = lax.dot_general(x, gate_rows, nt, preferred_element_type=F32)
    up = lax.dot_general(x, up_rows, nt, preferred_element_type=F32)
    dhidden = lax.dot_general(grad, down_rows, nt, preferred_element_type=F32)
    dhidden = dhidden.astype(BF16).astype(F32)
    sigmoid = jax.nn.sigmoid(gate)
    silu = gate * sigmoid
    hidden = (silu * up).astype(BF16)
    dgate = (dhidden * up * sigmoid * (1.0 + gate * (1.0 - sigmoid))).astype(BF16)
    dup = (dhidden * silu).astype(BF16)
    out = jnp.dot(hidden, down_rows, preferred_element_type=F32).astype(BF16)
    step = 512 if x.shape[1] % 512 == 0 else x.shape[1]
    back = jnp.concatenate(
        [
            (
                jnp.dot(dgate, gate_rows[:, at_col : at_col + step], preferred_element_type=F32)
                + jnp.dot(dup, up_rows[:, at_col : at_col + step], preferred_element_type=F32)
            ).astype(BF16)
            for at_col in range(0, x.shape[1], step)
        ],
        axis=1,
    )
    x_all[...] = x
    g_all[...] = grad
    hidden_all[...] = hidden
    dgate_all[...] = dgate
    dup_all[...] = dup

    @pl.when(early)
    def _():
        back_a[...] = back
        out_a[...] = out

    @pl.when(jnp.logical_not(early))
    def _():
        back_b[...] = back
        out_b[...] = out


def ffn_pair(place, pairs, xa, xb, ga, gb, weights, kept):
    rows, model_dim = xa.shape
    planes, _, share, _ = weights.shape
    units = planes * share
    tile = min(256, rows)
    tiles = rows // tile
    weight = lambda which: pl.BlockSpec(
        (planes, 1, share, model_dim), lambda i, *_: (0, which, 0, 0), pipeline_mode=pl.Buffered(1)
    )
    turn_a = lambda i: jnp.minimum(i, tiles - 1)
    turn_b = lambda i: jnp.maximum(i - tiles, 0)
    block = lambda index: pl.BlockSpec((tile, model_dim), index)
    here_a, here_b = block(lambda i, *_: (turn_a(i), 0)), block(lambda i, *_: (turn_b(i), 0))
    out_a = block(lambda i, place_ref: (place_ref[0] * tiles + turn_a(i), 0))
    out_b = block(lambda i, place_ref: (place_ref[0] * tiles + turn_b(i), 0))
    there = lambda wide: pl.BlockSpec((tile, wide), lambda i, place_ref: (place_ref[0] * 2 * tiles + i, 0))
    count = len(kept)
    shape = lambda tall, wide: jax.ShapeDtypeStruct((tall, wide), BF16)
    return pl.pallas_call(
        functools.partial(ffn_rows, count, tiles),
        grid_spec=pltpu.PrefetchScalarGridSpec(
            num_scalar_prefetch=1,
            grid=(2 * tiles,),
            in_specs=[here_a, here_b, here_a, here_b, weight(0), weight(1), weight(2)]
            + [pl.BlockSpec(memory_space=pl.ANY)] * count,
            out_specs=[here_a, here_b, out_a, out_b] + [there(model_dim)] * 2 + [there(units)] * 3,
        ),
        out_shape=[shape(rows, model_dim)] * 2
        + [shape(pairs * rows, model_dim)] * 2
        + [shape(pairs * 2 * rows, model_dim)] * 2
        + [shape(pairs * 2 * rows, units)] * 3,
        input_output_aliases={8 + i: 2 + i for i in range(count)},
        compiler_params=pltpu.CompilerParams(vmem_limit_bytes=52 * 2**20),
        cost_estimate=pl.CostEstimate(flops=2**20, bytes_accessed=2**16, transcendentals=0),
        name="ffn_pair",
    )(place, xa, xb, ga, gb, weights, weights, weights, *kept)


def pack_columns(*refs):
    out_ref = refs[-1]
    columns = out_ref.shape[3]
    for which, in_ref in enumerate(refs[:-1]):
        for place in range(out_ref.shape[0]):
            out_ref[place, which] = in_ref[:, place * columns : (place + 1) * columns]


def pack_units(terms, places):
    share, columns = terms[0].shape
    if share % 16:
        return jnp.stack(terms).reshape(len(terms), share, places, columns // places).transpose(2, 0, 1, 3)
    return pl.pallas_call(
        pack_columns,
        out_shape=jax.ShapeDtypeStruct((places, len(terms), share, columns // places), BF16),
        compiler_params=pltpu.CompilerParams(vmem_limit_bytes=32 * 2**20),
        cost_estimate=pl.CostEstimate(flops=2**16, bytes_accessed=len(terms) * terms[0].size * 4, transcendentals=0),
        name="pack_units",
    )(*terms)


def turn_rows(in_ref, *out_refs):
    for which, out_ref in enumerate(out_refs):
        out_ref[...] = in_ref[:, which].reshape(out_ref.shape[1], out_ref.shape[0]).T.astype(F32)


def turn_units(terms):
    places, count, share, columns = terms.shape
    if share % 16:
        turned = terms.transpose(1, 3, 0, 2).reshape(count, columns, places * share).astype(F32)
        return [turned[which] for which in range(count)]
    return pl.pallas_call(
        turn_rows,
        out_shape=[jax.ShapeDtypeStruct((columns, places * share), F32)] * count,
        compiler_params=pltpu.CompilerParams(vmem_limit_bytes=32 * 2**20),
        cost_estimate=pl.CostEstimate(flops=2**20, bytes_accessed=terms.size * 6, transcendentals=0),
        name="turn_units",
    )(terms)


def alternate_columns(part, first_ref, second_ref, out_ref):
    for at_col in range(0, first_ref.shape[1], part):
        out_ref[:, 2 * at_col : 2 * at_col + part] = first_ref[:, at_col : at_col + part]
        out_ref[:, 2 * at_col + part : 2 * at_col + 2 * part] = second_ref[:, at_col : at_col + part]


def alternate(first, second, part):
    rows, width = first.shape
    return pl.pallas_call(
        functools.partial(alternate_columns, part),
        out_shape=jax.ShapeDtypeStruct((rows, 2 * width), F32),
        cost_estimate=pl.CostEstimate(flops=2**16, bytes_accessed=first.size * 16, transcendentals=0),
        name="alternate",
    )(first, second)


def sum_chips(plane_ref, dealt_ref, *out_refs):
    rows = out_refs[0].shape[1]
    for k, out_ref in enumerate(out_refs):
        start = pl.multiple_of((plane_ref[0] ^ k) * rows, rows)
        for core in range(2):
            total = dealt_ref[core, pl.ds(start, rows), :].astype(F32)
            for place in range(2 + core, dealt_ref.shape[0], 2):
                total = total + dealt_ref[place, pl.ds(start, rows), :].astype(F32)
            out_ref[core] = total.astype(BF16)


def split_planes(dealt, plane, planes):
    rows, columns = dealt.shape[1] // planes, dealt.shape[2]
    return pl.pallas_call(
        sum_chips,
        grid_spec=pltpu.PrefetchScalarGridSpec(
            num_scalar_prefetch=1,
            grid=(1,),
            in_specs=[pl.BlockSpec(dealt.shape, lambda i, *_: (0, 0, 0), pipeline_mode=pl.Buffered(1))],
            out_specs=[pl.BlockSpec((2, rows, columns), lambda i, *_: (0, 0, 0))] * planes,
        ),
        out_shape=[jax.ShapeDtypeStruct((2, rows, columns), BF16)] * planes,
        compiler_params=pltpu.CompilerParams(vmem_limit_bytes=32 * 2**20),
        cost_estimate=pl.CostEstimate(flops=2**20, bytes_accessed=dealt.size * 3, transcendentals=0),
        name="sum_chips",
    )(plane.reshape(1).astype(jnp.int32), dealt)


def angles(positions):
    frequency = ROPE_BASE ** (-2.0 * jnp.arange(HALF, dtype=F32) / HD)
    phase_angle = frequency[:, None] * positions.astype(F32)[None, :]
    return (jnp.cos(phase_angle), jnp.sin(phase_angle))


def rotate(vectors, cosine, sine_vals):
    first_half = vectors[..., :HALF]
    second_half = vectors[..., HALF:]
    return jnp.concatenate(
        [
            first_half * cosine - second_half * sine_vals,
            second_half * cosine + first_half * sine_vals,
        ],
        axis=-1,
    )


def matmul(left, right):
    return jnp.dot(left, right, preferred_element_type=F32)


def contract_rows(left, right):
    return lax.dot_general(left, right, (((0,), (0,)), ((), ())), preferred_element_type=F32)


def contract_cols(left, right):
    return lax.dot_general(left, right, (((1,), (1,)), ((), ())), preferred_element_type=F32)


def after(value, *earlier):
    return lax.optimization_barrier((value, earlier))[0]


def exchange(value, axis, distance):
    size = lax.axis_size(axis)
    return lax.ppermute(value, axis, [(i, i ^ distance) for i in range(size)])


def swap_core(value):
    return exchange(value, "core", 1)


def spread_chips(value):
    chips = lax.axis_size("chip")
    copies = jnp.broadcast_to(value[None], (chips,) + value.shape)
    return lax.all_to_all(copies, "chip", 0, 0, tiled=False)


def gather_near(value):
    if lax.axis_size("chip") != 4:
        return [value] + [exchange(value, "chip", k) for k in range(1, lax.axis_size("chip"))]
    return [value, exchange(value, "chip", 1), exchange(value, "chip", 2)]


def send_far(near):
    if lax.axis_size("chip") != 4:
        return ()
    value, first, second = lax.optimization_barrier(near)
    half = value.shape[0] // 2
    first, second = lax.optimization_barrier((first[:half], second[half:]))
    return exchange(first, "chip", 2), exchange(second, "chip", 1)


def gather_far(near):
    halves = lax.optimization_barrier(send_far(near))
    return near + [jnp.concatenate(halves, axis=0)] if halves else near


def gather_chips(value):
    return gather_far(gather_near(value))


def add_cores(terms, terms_of_other):
    return (terms.astype(F32) + swap_core(terms_of_other.astype(BF16)).astype(F32)).astype(BF16)


def deal(terms, axis):
    dealt = lax.all_to_all(terms.astype(BF16), axis, 0, 0, tiled=False)
    return jnp.sum(dealt.astype(F32), axis=0)


def at(value, index, axis=0):
    return lax.dynamic_index_in_dim(value, index, axis, keepdims=False)


def sum_planes(terms, plane):
    total = at(terms, plane).astype(F32)
    for k in range(1, lax.axis_size("fsdp")):
        total = total + exchange(at(terms, plane ^ k).astype(BF16), "fsdp", k).astype(F32)
    return total


def reduce_far(last):
    half = last.shape[0] // 2
    return exchange(last[:half], "chip", 1), exchange(last[half:], "chip", 2)


def add_half(term, passing, which):
    pad = term.shape[0] - passing.shape[0]
    passing = jnp.pad(passing, ((pad, 0) if which else (0, pad), (0, 0)))
    return (term.astype(F32) + passing.astype(F32)).astype(BF16)


def lay_columns(chunks, chip):
    rows, width = chunks[0].shape
    whole = jnp.zeros((rows, width * len(chunks)), chunks[0].dtype)
    for k, chunk in enumerate(chunks):
        whole = lax.dynamic_update_slice(whole, chunk, (0, (chip ^ k) * width))
    return whole


def shards(
    tokens,
    cotangent,
    kv_cotangent,
    lengths,
    block_order,
    w_query,
    w_kv,
    w_out,
    gain_attn,
    gain_ffn,
    w_gate,
    w_up,
    w_down,
):
    local_len, model_dim = tokens.shape[1:]
    chips, planes = lax.axis_size("chip"), lax.axis_size("fsdp")
    chip, core, plane = lax.axis_index("chip"), lax.axis_index("core"), lax.axis_index("fsdp")
    own = chip * 2 + core
    places = chips * 2
    blk = local_len // 2
    order, length = block_order[0], lengths[0]
    depth = w_query.shape[0]

    part = depth // 2
    wide = part * planes
    out_cols = model_dim // chips
    kv_rows = depth // chips
    gain_rows = depth // (2 * HD)
    narrow = lambda value: value.reshape(-1, 2 * HD)
    pieces = [
        lax.dynamic_slice(w_query, (0, chip * 2 * part + core * part), (depth, part)),
        lax.dynamic_slice(w_out, (core * part, chip * out_cols), (part, out_cols)),
        lax.dynamic_slice_in_dim(w_kv, chip * kv_rows, kv_rows, 0),
        gain_attn,
        gain_ffn,
    ]
    heights = [piece.size // (2 * HD) for piece in pieces]
    packed = jnp.concatenate([narrow(piece) for piece in pieces], axis=0)
    packed = lax.all_gather(packed, "fsdp", axis=0)
    bounds = [sum(heights[: i + 1]) for i in range(4)]
    query_piece, out_piece, kv_piece, gain_one, gain_two = jnp.split(packed, bounds, axis=1)
    out_piece = out_piece.reshape(wide, out_cols)
    gain_one = gain_one.reshape(model_dim).astype(F32)
    gain_two = gain_two.reshape(model_dim).astype(F32)
    share = w_gate.shape[1] // places
    pieces = jnp.stack(
        [
            lax.dynamic_slice(weight, (0, own * share), (model_dim, share)).T
            for weight in (w_gate, w_up, w_down)
        ]
    )
    query_piece = query_piece.reshape(model_dim, part)
    own_pos = jnp.repeat(lax.dynamic_slice_in_dim(order, own * 2, 2, 0) * blk, blk) + (
        jnp.arange(local_len, dtype=jnp.int32) % blk
    )
    live_rows = (own_pos < length)[:, None]
    grad_out = jnp.where(live_rows, cotangent[0], jnp.zeros((), BF16))
    grad_near = after(gather_near(grad_out), pieces)
    kv_full = spread_chips(after(kv_piece, grad_near)).swapaxes(0, 1).reshape(model_dim, 2 * HD)
    kv_full = with_layout_constraint(kv_full, Layout((0, 1)))
    query_near = gather_near(after(query_piece, grad_near))
    query_half = lay_columns(gather_far(query_near), chip)
    grad_others = [swap_core(chunk) for chunk in after(grad_near, query_near)]
    grad_far = send_far(after(grad_near, query_half, grad_others))
    out_chunks = spread_chips(after(out_piece, query_half))
    ffn_weights = lax.all_gather(pieces, "fsdp", axis=0)

    offsets = jnp.arange(blk, dtype=jnp.int32)
    mine = lax.dynamic_slice_in_dim(order, own * 2, 2, 0)
    theirs = lax.dynamic_slice_in_dim(order, (own ^ 1) * 2, 2, 0)
    both_pos = (jnp.concatenate([mine, theirs])[:, None] * blk + offsets[None, :]).reshape(-1)
    cosine, sine_vals = angles(both_pos)
    own_cosine, own_sine = cosine[:, :local_len].T, sine_vals[:, :local_len].T

    tokens_low = tokens[0]
    tokens_flat = tokens_low.astype(F32)
    both_tokens = jnp.concatenate([tokens_low, swap_core(tokens_low)], axis=0).astype(F32)
    both_inverse = lax.rsqrt(jnp.mean(both_tokens * both_tokens, axis=1, keepdims=True) + EPSILON)
    both_normed = (both_tokens * both_inverse * gain_one).astype(BF16)
    inverse_one = both_inverse[:local_len]

    key_value = matmul(both_normed[:local_len], kv_full)
    key_rot = rotate(key_value[:, :HD], own_cosine, own_sine)
    local_kv = jnp.concatenate([key_rot, key_value[:, HD:]], axis=1).astype(BF16)
    slot_kv = after(spread_chips(local_kv), query_half).reshape(-1, 2 * HD)
    slot_kv = jnp.concatenate([slot_kv, swap_core(slot_kv)], axis=0)

    heads = wide // HD
    queries = matmul(both_normed, query_half)
    scalars = jnp.stack([own, length]).astype(jnp.int32)
    attended, lse, turned = attention_forward(
        scalars, order, queries, cosine, sine_vals, slot_kv, blk
    )

    attended, lse, turned, out_chunks, grad_far = lax.optimization_barrier(
        (attended, lse, turned, out_chunks, grad_far)
    )
    grad_mine = list(grad_near)
    if grad_far:
        grad_mine.append(jnp.concatenate(grad_far, axis=0))
        grad_others.append(swap_core(grad_mine[3]))
    out_half = out_chunks.swapaxes(0, 1).reshape(wide, model_dim)
    branch_other = swap_core(matmul(attended[local_len:], out_half).astype(BF16))
    residual = tokens_flat + matmul(attended[:local_len], out_half) + branch_other.astype(F32)
    inverse_two = lax.rsqrt(jnp.mean(residual * residual, axis=1, keepdims=True) + EPSILON)
    unit_two = residual * inverse_two
    normed_ffn = (unit_two * gain_two).astype(BF16)
    def pair(at_place, chunk, kept):
        result = ffn_pair(
            jnp.full((1,), at_place, jnp.int32),
            chips,
            chunk,
            swap_core(chunk),
            grad_mine[at_place],
            grad_others[at_place],
            ffn_weights,
            kept,
        )
        return result[0], result[1], tuple(result[2:])

    normed_near = gather_near(normed_ffn)
    back_own, back_other, kept = pair(0, normed_near[0], ())
    back_other = swap_core(back_other)
    if chips == 4:
        normed_near = after(normed_near, back_own)
        normed_far = send_far(normed_near)
        own_first, other_first, kept = pair(1, normed_near[1], kept)
        normed_far = after(normed_far, own_first)
        own_last, other_last, kept = pair(3, jnp.concatenate(normed_far, axis=0), kept)
        last = add_cores(own_last, other_last)
        other_first = swap_core(other_first)
        kept = after(kept, last, other_first)
        passing = reduce_far(last)
        own_second, other_second, kept = pair(2, normed_near[2], kept)
        passing, own_second, other_second, kept = lax.optimization_barrier(
            (passing, own_second, other_second, kept)
        )
        first = add_half(own_first.astype(F32) + other_first.astype(F32), passing[1], 1)
        second = add_half(own_second.astype(F32) + swap_core(other_second).astype(F32), passing[0], 0)
        kept = after(kept, first, second)
        arrived = [exchange(first, "chip", 1), exchange(second, "chip", 2), back_other]
    else:
        normed_chunks = gather_far(after(normed_near, back_own))
        arrived = [back_other]
        for k in range(1, chips):
            own_term, other_term, kept = pair(k, normed_chunks[k], kept)
            arrived.append(exchange(add_cores(own_term, other_term), "chip", k))

    out_own, out_other, normed_all, grad_all, hidden_all, dgate_all, dup_all = kept
    down_term = contract_rows(hidden_all, grad_all).astype(BF16)
    out_other = swap_core(out_other)
    cuts = [0, 1, 2, 3, 3.5, 4] if chips == 4 else range(chips + 1)
    out_parts = [
        (out_own[int(a * local_len) : int(b * local_len)].astype(F32) + out_other[int(a * local_len) : int(b * local_len)].astype(F32)).astype(BF16)
        for a, b in zip(cuts[:-1], cuts[1:])
    ]
    gate_term = contract_rows(dgate_all, normed_all).astype(BF16)
    arrived = after(arrived, down_term, out_parts, gate_term)
    grad_normed = back_own.astype(F32)
    for term in arrived:
        grad_normed = grad_normed + term.astype(F32)
    out_parts = after(out_parts, arrived)

    def over_planes(term):
        return lax.psum_scatter(term, "fsdp", scatter_dimension=0, tiled=True)

    gate_term, down_term = over_planes(gate_term), over_planes(down_term)

    grad_gain_two = jnp.sum(grad_normed * unit_two, axis=0)
    scaled_two = grad_normed * gain_two
    grad_residual = grad_out.astype(F32) + inverse_two * (
        scaled_two - unit_two * jnp.mean(scaled_two * unit_two, axis=1, keepdims=True)
    )
    grad_branch = grad_residual.astype(BF16)
    both_branch = jnp.concatenate([grad_branch, swap_core(grad_branch)], axis=0)
    grad_attn = contract_cols(both_branch, out_half).astype(BF16)
    branch_terms = contract_rows(attended, both_branch).astype(BF16)
    branch_terms = branch_terms.reshape(planes, part, model_dim)
    grad_attn = after(grad_attn, branch_terms)
    group = heads // 2

    def backward(grads, which, before=None):
        return attention_backward(
            scalars, order, turned, grads, attended, lse, cosine, sine_vals, slot_kv, blk, group, which, before
        )

    def deal_rows(terms):
        return lax.all_to_all(terms.reshape(places, planes * (depth // places), -1), ("chip", "core"), 0, 0, tiled=False)

    branch_dealt = lax.all_to_all(branch_terms, "chip", 0, 0, tiled=False)
    up_term = contract_rows(*after((dup_all, normed_all), branch_terms)).astype(BF16)
    if chips == 4:
        out_passing = exchange(out_parts[3], "chip", 1), exchange(out_parts[4], "chip", 2)
    else:
        out_passing = ()
    grad_query_a, kv_terms_a = backward(after(grad_attn, up_term), 0)
    grad_query_a, kv_terms_a, out_passing, branch_dealt = lax.optimization_barrier(
        (grad_query_a, kv_terms_a, out_passing, branch_dealt)
    )
    branch_sum = jnp.sum(branch_dealt.astype(F32), axis=0)
    query_terms_a = contract_rows(both_normed, grad_query_a).astype(BF16)
    if chips == 4:
        out_near = (add_half(out_parts[1], out_passing[1], 1), add_half(out_parts[2], out_passing[0], 0))
    else:
        out_near = tuple(out_parts[k] for k in range(1, chips))
    branch_sum = branch_sum.reshape(planes, part // planes, model_dim)
    grad_query_b, kv_mine, kv_other = backward(
        after(grad_attn, out_near, query_terms_a, branch_sum), 1, kv_terms_a
    )
    out_arrived = [exchange(term, "chip", k + 1) for k, term in enumerate(out_near)]
    grad_w_out = sum_planes(branch_sum, plane)
    query_sums_a = deal_rows(query_terms_a)
    ffn_terms = [gate_term, over_planes(up_term), down_term]
    grad_query_b, kv_mine, kv_other, out_arrived, grad_w_out, ffn_terms, query_sums_a = lax.optimization_barrier(
        (grad_query_b, kv_mine, kv_other, out_arrived, grad_w_out, ffn_terms, query_sums_a)
    )
    kv_parts = with_layout_constraint(add_cores(kv_mine, kv_other), Layout((0, 1)))
    kv_parts = kv_parts.reshape(chips, local_len, 2 * HD)
    kv_parts = [with_layout_constraint(at(kv_parts, chip ^ k), Layout((0, 1))) for k in range(chips)]
    kv_arrived = [exchange(kv_parts[k], "chip", k) for k in range(1, chips)]
    out_arrived, ffn_terms, grad_query_b, query_sums_a = after(
        (out_arrived, ffn_terms, grad_query_b, query_sums_a), kv_parts
    )
    query_terms_b = contract_rows(both_normed, grad_query_b).astype(BF16)
    kv_arrived = after(kv_arrived, query_terms_b)
    ffn_terms = pack_units(after(ffn_terms, query_sums_a), places)
    ffn_terms = lax.all_to_all(after(ffn_terms, kv_arrived), ("chip", "core"), 0, 0, tiled=False)
    kv_total = kv_parts[0].astype(F32)
    for term in kv_arrived:
        kv_total = kv_total + term.astype(F32)
    kv_total = kv_total + jnp.where(live_rows, kv_cotangent[0].astype(F32), 0.0)
    kv_low = kv_total.astype(BF16).astype(F32)
    grad_key = rotate(kv_low[:, :HD], own_cosine, -own_sine)
    grad_kv = jnp.concatenate([grad_key, kv_low[:, HD:]], axis=1).astype(BF16)
    both_grad_kv = jnp.concatenate([grad_kv, swap_core(grad_kv)], axis=0)
    kv_half = lax.dynamic_slice_in_dim(both_grad_kv, core * HD, HD, 1)
    kv_weight_half = lax.dynamic_slice_in_dim(kv_full, core * HD, HD, 1)
    rows = depth // places
    first_row = (own * planes + plane) * rows
    other_row = ((own ^ 1) * planes + plane) * rows
    kept_rows = lax.dynamic_slice_in_dim(query_half, first_row, rows, 0)
    sent_rows = swap_core(lax.dynamic_slice_in_dim(query_half, other_row, rows, 0))
    own_query_rows = jnp.where(
        core == 0, jnp.stack([kept_rows, sent_rows]), jnp.stack([sent_rows, kept_rows])
    )
    own_kv_rows = lax.dynamic_slice_in_dim(kv_full, first_row, rows, 0)
    both_query = jnp.concatenate([grad_query_a, grad_query_b], axis=1)

    def normed_one_term(rows):
        return contract_cols(both_query[rows], query_half) + contract_cols(kv_half[rows], kv_weight_half)

    gains = jnp.pad(grad_gain_two[:, None], ((0, 0), (0, HD - 1)))
    kv_grads = jnp.concatenate([contract_rows(both_normed, kv_half), gains], axis=1).astype(BF16)
    last_terms = jnp.concatenate([query_terms_b, kv_grads], axis=1)
    last_terms = with_layout_constraint(last_terms, Layout((0, 1)))
    last_dealt = deal_rows(after(last_terms, ffn_terms))
    first_planes = split_planes(after(query_sums_a, last_terms), plane, planes)
    first_arrived = [exchange(first_planes[k], "fsdp", k) for k in range(1, planes)]
    both_query = after(both_query, last_terms)
    other_one = swap_core(normed_one_term(slice(local_len, None)).astype(BF16))

    grad_normed_one = normed_one_term(slice(0, local_len)) + other_one.astype(F32)
    unit_one = tokens_flat * inverse_one
    scaled_one = grad_normed_one * gain_one
    grad_tokens = grad_residual + inverse_one * (
        scaled_one - unit_one * jnp.mean(scaled_one * unit_one, axis=1, keepdims=True)
    )
    grad_tokens = grad_tokens.astype(BF16)
    out_arrived = after(out_arrived, last_terms)
    ffn_out = out_parts[0].astype(F32)
    for term in out_arrived:
        ffn_out = ffn_out + term.astype(F32)
    output = jnp.where(live_rows, residual + ffn_out, 0.0).astype(BF16)

    ffn_grads = turn_units(after(ffn_terms, last_terms))
    last_dealt = after(last_dealt, grad_tokens, output, ffn_grads)
    last_planes = split_planes(last_dealt, plane, planes)
    last_arrived = [exchange(last_planes[k], "fsdp", k) for k in range(1, planes)]
    query_sums_a = first_planes[0].astype(F32)
    for term in after(first_arrived, last_planes[0]):
        query_sums_a = query_sums_a + term.astype(F32)
    last_sums = last_planes[0].astype(F32)
    for term in last_arrived:
        last_sums = last_sums + term.astype(F32)
    query_sums = jnp.concatenate([query_sums_a, last_sums[:, :, : -2 * HD]], axis=2)
    kv_sums = last_sums[:, :, -2 * HD :]

    own_gain = lax.dynamic_slice_in_dim(gain_one, first_row, rows, 0)
    grad_gain_one = (
        jnp.sum(own_query_rows.astype(F32) * query_sums, axis=(0, 2))
        + jnp.sum(own_kv_rows.astype(F32) * jnp.concatenate([kv_sums[0, :, :HD], kv_sums[1, :, :HD]], axis=1), axis=1)
    ) / own_gain
    grad_gain_two = kv_sums[0, :, HD] + kv_sums[1, :, HD]
    grad_w_query = alternate(query_sums[0], query_sums[1], part)
    grad_w_kv = jnp.concatenate([kv_sums[0, :, :HD], kv_sums[1, :, :HD]], axis=1)
    return (
        output[None],
        grad_tokens.astype(BF16)[None],
        grad_w_query,
        grad_w_kv,
        grad_w_out,
        grad_gain_one,
        grad_gain_two,
        ffn_grads[0],
        ffn_grads[1],
        ffn_grads[2],
    )


def solution(mesh):
    ctx, planes = mesh.shape["ctx"], mesh.shape["fsdp"]
    split = Mesh(mesh.devices.reshape(ctx // 2, 2, planes), ("chip", "core", "fsdp"))
    ctx_axes = ("chip", "core")
    return jax.shard_map(
        shards,
        mesh=split,
        in_specs=(
            P("fsdp", ctx_axes, None),
            P("fsdp", ctx_axes, None),
            P("fsdp", ctx_axes, None),
            P("fsdp"),
            P("fsdp", None),
            P("fsdp", None),
            P("fsdp", None),
            P("fsdp", None),
            P("fsdp"),
            P("fsdp"),
            P(None, "fsdp"),
            P(None, "fsdp"),
            P(None, "fsdp"),
        ),
        out_specs=(
            P("fsdp", ctx_axes, None),
            P("fsdp", ctx_axes, None),
            P(("chip", "core", "fsdp"), None),
            P(("chip", "core", "fsdp"), None),
            P(("chip", "core", "fsdp"), None),
            P(("chip", "core", "fsdp")),
            P(("chip", "core", "fsdp")),
            P(ctx_axes, "fsdp"),
            P(ctx_axes, "fsdp"),
            P(ctx_axes, "fsdp"),
        ),
        check_vma=False,
    )
```

```python
import functools

import jax
import jax.numpy as jnp
from jax import lax
from jax.experimental import pallas as pl
from jax.experimental.layout import Layout, with_layout_constraint
from jax.experimental.pallas import tpu as pltpu
from jax.sharding import Mesh
from jax.sharding import PartitionSpec as P

H = 16
HD = 128
HALF = HD // 2
MASKED = -1e30
LN2 = 0.6931471805599453
LOG2E = 1.4426950408889634
EPSILON = 1e-05
ROPE_BASE = 10000.0
BF16 = jnp.bfloat16
F32 = jnp.float32


def block_places(order_ref, place_ref, own):
    count = order_ref.shape[0]
    for stored in range(count):
        device = stored // 2
        place_ref[order_ref[stored]] = ((device ^ own) % 2 * (count // 4) + device // 2) * 2 + stored % 2


def causal(blk, group):
    keys = lax.broadcasted_iota(jnp.int32, (blk, blk), 0)
    rows = lax.broadcasted_iota(jnp.int32, (blk, blk), 1)
    return jnp.concatenate([keys <= rows] * group, axis=1)


def row_position(order_ref, own, row_block):
    return order_ref[2 * (own ^ (row_block // 2)) + row_block % 2]


def attend_forward(group, blk, scal_ref, order_ref, q_ref, cos_ref, sin_ref, kv_ref, out_ref, lse_ref, qt_ref, place_ref, vt_ref, acc_ref, max_ref, sum_ref):
    row_block = pl.program_id(0)
    own, length = scal_ref[0], scal_ref[1]

    @pl.when(row_block == 0)
    def _():
        block_places(order_ref, place_ref, own)
        for piece in range(order_ref.shape[0]):
            cells = slice(piece * blk, (piece + 1) * blk)
            vt_ref[:, cells] = kv_ref[cells, HD:].T

    mine = row_position(order_ref, own, row_block)

    def step(places, masked):
        starts = [pl.multiple_of(place * blk, blk) for place in places]
        scores = [
            jnp.dot(kv_ref[pl.ds(start, blk), :HD], qt_ref[0], preferred_element_type=F32)
            for start in starts
        ]
        if masked:
            scores = [jnp.where(causal(blk, group), part, MASKED) for part in scores]
        old = max_ref[...]
        new = old
        for part in scores:
            new = jnp.maximum(new, jnp.max(part, axis=0, keepdims=True))
        scale = jnp.exp2(old - new)
        total = sum_ref[...] * scale
        acc = acc_ref[...] * scale
        for start, part in zip(starts, scores):
            weights = jnp.exp2(part - new)
            total = total + jnp.sum(weights, axis=0, keepdims=True)
            acc = acc + jnp.dot(
                vt_ref[:, pl.ds(start, blk)], weights.astype(BF16), preferred_element_type=F32
            )
        max_ref[...] = new
        sum_ref[...] = total
        acc_ref[...] = acc

    @pl.when(mine * blk < length)
    def _():
        cosine, sine = cos_ref[...], sin_ref[...]
        for head in range(group):
            query = q_ref[:, head * HD : (head + 1) * HD].T
            first, second = query[:HALF], query[HALF:]
            turned = jnp.concatenate(
                [first * cosine - second * sine, second * cosine + first * sine], axis=0
            )
            qt_ref[0, :, head * blk : (head + 1) * blk] = (turned * (LOG2E * HD**-0.5)).astype(BF16)
        max_ref[...] = jnp.full(max_ref.shape, MASKED, F32)
        sum_ref[...] = jnp.zeros(sum_ref.shape, F32)
        acc_ref[...] = jnp.zeros(acc_ref.shape, F32)
        step([place_ref[mine]], True)

        def body(j, carried):
            step([place_ref[2 * j], place_ref[2 * j + 1]], False)
            return carried

        lax.fori_loop(0, mine // 2, body, 0)

        @pl.when(mine % 2 == 1)
        def _():
            step([place_ref[mine - 1]], False)

        total = sum_ref[...]
        result = acc_ref[...] * (1.0 / total)
        for head in range(group):
            out_ref[:, head * HD : (head + 1) * HD] = (
                result[:, head * blk : (head + 1) * blk].T.astype(BF16)
            )
        lse_ref[0] = max_ref[...] + jnp.log2(total)

    @pl.when(mine * blk >= length)
    def _():
        out_ref[...] = jnp.zeros(out_ref.shape, BF16)
        lse_ref[...] = jnp.zeros(lse_ref.shape, F32)
        qt_ref[...] = jnp.zeros(qt_ref.shape, BF16)


def attention_forward(scalars, order, queries, cosine, sine, keys_values, blk):
    rows, width = queries.shape
    span = keys_values.shape[0]
    row_blocks, heads = rows // blk, width // HD
    table = pl.BlockSpec((HALF, blk), lambda i, *_: (0, i))
    per_block = lambda *dims: pl.BlockSpec((1,) + dims, lambda i, *_: (i, 0, 0))
    return pl.pallas_call(
        functools.partial(attend_forward, heads, blk),
        grid_spec=pltpu.PrefetchScalarGridSpec(
            num_scalar_prefetch=2,
            grid=(row_blocks,),
            in_specs=[
                pl.BlockSpec((blk, width), lambda i, *_: (i, 0)),
                table,
                table,
                pl.BlockSpec((span, 2 * HD), lambda i, *_: (0, 0)),
            ],
            out_specs=[
                pl.BlockSpec((blk, width), lambda i, *_: (i, 0)),
                per_block(1, heads * blk),
                per_block(HD, heads * blk),
            ],
            scratch_shapes=[
                pltpu.SMEM((order.shape[0],), jnp.int32),
                pltpu.VMEM((HD, span), BF16),
                pltpu.VMEM((HD, heads * blk), F32),
                pltpu.VMEM((1, heads * blk), F32),
                pltpu.VMEM((1, heads * blk), F32),
            ],
        ),
        out_shape=[
            jax.ShapeDtypeStruct((rows, width), BF16),
            jax.ShapeDtypeStruct((row_blocks, 1, heads * blk), F32),
            jax.ShapeDtypeStruct((row_blocks, HD, heads * blk), BF16),
        ],
        compiler_params=pltpu.CompilerParams(vmem_limit_bytes=40 * 2**20),
        cost_estimate=pl.CostEstimate(flops=2**20, bytes_accessed=2**16, transcendentals=0),
        name="attend_forward",
    )(scalars, order, queries, cosine, sine, keys_values)


def attend_backward(group, blk, last, scal_ref, order_ref, qt_ref, g_ref, a_ref, lse_ref, cos_ref, sin_ref, kv_ref, *rest):
    if last:
        before_ref, dq_ref, mine_ref, other_ref, place_ref, gt_ref, qs_ref, gs_ref, kt_ref, acc_ref, delta_ref, dkv_ref = rest
    else:
        dq_ref, dkv_ref, place_ref, gt_ref, qs_ref, gs_ref, kt_ref, acc_ref, delta_ref = rest
    row_block = pl.program_id(0)
    own, length = scal_ref[0], scal_ref[1]

    @pl.when(row_block == 0)
    def _():
        block_places(order_ref, place_ref, own)
        for piece in range(order_ref.shape[0]):
            cells = slice(piece * blk, (piece + 1) * blk)
            kt_ref[:, cells] = kv_ref[cells, :HD].T
        dkv_ref[...] = before_ref[...] if last else jnp.zeros(dkv_ref.shape, F32)

    mine = row_position(order_ref, own, row_block)

    def step(place, masked):
        start = pl.multiple_of(place * blk, blk)
        scores = jnp.dot(kv_ref[pl.ds(start, blk), :HD], qt_ref[0], preferred_element_type=F32)
        weights = jnp.exp2(scores - lse_ref[0])
        if masked:
            weights = jnp.where(causal(blk, group), weights, 0.0)
        grads = jnp.dot(kv_ref[pl.ds(start, blk), HD:], gt_ref[...], preferred_element_type=F32)
        dscores = (weights * (grads - delta_ref[...])).astype(BF16)
        dkv_ref[pl.ds(start, blk), HD:] += jnp.dot(
            weights.astype(BF16), gs_ref[...], preferred_element_type=F32
        )
        dkv_ref[pl.ds(start, blk), :HD] += jnp.dot(dscores, qs_ref[...], preferred_element_type=F32)
        acc_ref[...] += jnp.dot(kt_ref[:, pl.ds(start, blk)], dscores, preferred_element_type=F32)

    @pl.when(mine * blk < length)
    def _():
        for head in range(group):
            lanes = slice(head * HD, (head + 1) * HD)
            cells = slice(head * blk, (head + 1) * blk)
            grad = g_ref[:, lanes]
            gt_ref[:, cells] = grad.T
            qs_ref[cells, :] = qt_ref[0, :, cells].T
            gs_ref[cells, :] = grad
            product = grad.astype(F32) * a_ref[:, lanes].astype(F32)
            delta_ref[:, cells] = jnp.sum(product.T, axis=0, keepdims=True)
        acc_ref[...] = jnp.zeros(acc_ref.shape, F32)
        step(place_ref[mine], True)

        def body(j, carried):
            step(place_ref[2 * j], False)
            step(place_ref[2 * j + 1], False)
            return carried

        lax.fori_loop(0, mine // 2, body, 0)

        @pl.when(mine % 2 == 1)
        def _():
            step(place_ref[mine - 1], False)

        cosine, sine = cos_ref[...], sin_ref[...]
        for head in range(group):
            turned = acc_ref[:, head * blk : (head + 1) * blk].astype(BF16).astype(F32)
            first, second = turned[:HALF], turned[HALF:]
            grad = jnp.concatenate(
                [first * cosine + second * sine, second * cosine - first * sine], axis=0
            )
            dq_ref[:, head * HD : (head + 1) * HD] = (grad * HD**-0.5).T.astype(BF16)

    @pl.when(mine * blk >= length)
    def _():
        dq_ref[...] = jnp.zeros(dq_ref.shape, BF16)

    if last:

        @pl.when(row_block == pl.num_programs(0) - 1)
        def _():
            half = mine_ref.shape[0]
            for total_ref, rows in ((mine_ref, slice(0, half)), (other_ref, slice(half, 2 * half))):
                total_ref[:, :HD] = (dkv_ref[rows, :HD] * LN2).astype(BF16)
                total_ref[:, HD:] = dkv_ref[rows, HD:].astype(BF16)


def attention_backward(scalars, order, turned, grads, attended, lse, cosine, sine, keys_values, blk, group, which, before=None):
    last = before is not None
    rows = grads.shape[0]
    span = keys_values.shape[0]
    row_blocks = rows // blk
    whole = pl.BlockSpec((span, 2 * HD), lambda i, *_: (0, 0))
    table = pl.BlockSpec((HALF, blk), lambda i, *_: (0, i))
    rowspec = pl.BlockSpec((blk, group * HD), lambda i, *_: (i, which))
    per_block = lambda *dims: pl.BlockSpec((1,) + dims, lambda i, *_: (i, 0, which))
    return pl.pallas_call(
        functools.partial(attend_backward, group, blk, last),
        grid_spec=pltpu.PrefetchScalarGridSpec(
            num_scalar_prefetch=2,
            grid=(row_blocks,),
            in_specs=[
                per_block(HD, group * blk),
                rowspec,
                rowspec,
                per_block(1, group * blk),
                table,
                table,
                whole,
            ]
            + [whole] * last,
            out_specs=[
                pl.BlockSpec((blk, group * HD), lambda i, *_: (i, 0)),
            ]
            + ([pl.BlockSpec((span // 2, 2 * HD), lambda i, *_: (0, 0))] * 2 if last else [whole]),
            scratch_shapes=[
                pltpu.SMEM((order.shape[0],), jnp.int32),
                pltpu.VMEM((HD, group * blk), BF16),
                pltpu.VMEM((group * blk, HD), BF16),
                pltpu.VMEM((group * blk, HD), BF16),
                pltpu.VMEM((HD, span), BF16),
                pltpu.VMEM((HD, group * blk), F32),
                pltpu.VMEM((1, group * blk), F32),
            ]
            + [pltpu.VMEM((span, 2 * HD), F32)] * last,
        ),
        out_shape=[
            jax.ShapeDtypeStruct((rows, group * HD), BF16),
        ]
        + (
            [jax.ShapeDtypeStruct((span // 2, 2 * HD), BF16)] * 2
            if last
            else [jax.ShapeDtypeStruct((span, 2 * HD), F32)]
        ),
        compiler_params=pltpu.CompilerParams(vmem_limit_bytes=48 * 2**20),
        cost_estimate=pl.CostEstimate(flops=2**20, bytes_accessed=2**16, transcendentals=0),
        name="attend_backward",
    )(scalars, order, turned, grads, attended, lse, cosine, sine, keys_values, *([before] if last else []))


def ffn_rows(count, tiles, place_ref, xa_ref, xb_ref, ga_ref, gb_ref, gate_ref, up_ref, down_ref, *rest):
    back_a, back_b, out_a, out_b, x_all, g_all, hidden_all, dgate_all, dup_all = rest[count:]
    units = gate_ref.shape[0] * gate_ref.shape[2]
    gate_rows, up_rows, down_rows = (ref[...].reshape(units, -1) for ref in (gate_ref, up_ref, down_ref))
    nt = (((1,), (1,)), ((), ()))
    early = pl.program_id(0) < tiles
    x = jnp.where(early, xa_ref[...], xb_ref[...])
    grad = jnp.where(early, ga_ref[...], gb_ref[...])
    gate = lax.dot_general(x, gate_rows, nt, preferred_element_type=F32)
    up = lax.dot_general(x, up_rows, nt, preferred_element_type=F32)
    dhidden = lax.dot_general(grad, down_rows, nt, preferred_element_type=F32)
    dhidden = dhidden.astype(BF16).astype(F32)
    sigmoid = jax.nn.sigmoid(gate)
    silu = gate * sigmoid
    hidden = (silu * up).astype(BF16)
    dgate = (dhidden * up * sigmoid * (1.0 + gate * (1.0 - sigmoid))).astype(BF16)
    dup = (dhidden * silu).astype(BF16)
    out = jnp.dot(hidden, down_rows, preferred_element_type=F32).astype(BF16)
    step = 512 if x.shape[1] % 512 == 0 else x.shape[1]
    back = jnp.concatenate(
        [
            (
                jnp.dot(dgate, gate_rows[:, at_col : at_col + step], preferred_element_type=F32)
                + jnp.dot(dup, up_rows[:, at_col : at_col + step], preferred_element_type=F32)
            ).astype(BF16)
            for at_col in range(0, x.shape[1], step)
        ],
        axis=1,
    )
    x_all[...] = x
    g_all[...] = grad
    hidden_all[...] = hidden
    dgate_all[...] = dgate
    dup_all[...] = dup

    @pl.when(early)
    def _():
        back_a[...] = back
        out_a[...] = out

    @pl.when(jnp.logical_not(early))
    def _():
        back_b[...] = back
        out_b[...] = out


def ffn_pair(place, pairs, xa, xb, ga, gb, weights, kept):
    rows, model_dim = xa.shape
    planes, _, share, _ = weights.shape
    units = planes * share
    tile = min(256, rows)
    tiles = rows // tile
    weight = lambda which: pl.BlockSpec(
        (planes, 1, share, model_dim), lambda i, *_: (0, which, 0, 0), pipeline_mode=pl.Buffered(1)
    )
    turn_a = lambda i: jnp.minimum(i, tiles - 1)
    turn_b = lambda i: jnp.maximum(i - tiles, 0)
    block = lambda index: pl.BlockSpec((tile, model_dim), index)
    here_a, here_b = block(lambda i, *_: (turn_a(i), 0)), block(lambda i, *_: (turn_b(i), 0))
    out_a = block(lambda i, place_ref: (place_ref[0] * tiles + turn_a(i), 0))
    out_b = block(lambda i, place_ref: (place_ref[0] * tiles + turn_b(i), 0))
    there = lambda wide: pl.BlockSpec((tile, wide), lambda i, place_ref: (place_ref[0] * 2 * tiles + i, 0))
    count = len(kept)
    shape = lambda tall, wide: jax.ShapeDtypeStruct((tall, wide), BF16)
    return pl.pallas_call(
        functools.partial(ffn_rows, count, tiles),
        grid_spec=pltpu.PrefetchScalarGridSpec(
            num_scalar_prefetch=1,
            grid=(2 * tiles,),
            in_specs=[here_a, here_b, here_a, here_b, weight(0), weight(1), weight(2)]
            + [pl.BlockSpec(memory_space=pl.ANY)] * count,
            out_specs=[here_a, here_b, out_a, out_b] + [there(model_dim)] * 2 + [there(units)] * 3,
        ),
        out_shape=[shape(rows, model_dim)] * 2
        + [shape(pairs * rows, model_dim)] * 2
        + [shape(pairs * 2 * rows, model_dim)] * 2
        + [shape(pairs * 2 * rows, units)] * 3,
        input_output_aliases={8 + i: 2 + i for i in range(count)},
        compiler_params=pltpu.CompilerParams(vmem_limit_bytes=52 * 2**20),
        cost_estimate=pl.CostEstimate(flops=2**20, bytes_accessed=2**16, transcendentals=0),
        name="ffn_pair",
    )(place, xa, xb, ga, gb, weights, weights, weights, *kept)


def pack_columns(*refs):
    out_ref = refs[-1]
    columns = out_ref.shape[3]
    for which, in_ref in enumerate(refs[:-1]):
        for place in range(out_ref.shape[0]):
            out_ref[place, which] = in_ref[:, place * columns : (place + 1) * columns]


def pack_units(terms, places):
    share, columns = terms[0].shape
    if share % 16:
        return jnp.stack(terms).reshape(len(terms), share, places, columns // places).transpose(2, 0, 1, 3)
    return pl.pallas_call(
        pack_columns,
        out_shape=jax.ShapeDtypeStruct((places, len(terms), share, columns // places), BF16),
        compiler_params=pltpu.CompilerParams(vmem_limit_bytes=32 * 2**20),
        cost_estimate=pl.CostEstimate(flops=2**16, bytes_accessed=len(terms) * terms[0].size * 4, transcendentals=0),
        name="pack_units",
    )(*terms)


def turn_rows(in_ref, *out_refs):
    for which, out_ref in enumerate(out_refs):
        out_ref[...] = in_ref[:, which].reshape(out_ref.shape[1], out_ref.shape[0]).T.astype(F32)


def turn_units(terms):
    places, count, share, columns = terms.shape
    if share % 16:
        turned = terms.transpose(1, 3, 0, 2).reshape(count, columns, places * share).astype(F32)
        return [turned[which] for which in range(count)]
    return pl.pallas_call(
        turn_rows,
        out_shape=[jax.ShapeDtypeStruct((columns, places * share), F32)] * count,
        compiler_params=pltpu.CompilerParams(vmem_limit_bytes=32 * 2**20),
        cost_estimate=pl.CostEstimate(flops=2**20, bytes_accessed=terms.size * 6, transcendentals=0),
        name="turn_units",
    )(terms)


def alternate_columns(part, first_ref, second_ref, out_ref):
    for at_col in range(0, first_ref.shape[1], part):
        out_ref[:, 2 * at_col : 2 * at_col + part] = first_ref[:, at_col : at_col + part]
        out_ref[:, 2 * at_col + part : 2 * at_col + 2 * part] = second_ref[:, at_col : at_col + part]


def alternate(first, second, part):
    rows, width = first.shape
    return pl.pallas_call(
        functools.partial(alternate_columns, part),
        out_shape=jax.ShapeDtypeStruct((rows, 2 * width), F32),
        cost_estimate=pl.CostEstimate(flops=2**16, bytes_accessed=first.size * 16, transcendentals=0),
        name="alternate",
    )(first, second)


def sum_chips(plane_ref, dealt_ref, *out_refs):
    rows = out_refs[0].shape[1]
    for k, out_ref in enumerate(out_refs):
        start = pl.multiple_of((plane_ref[0] ^ k) * rows, rows)
        for core in range(2):
            total = dealt_ref[core, pl.ds(start, rows), :].astype(F32)
            for place in range(2 + core, dealt_ref.shape[0], 2):
                total = total + dealt_ref[place, pl.ds(start, rows), :].astype(F32)
            out_ref[core] = total.astype(BF16)


def split_planes(dealt, plane, planes):
    rows, columns = dealt.shape[1] // planes, dealt.shape[2]
    return pl.pallas_call(
        sum_chips,
        grid_spec=pltpu.PrefetchScalarGridSpec(
            num_scalar_prefetch=1,
            grid=(1,),
            in_specs=[pl.BlockSpec(dealt.shape, lambda i, *_: (0, 0, 0), pipeline_mode=pl.Buffered(1))],
            out_specs=[pl.BlockSpec((2, rows, columns), lambda i, *_: (0, 0, 0))] * planes,
        ),
        out_shape=[jax.ShapeDtypeStruct((2, rows, columns), BF16)] * planes,
        compiler_params=pltpu.CompilerParams(vmem_limit_bytes=32 * 2**20),
        cost_estimate=pl.CostEstimate(flops=2**20, bytes_accessed=dealt.size * 3, transcendentals=0),
        name="sum_chips",
    )(plane.reshape(1).astype(jnp.int32), dealt)


def angles(positions):
    frequency = ROPE_BASE ** (-2.0 * jnp.arange(HALF, dtype=F32) / HD)
    phase_angle = frequency[:, None] * positions.astype(F32)[None, :]
    return (jnp.cos(phase_angle), jnp.sin(phase_angle))


def rotate(vectors, cosine, sine_vals):
    first_half = vectors[..., :HALF]
    second_half = vectors[..., HALF:]
    return jnp.concatenate(
        [
            first_half * cosine - second_half * sine_vals,
            second_half * cosine + first_half * sine_vals,
        ],
        axis=-1,
    )


def matmul(left, right):
    return jnp.dot(left, right, preferred_element_type=F32)


def contract_rows(left, right):
    return lax.dot_general(left, right, (((0,), (0,)), ((), ())), preferred_element_type=F32)


def contract_cols(left, right):
    return lax.dot_general(left, right, (((1,), (1,)), ((), ())), preferred_element_type=F32)


def after(value, *earlier):
    return lax.optimization_barrier((value, earlier))[0]


def exchange(value, axis, distance):
    size = lax.axis_size(axis)
    return lax.ppermute(value, axis, [(i, i ^ distance) for i in range(size)])


def swap_core(value):
    return exchange(value, "core", 1)


def spread_chips(value):
    chips = lax.axis_size("chip")
    copies = jnp.broadcast_to(value[None], (chips,) + value.shape)
    return lax.all_to_all(copies, "chip", 0, 0, tiled=False)


def gather_near(value):
    if lax.axis_size("chip") != 4:
        return [value] + [exchange(value, "chip", k) for k in range(1, lax.axis_size("chip"))]
    return [value, exchange(value, "chip", 1), exchange(value, "chip", 2)]


def send_far(near):
    if lax.axis_size("chip") != 4:
        return ()
    value, first, second = lax.optimization_barrier(near)
    half = value.shape[0] // 2
    first, second = lax.optimization_barrier((first[:half], second[half:]))
    return exchange(first, "chip", 2), exchange(second, "chip", 1)


def gather_far(near):
    halves = lax.optimization_barrier(send_far(near))
    return near + [jnp.concatenate(halves, axis=0)] if halves else near


def gather_chips(value):
    return gather_far(gather_near(value))


def add_cores(terms, terms_of_other):
    return (terms.astype(F32) + swap_core(terms_of_other.astype(BF16)).astype(F32)).astype(BF16)


def deal(terms, axis):
    dealt = lax.all_to_all(terms.astype(BF16), axis, 0, 0, tiled=False)
    return jnp.sum(dealt.astype(F32), axis=0)


def at(value, index, axis=0):
    return lax.dynamic_index_in_dim(value, index, axis, keepdims=False)


def sum_planes(terms, plane):
    total = at(terms, plane).astype(F32)
    for k in range(1, lax.axis_size("fsdp")):
        total = total + exchange(at(terms, plane ^ k).astype(BF16), "fsdp", k).astype(F32)
    return total


def reduce_far(last):
    half = last.shape[0] // 2
    return exchange(last[:half], "chip", 1), exchange(last[half:], "chip", 2)


def add_half(term, passing, which):
    pad = term.shape[0] - passing.shape[0]
    passing = jnp.pad(passing, ((pad, 0) if which else (0, pad), (0, 0)))
    return (term.astype(F32) + passing.astype(F32)).astype(BF16)


def lay_columns(chunks, chip):
    rows, width = chunks[0].shape
    whole = jnp.zeros((rows, width * len(chunks)), chunks[0].dtype)
    for k, chunk in enumerate(chunks):
        whole = lax.dynamic_update_slice(whole, chunk, (0, (chip ^ k) * width))
    return whole


def shards(
    tokens,
    cotangent,
    kv_cotangent,
    lengths,
    block_order,
    w_query,
    w_kv,
    w_out,
    gain_attn,
    gain_ffn,
    w_gate,
    w_up,
    w_down,
):
    local_len, model_dim = tokens.shape[1:]
    chips, planes = lax.axis_size("chip"), lax.axis_size("fsdp")
    chip, core, plane = lax.axis_index("chip"), lax.axis_index("core"), lax.axis_index("fsdp")
    own = chip * 2 + core
    places = chips * 2
    blk = local_len // 2
    order, length = block_order[0], lengths[0]
    depth = w_query.shape[0]

    part = depth // 2
    wide = part * planes
    out_cols = model_dim // chips
    kv_rows = depth // chips
    gain_rows = depth // (2 * HD)
    narrow = lambda value: value.reshape(-1, 2 * HD)
    pieces = [
        lax.dynamic_slice(w_query, (0, chip * 2 * part + core * part), (depth, part)),
        lax.dynamic_slice(w_out, (core * part, chip * out_cols), (part, out_cols)),
        lax.dynamic_slice_in_dim(w_kv, chip * kv_rows, kv_rows, 0),
        gain_attn,
        gain_ffn,
    ]
    heights = [piece.size // (2 * HD) for piece in pieces]
    packed = jnp.concatenate([narrow(piece) for piece in pieces], axis=0)
    packed = lax.all_gather(packed, "fsdp", axis=0)
    bounds = [sum(heights[: i + 1]) for i in range(4)]
    query_piece, out_piece, kv_piece, gain_one, gain_two = jnp.split(packed, bounds, axis=1)
    out_piece = out_piece.reshape(wide, out_cols)
    gain_one = gain_one.reshape(model_dim).astype(F32)
    gain_two = gain_two.reshape(model_dim).astype(F32)
    share = w_gate.shape[1] // places
    pieces = jnp.stack(
        [
            lax.dynamic_slice(weight, (0, own * share), (model_dim, share)).T
            for weight in (w_gate, w_up, w_down)
        ]
    )
    query_piece = query_piece.reshape(model_dim, part)
    own_pos = jnp.repeat(lax.dynamic_slice_in_dim(order, own * 2, 2, 0) * blk, blk) + (
        jnp.arange(local_len, dtype=jnp.int32) % blk
    )
    live_rows = (own_pos < length)[:, None]
    grad_out = jnp.where(live_rows, cotangent[0], jnp.zeros((), BF16))
    grad_near = after(gather_near(grad_out), pieces)
    kv_full = spread_chips(after(kv_piece, grad_near)).swapaxes(0, 1).reshape(model_dim, 2 * HD)
    kv_full = with_layout_constraint(kv_full, Layout((0, 1)))
    query_near = gather_near(after(query_piece, grad_near))
    query_half = lay_columns(gather_far(query_near), chip)
    grad_others = [swap_core(chunk) for chunk in after(grad_near, query_near)]
    grad_far = send_far(after(grad_near, query_half, grad_others))
    out_chunks = spread_chips(after(out_piece, query_half))
    ffn_weights = lax.all_gather(pieces, "fsdp", axis=0)

    offsets = jnp.arange(blk, dtype=jnp.int32)
    mine = lax.dynamic_slice_in_dim(order, own * 2, 2, 0)
    theirs = lax.dynamic_slice_in_dim(order, (own ^ 1) * 2, 2, 0)
    both_pos = (jnp.concatenate([mine, theirs])[:, None] * blk + offsets[None, :]).reshape(-1)
    cosine, sine_vals = angles(both_pos)
    own_cosine, own_sine = cosine[:, :local_len].T, sine_vals[:, :local_len].T

    tokens_low = tokens[0]
    tokens_flat = tokens_low.astype(F32)
    both_tokens = jnp.concatenate([tokens_low, swap_core(tokens_low)], axis=0).astype(F32)
    both_inverse = lax.rsqrt(jnp.mean(both_tokens * both_tokens, axis=1, keepdims=True) + EPSILON)
    both_normed = (both_tokens * both_inverse * gain_one).astype(BF16)
    inverse_one = both_inverse[:local_len]

    key_value = matmul(both_normed[:local_len], kv_full)
    key_rot = rotate(key_value[:, :HD], own_cosine, own_sine)
    local_kv = jnp.concatenate([key_rot, key_value[:, HD:]], axis=1).astype(BF16)
    slot_kv = after(spread_chips(local_kv), query_half).reshape(-1, 2 * HD)
    slot_kv = jnp.concatenate([slot_kv, swap_core(slot_kv)], axis=0)

    heads = wide // HD
    queries = matmul(both_normed, query_half)
    scalars = jnp.stack([own, length]).astype(jnp.int32)
    attended, lse, turned = attention_forward(
        scalars, order, queries, cosine, sine_vals, slot_kv, blk
    )

    attended, lse, turned, out_chunks, grad_far = lax.optimization_barrier(
        (attended, lse, turned, out_chunks, grad_far)
    )
    grad_mine = list(grad_near)
    if grad_far:
        grad_mine.append(jnp.concatenate(grad_far, axis=0))
        grad_others.append(swap_core(grad_mine[3]))
    out_half = out_chunks.swapaxes(0, 1).reshape(wide, model_dim)
    branch_other = swap_core(matmul(attended[local_len:], out_half).astype(BF16))
    residual = tokens_flat + matmul(attended[:local_len], out_half) + branch_other.astype(F32)
    inverse_two = lax.rsqrt(jnp.mean(residual * residual, axis=1, keepdims=True) + EPSILON)
    unit_two = residual * inverse_two
    normed_ffn = (unit_two * gain_two).astype(BF16)
    def pair(at_place, chunk, kept):
        result = ffn_pair(
            jnp.full((1,), at_place, jnp.int32),
            chips,
            chunk,
            swap_core(chunk),
            grad_mine[at_place],
            grad_others[at_place],
            ffn_weights,
            kept,
        )
        return result[0], result[1], tuple(result[2:])

    normed_near = gather_near(normed_ffn)
    back_own, back_other, kept = pair(0, normed_near[0], ())
    back_other = swap_core(back_other)
    if chips == 4:
        normed_near = after(normed_near, back_own)
        normed_far = send_far(normed_near)
        own_first, other_first, kept = pair(1, normed_near[1], kept)
        normed_far = after(normed_far, own_first)
        own_last, other_last, kept = pair(3, jnp.concatenate(normed_far, axis=0), kept)
        last = add_cores(own_last, other_last)
        other_first = swap_core(other_first)
        kept = after(kept, last, other_first)
        passing = reduce_far(last)
        own_second, other_second, kept = pair(2, normed_near[2], kept)
        passing, own_second, other_second, kept = lax.optimization_barrier(
            (passing, own_second, other_second, kept)
        )
        first = add_half(own_first.astype(F32) + other_first.astype(F32), passing[1], 1)
        second = add_half(own_second.astype(F32) + swap_core(other_second).astype(F32), passing[0], 0)
        kept = after(kept, first, second)
        arrived = [exchange(first, "chip", 1), exchange(second, "chip", 2), back_other]
    else:
        normed_chunks = gather_far(after(normed_near, back_own))
        arrived = [back_other]
        for k in range(1, chips):
            own_term, other_term, kept = pair(k, normed_chunks[k], kept)
            arrived.append(exchange(add_cores(own_term, other_term), "chip", k))

    out_own, out_other, normed_all, grad_all, hidden_all, dgate_all, dup_all = kept
    down_term = contract_rows(hidden_all, grad_all).astype(BF16)
    out_other = swap_core(out_other)
    cuts = [0, 1, 2, 3, 3.5, 4] if chips == 4 else range(chips + 1)
    out_parts = [
        (out_own[int(a * local_len) : int(b * local_len)].astype(F32) + out_other[int(a * local_len) : int(b * local_len)].astype(F32)).astype(BF16)
        for a, b in zip(cuts[:-1], cuts[1:])
    ]
    gate_term = contract_rows(dgate_all, normed_all).astype(BF16)
    arrived = after(arrived, down_term, out_parts, gate_term)
    grad_normed = back_own.astype(F32)
    for term in arrived:
        grad_normed = grad_normed + term.astype(F32)
    out_parts = after(out_parts, arrived)

    def over_planes(term):
        return lax.psum_scatter(term, "fsdp", scatter_dimension=0, tiled=True)

    gate_term, down_term = over_planes(gate_term), over_planes(down_term)

    grad_gain_two = jnp.sum(grad_normed * unit_two, axis=0)
    scaled_two = grad_normed * gain_two
    grad_residual = grad_out.astype(F32) + inverse_two * (
        scaled_two - unit_two * jnp.mean(scaled_two * unit_two, axis=1, keepdims=True)
    )
    grad_branch = grad_residual.astype(BF16)
    both_branch = jnp.concatenate([grad_branch, swap_core(grad_branch)], axis=0)
    grad_attn = contract_cols(both_branch, out_half).astype(BF16)
    branch_terms = contract_rows(attended, both_branch).astype(BF16)
    branch_terms = branch_terms.reshape(planes, part, model_dim)
    grad_attn = after(grad_attn, branch_terms)
    group = heads // 2

    def backward(grads, which, before=None):
        return attention_backward(
            scalars, order, turned, grads, attended, lse, cosine, sine_vals, slot_kv, blk, group, which, before
        )

    def deal_rows(terms):
        return lax.all_to_all(terms.reshape(places, planes * (depth // places), -1), ("chip", "core"), 0, 0, tiled=False)

    branch_dealt = lax.all_to_all(branch_terms, "chip", 0, 0, tiled=False)
    up_term = contract_rows(*after((dup_all, normed_all), branch_terms)).astype(BF16)
    if chips == 4:
        out_passing = exchange(out_parts[3], "chip", 1), exchange(out_parts[4], "chip", 2)
    else:
        out_passing = ()
    grad_query_a, kv_terms_a = backward(after(grad_attn, up_term), 0)
    grad_query_a, kv_terms_a, out_passing, branch_dealt = lax.optimization_barrier(
        (grad_query_a, kv_terms_a, out_passing, branch_dealt)
    )
    branch_sum = jnp.sum(branch_dealt.astype(F32), axis=0)
    query_terms_a = contract_rows(both_normed, grad_query_a).astype(BF16)
    if chips == 4:
        out_near = (add_half(out_parts[1], out_passing[1], 1), add_half(out_parts[2], out_passing[0], 0))
    else:
        out_near = tuple(out_parts[k] for k in range(1, chips))
    branch_sum = branch_sum.reshape(planes, part // planes, model_dim)
    grad_query_b, kv_mine, kv_other = backward(
        after(grad_attn, out_near, query_terms_a, branch_sum), 1, kv_terms_a
    )
    out_arrived = [exchange(term, "chip", k + 1) for k, term in enumerate(out_near)]
    grad_w_out = sum_planes(branch_sum, plane)
    query_sums_a = deal_rows(query_terms_a)
    ffn_terms = [gate_term, over_planes(up_term), down_term]
    grad_query_b, kv_mine, kv_other, out_arrived, grad_w_out, ffn_terms, query_sums_a = lax.optimization_barrier(
        (grad_query_b, kv_mine, kv_other, out_arrived, grad_w_out, ffn_terms, query_sums_a)
    )
    kv_parts = with_layout_constraint(add_cores(kv_mine, kv_other), Layout((0, 1)))
    kv_parts = kv_parts.reshape(chips, local_len, 2 * HD)
    kv_parts = [with_layout_constraint(at(kv_parts, chip ^ k), Layout((0, 1))) for k in range(chips)]
    kv_arrived = [exchange(kv_parts[k], "chip", k) for k in range(1, chips)]
    out_arrived, ffn_terms, grad_query_b, query_sums_a = after(
        (out_arrived, ffn_terms, grad_query_b, query_sums_a), kv_parts
    )
    query_terms_b = contract_rows(both_normed, grad_query_b).astype(BF16)
    kv_arrived = after(kv_arrived, query_terms_b)
    ffn_terms = pack_units(after(ffn_terms, query_sums_a), places)
    ffn_terms = lax.all_to_all(after(ffn_terms, kv_arrived), ("chip", "core"), 0, 0, tiled=False)
    kv_total = kv_parts[0].astype(F32)
    for term in kv_arrived:
        kv_total = kv_total + term.astype(F32)
    kv_total = kv_total + jnp.where(live_rows, kv_cotangent[0].astype(F32), 0.0)
    kv_low = kv_total.astype(BF16).astype(F32)
    grad_key = rotate(kv_low[:, :HD], own_cosine, -own_sine)
    grad_kv = jnp.concatenate([grad_key, kv_low[:, HD:]], axis=1).astype(BF16)
    both_grad_kv = jnp.concatenate([grad_kv, swap_core(grad_kv)], axis=0)
    kv_half = lax.dynamic_slice_in_dim(both_grad_kv, core * HD, HD, 1)
    kv_weight_half = lax.dynamic_slice_in_dim(kv_full, core * HD, HD, 1)
    rows = depth // places
    first_row = (own * planes + plane) * rows
    other_row = ((own ^ 1) * planes + plane) * rows
    kept_rows = lax.dynamic_slice_in_dim(query_half, first_row, rows, 0)
    sent_rows = swap_core(lax.dynamic_slice_in_dim(query_half, other_row, rows, 0))
    own_query_rows = jnp.where(
        core == 0, jnp.stack([kept_rows, sent_rows]), jnp.stack([sent_rows, kept_rows])
    )
    own_kv_rows = lax.dynamic_slice_in_dim(kv_full, first_row, rows, 0)
    both_query = jnp.concatenate([grad_query_a, grad_query_b], axis=1)

    def normed_one_term(rows):
        return contract_cols(both_query[rows], query_half) + contract_cols(kv_half[rows], kv_weight_half)

    gains = jnp.pad(grad_gain_two[:, None], ((0, 0), (0, HD - 1)))
    kv_grads = jnp.concatenate([contract_rows(both_normed, kv_half), gains], axis=1).astype(BF16)
    last_terms = jnp.concatenate([query_terms_b, kv_grads], axis=1)
    last_terms = with_layout_constraint(last_terms, Layout((0, 1)))
    last_dealt = deal_rows(after(last_terms, ffn_terms))
    first_planes = split_planes(after(query_sums_a, last_terms), plane, planes)
    first_arrived = [exchange(first_planes[k], "fsdp", k) for k in range(1, planes)]
    both_query = after(both_query, last_terms)
    other_one = swap_core(normed_one_term(slice(local_len, None)).astype(BF16))

    grad_normed_one = normed_one_term(slice(0, local_len)) + other_one.astype(F32)
    unit_one = tokens_flat * inverse_one
    scaled_one = grad_normed_one * gain_one
    grad_tokens = grad_residual + inverse_one * (
        scaled_one - unit_one * jnp.mean(scaled_one * unit_one, axis=1, keepdims=True)
    )
    grad_tokens = grad_tokens.astype(BF16)
    out_arrived = after(out_arrived, last_terms)
    ffn_out = out_parts[0].astype(F32)
    for term in out_arrived:
        ffn_out = ffn_out + term.astype(F32)
    output = jnp.where(live_rows, residual + ffn_out, 0.0).astype(BF16)

    ffn_grads = turn_units(after(ffn_terms, last_terms))
    last_dealt = after(last_dealt, grad_tokens, output, ffn_grads)
    last_planes = split_planes(last_dealt, plane, planes)
    last_arrived = [exchange(last_planes[k], "fsdp", k) for k in range(1, planes)]
    query_sums_a = first_planes[0].astype(F32)
    for term in after(first_arrived, last_planes[0]):
        query_sums_a = query_sums_a + term.astype(F32)
    last_sums = last_planes[0].astype(F32)
    for term in last_arrived:
        last_sums = last_sums + term.astype(F32)
    query_sums = jnp.concatenate([query_sums_a, last_sums[:, :, : -2 * HD]], axis=2)
    kv_sums = last_sums[:, :, -2 * HD :]

    own_gain = lax.dynamic_slice_in_dim(gain_one, first_row, rows, 0)
    grad_gain_one = (
        jnp.sum(own_query_rows.astype(F32) * query_sums, axis=(0, 2))
        + jnp.sum(own_kv_rows.astype(F32) * jnp.concatenate([kv_sums[0, :, :HD], kv_sums[1, :, :HD]], axis=1), axis=1)
    ) / own_gain
    grad_gain_two = kv_sums[0, :, HD] + kv_sums[1, :, HD]
    grad_w_query = alternate(query_sums[0], query_sums[1], part)
    grad_w_kv = jnp.concatenate([kv_sums[0, :, :HD], kv_sums[1, :, :HD]], axis=1)
    return (
        output[None],
        grad_tokens.astype(BF16)[None],
        grad_w_query,
        grad_w_kv,
        grad_w_out,
        grad_gain_one,
        grad_gain_two,
        ffn_grads[0],
        ffn_grads[1],
        ffn_grads[2],
    )


def solution(mesh):
    ctx, planes = mesh.shape["ctx"], mesh.shape["fsdp"]
    split = Mesh(mesh.devices.reshape(ctx // 2, 2, planes), ("chip", "core", "fsdp"))
    ctx_axes = ("chip", "core")
    return jax.shard_map(
        shards,
        mesh=split,
        in_specs=(
            P("fsdp", ctx_axes, None),
            P("fsdp", ctx_axes, None),
            P("fsdp", ctx_axes, None),
            P("fsdp"),
            P("fsdp", None),
            P("fsdp", None),
            P("fsdp", None),
            P("fsdp", None),
            P("fsdp"),
            P("fsdp"),
            P(None, "fsdp"),
            P(None, "fsdp"),
            P(None, "fsdp"),
        ),
        out_specs=(
            P("fsdp", ctx_axes, None),
            P("fsdp", ctx_axes, None),
            P(("chip", "core", "fsdp"), None),
            P(("chip", "core", "fsdp"), None),
            P(("chip", "core", "fsdp"), None),
            P(("chip", "core", "fsdp")),
            P(("chip", "core", "fsdp")),
            P(ctx_axes, "fsdp"),
            P(ctx_axes, "fsdp"),
            P(ctx_axes, "fsdp"),
        ),
        check_vma=False,
    )
```

```python
import functools

import jax
import jax.numpy as jnp
from jax import lax
from jax.experimental import pallas as pl
from jax.experimental.layout import Layout, with_layout_constraint
from jax.experimental.pallas import tpu as pltpu
from jax.sharding import Mesh
from jax.sharding import PartitionSpec as P

H = 16
HD = 128
HALF = HD // 2
MASKED = -1e30
LN2 = 0.6931471805599453
LOG2E = 1.4426950408889634
EPSILON = 1e-05
ROPE_BASE = 10000.0
BF16 = jnp.bfloat16
F32 = jnp.float32


def block_places(order_ref, place_ref, own):
    count = order_ref.shape[0]
    for stored in range(count):
        device = stored // 2
        place_ref[order_ref[stored]] = ((device ^ own) % 2 * (count // 4) + device // 2) * 2 + stored % 2


def causal(blk, group):
    keys = lax.broadcasted_iota(jnp.int32, (blk, blk), 0)
    rows = lax.broadcasted_iota(jnp.int32, (blk, blk), 1)
    return jnp.concatenate([keys <= rows] * group, axis=1)


def row_position(order_ref, own, row_block):
    return order_ref[2 * (own ^ (row_block // 2)) + row_block % 2]


def attend_forward(group, blk, scal_ref, order_ref, q_ref, cos_ref, sin_ref, kv_ref, out_ref, lse_ref, qt_ref, place_ref, vt_ref, acc_ref, max_ref, sum_ref):
    row_block = pl.program_id(0)
    own, length = scal_ref[0], scal_ref[1]

    @pl.when(row_block == 0)
    def _():
        block_places(order_ref, place_ref, own)
        for piece in range(order_ref.shape[0]):
            cells = slice(piece * blk, (piece + 1) * blk)
            vt_ref[:, cells] = kv_ref[cells, HD:].T

    mine = row_position(order_ref, own, row_block)

    def step(places, masked):
        starts = [pl.multiple_of(place * blk, blk) for place in places]
        scores = [
            jnp.dot(kv_ref[pl.ds(start, blk), :HD], qt_ref[0], preferred_element_type=F32)
            for start in starts
        ]
        if masked:
            scores = [jnp.where(causal(blk, group), part, MASKED) for part in scores]
        old = max_ref[...]
        new = old
        for part in scores:
            new = jnp.maximum(new, jnp.max(part, axis=0, keepdims=True))
        scale = jnp.exp2(old - new)
        total = sum_ref[...] * scale
        acc = acc_ref[...] * scale
        for start, part in zip(starts, scores):
            weights = jnp.exp2(part - new)
            total = total + jnp.sum(weights, axis=0, keepdims=True)
            acc = acc + jnp.dot(
                vt_ref[:, pl.ds(start, blk)], weights.astype(BF16), preferred_element_type=F32
            )
        max_ref[...] = new
        sum_ref[...] = total
        acc_ref[...] = acc

    @pl.when(mine * blk < length)
    def _():
        cosine, sine = cos_ref[...], sin_ref[...]
        for head in range(group):
            query = q_ref[:, head * HD : (head + 1) * HD].T
            first, second = query[:HALF], query[HALF:]
            turned = jnp.concatenate(
                [first * cosine - second * sine, second * cosine + first * sine], axis=0
            )
            qt_ref[0, :, head * blk : (head + 1) * blk] = (turned * (LOG2E * HD**-0.5)).astype(BF16)
        max_ref[...] = jnp.full(max_ref.shape, MASKED, F32)
        sum_ref[...] = jnp.zeros(sum_ref.shape, F32)
        acc_ref[...] = jnp.zeros(acc_ref.shape, F32)
        step([place_ref[mine]], True)

        def body(j, carried):
            step([place_ref[2 * j], place_ref[2 * j + 1]], False)
            return carried

        lax.fori_loop(0, mine // 2, body, 0)

        @pl.when(mine % 2 == 1)
        def _():
            step([place_ref[mine - 1]], False)

        total = sum_ref[...]
        result = acc_ref[...] * (1.0 / total)
        for head in range(group):
            out_ref[:, head * HD : (head + 1) * HD] = (
                result[:, head * blk : (head + 1) * blk].T.astype(BF16)
            )
        lse_ref[0] = max_ref[...] + jnp.log2(total)

    @pl.when(mine * blk >= length)
    def _():
        out_ref[...] = jnp.zeros(out_ref.shape, BF16)
        lse_ref[...] = jnp.zeros(lse_ref.shape, F32)
        qt_ref[...] = jnp.zeros(qt_ref.shape, BF16)


def attention_forward(scalars, order, queries, cosine, sine, keys_values, blk):
    rows, width = queries.shape
    span = keys_values.shape[0]
    row_blocks, heads = rows // blk, width // HD
    table = pl.BlockSpec((HALF, blk), lambda i, *_: (0, i))
    per_block = lambda *dims: pl.BlockSpec((1,) + dims, lambda i, *_: (i, 0, 0))
    return pl.pallas_call(
        functools.partial(attend_forward, heads, blk),
        grid_spec=pltpu.PrefetchScalarGridSpec(
            num_scalar_prefetch=2,
            grid=(row_blocks,),
            in_specs=[
                pl.BlockSpec((blk, width), lambda i, *_: (i, 0)),
                table,
                table,
                pl.BlockSpec((span, 2 * HD), lambda i, *_: (0, 0)),
            ],
            out_specs=[
                pl.BlockSpec((blk, width), lambda i, *_: (i, 0)),
                per_block(1, heads * blk),
                per_block(HD, heads * blk),
            ],
            scratch_shapes=[
                pltpu.SMEM((order.shape[0],), jnp.int32),
                pltpu.VMEM((HD, span), BF16),
                pltpu.VMEM((HD, heads * blk), F32),
                pltpu.VMEM((1, heads * blk), F32),
                pltpu.VMEM((1, heads * blk), F32),
            ],
        ),
        out_shape=[
            jax.ShapeDtypeStruct((rows, width), BF16),
            jax.ShapeDtypeStruct((row_blocks, 1, heads * blk), F32),
            jax.ShapeDtypeStruct((row_blocks, HD, heads * blk), BF16),
        ],
        compiler_params=pltpu.CompilerParams(vmem_limit_bytes=40 * 2**20),
        cost_estimate=pl.CostEstimate(flops=2**20, bytes_accessed=2**16, transcendentals=0),
        name="attend_forward",
    )(scalars, order, queries, cosine, sine, keys_values)


def attend_backward(group, blk, last, scal_ref, order_ref, qt_ref, g_ref, a_ref, lse_ref, cos_ref, sin_ref, kv_ref, *rest):
    if last:
        before_ref, dq_ref, mine_ref, other_ref, place_ref, gt_ref, qs_ref, gs_ref, kt_ref, acc_ref, delta_ref, dkv_ref = rest
    else:
        dq_ref, dkv_ref, place_ref, gt_ref, qs_ref, gs_ref, kt_ref, acc_ref, delta_ref = rest
    row_block = pl.program_id(0)
    own, length = scal_ref[0], scal_ref[1]

    @pl.when(row_block == 0)
    def _():
        block_places(order_ref, place_ref, own)
        for piece in range(order_ref.shape[0]):
            cells = slice(piece * blk, (piece + 1) * blk)
            kt_ref[:, cells] = kv_ref[cells, :HD].T
        dkv_ref[...] = before_ref[...] if last else jnp.zeros(dkv_ref.shape, F32)

    mine = row_position(order_ref, own, row_block)

    def step(place, masked):
        start = pl.multiple_of(place * blk, blk)
        scores = jnp.dot(kv_ref[pl.ds(start, blk), :HD], qt_ref[0], preferred_element_type=F32)
        weights = jnp.exp2(scores - lse_ref[0])
        if masked:
            weights = jnp.where(causal(blk, group), weights, 0.0)
        grads = jnp.dot(kv_ref[pl.ds(start, blk), HD:], gt_ref[...], preferred_element_type=F32)
        dscores = (weights * (grads - delta_ref[...])).astype(BF16)
        dkv_ref[pl.ds(start, blk), HD:] += jnp.dot(
            weights.astype(BF16), gs_ref[...], preferred_element_type=F32
        )
        dkv_ref[pl.ds(start, blk), :HD] += jnp.dot(dscores, qs_ref[...], preferred_element_type=F32)
        acc_ref[...] += jnp.dot(kt_ref[:, pl.ds(start, blk)], dscores, preferred_element_type=F32)

    @pl.when(mine * blk < length)
    def _():
        for head in range(group):
            lanes = slice(head * HD, (head + 1) * HD)
            cells = slice(head * blk, (head + 1) * blk)
            grad = g_ref[:, lanes]
            gt_ref[:, cells] = grad.T
            qs_ref[cells, :] = qt_ref[0, :, cells].T
            gs_ref[cells, :] = grad
            product = grad.astype(F32) * a_ref[:, lanes].astype(F32)
            delta_ref[:, cells] = jnp.sum(product.T, axis=0, keepdims=True)
        acc_ref[...] = jnp.zeros(acc_ref.shape, F32)
        step(place_ref[mine], True)

        def body(j, carried):
            step(place_ref[2 * j], False)
            step(place_ref[2 * j + 1], False)
            return carried

        lax.fori_loop(0, mine // 2, body, 0)

        @pl.when(mine % 2 == 1)
        def _():
            step(place_ref[mine - 1], False)

        cosine, sine = cos_ref[...], sin_ref[...]
        for head in range(group):
            turned = acc_ref[:, head * blk : (head + 1) * blk].astype(BF16).astype(F32)
            first, second = turned[:HALF], turned[HALF:]
            grad = jnp.concatenate(
                [first * cosine + second * sine, second * cosine - first * sine], axis=0
            )
            dq_ref[:, head * HD : (head + 1) * HD] = (grad * HD**-0.5).T.astype(BF16)

    @pl.when(mine * blk >= length)
    def _():
        dq_ref[...] = jnp.zeros(dq_ref.shape, BF16)

    if last:

        @pl.when(row_block == pl.num_programs(0) - 1)
        def _():
            half = mine_ref.shape[0]
            for total_ref, rows in ((mine_ref, slice(0, half)), (other_ref, slice(half, 2 * half))):
                total_ref[:, :HD] = (dkv_ref[rows, :HD] * LN2).astype(BF16)
                total_ref[:, HD:] = dkv_ref[rows, HD:].astype(BF16)


def attention_backward(scalars, order, turned, grads, attended, lse, cosine, sine, keys_values, blk, group, which, before=None):
    last = before is not None
    rows = grads.shape[0]
    span = keys_values.shape[0]
    row_blocks = rows // blk
    whole = pl.BlockSpec((span, 2 * HD), lambda i, *_: (0, 0))
    table = pl.BlockSpec((HALF, blk), lambda i, *_: (0, i))
    rowspec = pl.BlockSpec((blk, group * HD), lambda i, *_: (i, which))
    per_block = lambda *dims: pl.BlockSpec((1,) + dims, lambda i, *_: (i, 0, which))
    return pl.pallas_call(
        functools.partial(attend_backward, group, blk, last),
        grid_spec=pltpu.PrefetchScalarGridSpec(
            num_scalar_prefetch=2,
            grid=(row_blocks,),
            in_specs=[
                per_block(HD, group * blk),
                rowspec,
                rowspec,
                per_block(1, group * blk),
                table,
                table,
                whole,
            ]
            + [whole] * last,
            out_specs=[
                pl.BlockSpec((blk, group * HD), lambda i, *_: (i, 0)),
            ]
            + ([pl.BlockSpec((span // 2, 2 * HD), lambda i, *_: (0, 0))] * 2 if last else [whole]),
            scratch_shapes=[
                pltpu.SMEM((order.shape[0],), jnp.int32),
                pltpu.VMEM((HD, group * blk), BF16),
                pltpu.VMEM((group * blk, HD), BF16),
                pltpu.VMEM((group * blk, HD), BF16),
                pltpu.VMEM((HD, span), BF16),
                pltpu.VMEM((HD, group * blk), F32),
                pltpu.VMEM((1, group * blk), F32),
            ]
            + [pltpu.VMEM((span, 2 * HD), F32)] * last,
        ),
        out_shape=[
            jax.ShapeDtypeStruct((rows, group * HD), BF16),
        ]
        + (
            [jax.ShapeDtypeStruct((span // 2, 2 * HD), BF16)] * 2
            if last
            else [jax.ShapeDtypeStruct((span, 2 * HD), F32)]
        ),
        compiler_params=pltpu.CompilerParams(vmem_limit_bytes=48 * 2**20),
        cost_estimate=pl.CostEstimate(flops=2**20, bytes_accessed=2**16, transcendentals=0),
        name="attend_backward",
    )(scalars, order, turned, grads, attended, lse, cosine, sine, keys_values, *([before] if last else []))


def ffn_rows(count, tiles, place_ref, xa_ref, xb_ref, ga_ref, gb_ref, gate_ref, up_ref, down_ref, *rest):
    back_a, back_b, out_a, out_b, x_all, g_all, hidden_all, dgate_all, dup_all = rest[count:]
    units = gate_ref.shape[0] * gate_ref.shape[2]
    gate_rows, up_rows, down_rows = (ref[...].reshape(units, -1) for ref in (gate_ref, up_ref, down_ref))
    nt = (((1,), (1,)), ((), ()))
    early = pl.program_id(0) < tiles
    x = jnp.where(early, xa_ref[...], xb_ref[...])
    grad = jnp.where(early, ga_ref[...], gb_ref[...])
    gate = lax.dot_general(x, gate_rows, nt, preferred_element_type=F32)
    up = lax.dot_general(x, up_rows, nt, preferred_element_type=F32)
    dhidden = lax.dot_general(grad, down_rows, nt, preferred_element_type=F32)
    dhidden = dhidden.astype(BF16).astype(F32)
    sigmoid = jax.nn.sigmoid(gate)
    silu = gate * sigmoid
    hidden = (silu * up).astype(BF16)
    dgate = (dhidden * up * sigmoid * (1.0 + gate * (1.0 - sigmoid))).astype(BF16)
    dup = (dhidden * silu).astype(BF16)
    out = jnp.dot(hidden, down_rows, preferred_element_type=F32).astype(BF16)
    step = 512 if x.shape[1] % 512 == 0 else x.shape[1]
    back = jnp.concatenate(
        [
            (
                jnp.dot(dgate, gate_rows[:, at_col : at_col + step], preferred_element_type=F32)
                + jnp.dot(dup, up_rows[:, at_col : at_col + step], preferred_element_type=F32)
            ).astype(BF16)
            for at_col in range(0, x.shape[1], step)
        ],
        axis=1,
    )
    x_all[...] = x
    g_all[...] = grad
    hidden_all[...] = hidden
    dgate_all[...] = dgate
    dup_all[...] = dup

    @pl.when(early)
    def _():
        back_a[...] = back
        out_a[...] = out

    @pl.when(jnp.logical_not(early))
    def _():
        back_b[...] = back
        out_b[...] = out


def ffn_pair(place, pairs, xa, xb, ga, gb, weights, kept):
    rows, model_dim = xa.shape
    planes, _, share, _ = weights.shape
    units = planes * share
    tile = min(256, rows)
    tiles = rows // tile
    weight = lambda which: pl.BlockSpec(
        (planes, 1, share, model_dim), lambda i, *_: (0, which, 0, 0), pipeline_mode=pl.Buffered(1)
    )
    turn_a = lambda i: jnp.minimum(i, tiles - 1)
    turn_b = lambda i: jnp.maximum(i - tiles, 0)
    block = lambda index: pl.BlockSpec((tile, model_dim), index)
    here_a, here_b = block(lambda i, *_: (turn_a(i), 0)), block(lambda i, *_: (turn_b(i), 0))
    out_a = block(lambda i, place_ref: (place_ref[0] * tiles + turn_a(i), 0))
    out_b = block(lambda i, place_ref: (place_ref[0] * tiles + turn_b(i), 0))
    there = lambda wide: pl.BlockSpec((tile, wide), lambda i, place_ref: (place_ref[0] * 2 * tiles + i, 0))
    count = len(kept)
    shape = lambda tall, wide: jax.ShapeDtypeStruct((tall, wide), BF16)
    return pl.pallas_call(
        functools.partial(ffn_rows, count, tiles),
        grid_spec=pltpu.PrefetchScalarGridSpec(
            num_scalar_prefetch=1,
            grid=(2 * tiles,),
            in_specs=[here_a, here_b, here_a, here_b, weight(0), weight(1), weight(2)]
            + [pl.BlockSpec(memory_space=pl.ANY)] * count,
            out_specs=[here_a, here_b, out_a, out_b] + [there(model_dim)] * 2 + [there(units)] * 3,
        ),
        out_shape=[shape(rows, model_dim)] * 2
        + [shape(pairs * rows, model_dim)] * 2
        + [shape(pairs * 2 * rows, model_dim)] * 2
        + [shape(pairs * 2 * rows, units)] * 3,
        input_output_aliases={8 + i: 2 + i for i in range(count)},
        compiler_params=pltpu.CompilerParams(vmem_limit_bytes=60 * 2**20),
        cost_estimate=pl.CostEstimate(flops=2**20, bytes_accessed=2**16, transcendentals=0),
        name="ffn_pair",
    )(place, xa, xb, ga, gb, weights, weights, weights, *kept)


def pack_columns(*refs):
    out_ref = refs[-1]
    columns = out_ref.shape[3]
    for which, in_ref in enumerate(refs[:-1]):
        for place in range(out_ref.shape[0]):
            out_ref[place, which] = in_ref[:, place * columns : (place + 1) * columns]


def pack_units(terms, places):
    share, columns = terms[0].shape
    if share % 16:
        return jnp.stack(terms).reshape(len(terms), share, places, columns // places).transpose(2, 0, 1, 3)
    return pl.pallas_call(
        pack_columns,
        out_shape=jax.ShapeDtypeStruct((places, len(terms), share, columns // places), BF16),
        compiler_params=pltpu.CompilerParams(vmem_limit_bytes=32 * 2**20),
        cost_estimate=pl.CostEstimate(flops=2**16, bytes_accessed=len(terms) * terms[0].size * 4, transcendentals=0),
        name="pack_units",
    )(*terms)


def turn_rows(in_ref, *out_refs):
    for which, out_ref in enumerate(out_refs):
        out_ref[...] = in_ref[:, which].reshape(out_ref.shape[1], out_ref.shape[0]).T.astype(F32)


def turn_units(terms):
    places, count, share, columns = terms.shape
    if share % 16:
        turned = terms.transpose(1, 3, 0, 2).reshape(count, columns, places * share).astype(F32)
        return [turned[which] for which in range(count)]
    return pl.pallas_call(
        turn_rows,
        out_shape=[jax.ShapeDtypeStruct((columns, places * share), F32)] * count,
        compiler_params=pltpu.CompilerParams(vmem_limit_bytes=32 * 2**20),
        cost_estimate=pl.CostEstimate(flops=2**20, bytes_accessed=terms.size * 6, transcendentals=0),
        name="turn_units",
    )(terms)


def alternate_columns(part, first_ref, second_ref, out_ref):
    for at_col in range(0, first_ref.shape[1], part):
        out_ref[:, 2 * at_col : 2 * at_col + part] = first_ref[:, at_col : at_col + part]
        out_ref[:, 2 * at_col + part : 2 * at_col + 2 * part] = second_ref[:, at_col : at_col + part]


def alternate(first, second, part):
    rows, width = first.shape
    return pl.pallas_call(
        functools.partial(alternate_columns, part),
        out_shape=jax.ShapeDtypeStruct((rows, 2 * width), F32),
        cost_estimate=pl.CostEstimate(flops=2**16, bytes_accessed=first.size * 16, transcendentals=0),
        name="alternate",
    )(first, second)


def sum_chips(plane_ref, dealt_ref, *out_refs):
    rows = out_refs[0].shape[1]
    for k, out_ref in enumerate(out_refs):
        start = pl.multiple_of((plane_ref[0] ^ k) * rows, rows)
        for core in range(2):
            total = dealt_ref[core, pl.ds(start, rows), :].astype(F32)
            for place in range(2 + core, dealt_ref.shape[0], 2):
                total = total + dealt_ref[place, pl.ds(start, rows), :].astype(F32)
            out_ref[core] = total.astype(BF16)


def split_planes(dealt, plane, planes):
    rows, columns = dealt.shape[1] // planes, dealt.shape[2]
    return pl.pallas_call(
        sum_chips,
        grid_spec=pltpu.PrefetchScalarGridSpec(
            num_scalar_prefetch=1,
            grid=(1,),
            in_specs=[pl.BlockSpec(dealt.shape, lambda i, *_: (0, 0, 0), pipeline_mode=pl.Buffered(1))],
            out_specs=[pl.BlockSpec((2, rows, columns), lambda i, *_: (0, 0, 0))] * planes,
        ),
        out_shape=[jax.ShapeDtypeStruct((2, rows, columns), BF16)] * planes,
        compiler_params=pltpu.CompilerParams(vmem_limit_bytes=60 * 2**20),
        cost_estimate=pl.CostEstimate(flops=2**20, bytes_accessed=dealt.size * 3, transcendentals=0),
        name="sum_chips",
    )(plane.reshape(1).astype(jnp.int32), dealt)


def angles(positions):
    frequency = ROPE_BASE ** (-2.0 * jnp.arange(HALF, dtype=F32) / HD)
    phase_angle = frequency[:, None] * positions.astype(F32)[None, :]
    return (jnp.cos(phase_angle), jnp.sin(phase_angle))


def rotate(vectors, cosine, sine_vals):
    first_half = vectors[..., :HALF]
    second_half = vectors[..., HALF:]
    return jnp.concatenate(
        [
            first_half * cosine - second_half * sine_vals,
            second_half * cosine + first_half * sine_vals,
        ],
        axis=-1,
    )


def matmul(left, right):
    return jnp.dot(left, right, preferred_element_type=F32)


def contract_rows(left, right):
    return lax.dot_general(left, right, (((0,), (0,)), ((), ())), preferred_element_type=F32)


def contract_cols(left, right):
    return lax.dot_general(left, right, (((1,), (1,)), ((), ())), preferred_element_type=F32)


def after(value, *earlier):
    return lax.optimization_barrier((value, earlier))[0]


def exchange(value, axis, distance):
    size = lax.axis_size(axis)
    return lax.ppermute(value, axis, [(i, i ^ distance) for i in range(size)])


def swap_core(value):
    return exchange(value, "core", 1)


def spread_chips(value):
    chips = lax.axis_size("chip")
    copies = jnp.broadcast_to(value[None], (chips,) + value.shape)
    return lax.all_to_all(copies, "chip", 0, 0, tiled=False)


def gather_near(value):
    if lax.axis_size("chip") != 4:
        return [value] + [exchange(value, "chip", k) for k in range(1, lax.axis_size("chip"))]
    return [value, exchange(value, "chip", 1), exchange(value, "chip", 2)]


def send_far(near):
    if lax.axis_size("chip") != 4:
        return ()
    value, first, second = lax.optimization_barrier(near)
    half = value.shape[0] // 2
    first, second = lax.optimization_barrier((first[:half], second[half:]))
    return exchange(first, "chip", 2), exchange(second, "chip", 1)


def gather_far(near):
    halves = lax.optimization_barrier(send_far(near))
    return near + [jnp.concatenate(halves, axis=0)] if halves else near


def gather_chips(value):
    return gather_far(gather_near(value))


def add_cores(terms, terms_of_other):
    return (terms.astype(F32) + swap_core(terms_of_other.astype(BF16)).astype(F32)).astype(BF16)


def deal(terms, axis):
    dealt = lax.all_to_all(terms.astype(BF16), axis, 0, 0, tiled=False)
    return jnp.sum(dealt.astype(F32), axis=0)


def at(value, index, axis=0):
    return lax.dynamic_index_in_dim(value, index, axis, keepdims=False)


def sum_planes(terms, plane):
    total = at(terms, plane).astype(F32)
    for k in range(1, lax.axis_size("fsdp")):
        total = total + exchange(at(terms, plane ^ k).astype(BF16), "fsdp", k).astype(F32)
    return total


def reduce_far(last):
    half = last.shape[0] // 2
    return exchange(last[:half], "chip", 1), exchange(last[half:], "chip", 2)


def add_half(term, passing, which):
    pad = term.shape[0] - passing.shape[0]
    passing = jnp.pad(passing, ((pad, 0) if which else (0, pad), (0, 0)))
    return (term.astype(F32) + passing.astype(F32)).astype(BF16)


def lay_columns(chunks, chip):
    rows, width = chunks[0].shape
    whole = jnp.zeros((rows, width * len(chunks)), chunks[0].dtype)
    for k, chunk in enumerate(chunks):
        whole = lax.dynamic_update_slice(whole, chunk, (0, (chip ^ k) * width))
    return whole


def shards(
    tokens,
    cotangent,
    kv_cotangent,
    lengths,
    block_order,
    w_query,
    w_kv,
    w_out,
    gain_attn,
    gain_ffn,
    w_gate,
    w_up,
    w_down,
):
    local_len, model_dim = tokens.shape[1:]
    chips, planes = lax.axis_size("chip"), lax.axis_size("fsdp")
    chip, core, plane = lax.axis_index("chip"), lax.axis_index("core"), lax.axis_index("fsdp")
    own = chip * 2 + core
    places = chips * 2
    blk = local_len // 2
    order, length = block_order[0], lengths[0]
    depth = w_query.shape[0]

    part = depth // 2
    wide = part * planes
    out_cols = model_dim // chips
    kv_rows = depth // chips
    gain_rows = depth // (2 * HD)
    narrow = lambda value: value.reshape(-1, 2 * HD)
    pieces = [
        lax.dynamic_slice(w_query, (0, chip * 2 * part + core * part), (depth, part)),
        lax.dynamic_slice(w_out, (core * part, chip * out_cols), (part, out_cols)),
        lax.dynamic_slice_in_dim(w_kv, chip * kv_rows, kv_rows, 0),
        gain_attn,
        gain_ffn,
    ]
    heights = [piece.size // (2 * HD) for piece in pieces]
    packed = jnp.concatenate([narrow(piece) for piece in pieces], axis=0)
    packed = lax.all_gather(packed, "fsdp", axis=0)
    bounds = [sum(heights[: i + 1]) for i in range(4)]
    query_piece, out_piece, kv_piece, gain_one, gain_two = jnp.split(packed, bounds, axis=1)
    out_piece = out_piece.reshape(wide, out_cols)
    gain_one = gain_one.reshape(model_dim).astype(F32)
    gain_two = gain_two.reshape(model_dim).astype(F32)
    share = w_gate.shape[1] // places
    pieces = jnp.stack(
        [
            lax.dynamic_slice(weight, (0, own * share), (model_dim, share)).T
            for weight in (w_gate, w_up, w_down)
        ]
    )
    query_piece = query_piece.reshape(model_dim, part)
    own_pos = jnp.repeat(lax.dynamic_slice_in_dim(order, own * 2, 2, 0) * blk, blk) + (
        jnp.arange(local_len, dtype=jnp.int32) % blk
    )
    live_rows = (own_pos < length)[:, None]
    grad_out = jnp.where(live_rows, cotangent[0], jnp.zeros((), BF16))
    grad_near = after(gather_near(grad_out), pieces)
    kv_full = spread_chips(after(kv_piece, grad_near)).swapaxes(0, 1).reshape(model_dim, 2 * HD)
    kv_full = with_layout_constraint(kv_full, Layout((0, 1)))
    query_near = gather_near(after(query_piece, grad_near))
    query_half = lay_columns(gather_far(query_near), chip)
    grad_others = [swap_core(chunk) for chunk in after(grad_near, query_near)]
    grad_far = send_far(after(grad_near, query_half, grad_others))
    out_chunks = spread_chips(after(out_piece, query_half))
    ffn_weights = lax.all_gather(pieces, "fsdp", axis=0)

    offsets = jnp.arange(blk, dtype=jnp.int32)
    mine = lax.dynamic_slice_in_dim(order, own * 2, 2, 0)
    theirs = lax.dynamic_slice_in_dim(order, (own ^ 1) * 2, 2, 0)
    both_pos = (jnp.concatenate([mine, theirs])[:, None] * blk + offsets[None, :]).reshape(-1)
    cosine, sine_vals = angles(both_pos)
    own_cosine, own_sine = cosine[:, :local_len].T, sine_vals[:, :local_len].T

    tokens_low = tokens[0]
    tokens_flat = tokens_low.astype(F32)
    both_tokens = jnp.concatenate([tokens_low, swap_core(tokens_low)], axis=0).astype(F32)
    both_inverse = lax.rsqrt(jnp.mean(both_tokens * both_tokens, axis=1, keepdims=True) + EPSILON)
    both_normed = (both_tokens * both_inverse * gain_one).astype(BF16)
    inverse_one = both_inverse[:local_len]

    key_value = matmul(both_normed[:local_len], kv_full)
    key_rot = rotate(key_value[:, :HD], own_cosine, own_sine)
    local_kv = jnp.concatenate([key_rot, key_value[:, HD:]], axis=1).astype(BF16)
    slot_kv = after(spread_chips(local_kv), query_half).reshape(-1, 2 * HD)
    slot_kv = jnp.concatenate([slot_kv, swap_core(slot_kv)], axis=0)

    heads = wide // HD
    queries = matmul(both_normed, query_half)
    scalars = jnp.stack([own, length]).astype(jnp.int32)
    attended, lse, turned = attention_forward(
        scalars, order, queries, cosine, sine_vals, slot_kv, blk
    )

    attended, lse, turned, out_chunks, grad_far = lax.optimization_barrier(
        (attended, lse, turned, out_chunks, grad_far)
    )
    grad_mine = list(grad_near)
    if grad_far:
        grad_mine.append(jnp.concatenate(grad_far, axis=0))
        grad_others.append(swap_core(grad_mine[3]))
    out_half = out_chunks.swapaxes(0, 1).reshape(wide, model_dim)
    branch_other = swap_core(matmul(attended[local_len:], out_half).astype(BF16))
    residual = tokens_flat + matmul(attended[:local_len], out_half) + branch_other.astype(F32)
    inverse_two = lax.rsqrt(jnp.mean(residual * residual, axis=1, keepdims=True) + EPSILON)
    unit_two = residual * inverse_two
    normed_ffn = (unit_two * gain_two).astype(BF16)
    def pair(at_place, chunk, kept):
        result = ffn_pair(
            jnp.full((1,), at_place, jnp.int32),
            chips,
            chunk,
            swap_core(chunk),
            grad_mine[at_place],
            grad_others[at_place],
            ffn_weights,
            kept,
        )
        return result[0], result[1], tuple(result[2:])

    normed_near = gather_near(normed_ffn)
    back_own, back_other, kept = pair(0, normed_near[0], ())
    back_other = swap_core(back_other)
    if chips == 4:
        normed_near = after(normed_near, back_own)
        normed_far = send_far(normed_near)
        own_first, other_first, kept = pair(1, normed_near[1], kept)
        normed_far = after(normed_far, own_first)
        own_last, other_last, kept = pair(3, jnp.concatenate(normed_far, axis=0), kept)
        last = add_cores(own_last, other_last)
        other_first = swap_core(other_first)
        kept = after(kept, last, other_first)
        passing = reduce_far(last)
        own_second, other_second, kept = pair(2, normed_near[2], kept)
        passing, own_second, other_second, kept = lax.optimization_barrier(
            (passing, own_second, other_second, kept)
        )
        first = add_half(own_first.astype(F32) + other_first.astype(F32), passing[1], 1)
        second = add_half(own_second.astype(F32) + swap_core(other_second).astype(F32), passing[0], 0)
        kept = after(kept, first, second)
        arrived = [exchange(first, "chip", 1), exchange(second, "chip", 2), back_other]
    else:
        normed_chunks = gather_far(after(normed_near, back_own))
        arrived = [back_other]
        for k in range(1, chips):
            own_term, other_term, kept = pair(k, normed_chunks[k], kept)
            arrived.append(exchange(add_cores(own_term, other_term), "chip", k))

    out_own, out_other, normed_all, grad_all, hidden_all, dgate_all, dup_all = kept
    down_term = contract_rows(hidden_all, grad_all).astype(BF16)
    out_other = swap_core(out_other)
    cuts = [0, 1, 2, 3, 3.5, 4] if chips == 4 else range(chips + 1)
    out_parts = [
        (out_own[int(a * local_len) : int(b * local_len)].astype(F32) + out_other[int(a * local_len) : int(b * local_len)].astype(F32)).astype(BF16)
        for a, b in zip(cuts[:-1], cuts[1:])
    ]
    gate_term = contract_rows(dgate_all, normed_all).astype(BF16)
    arrived = after(arrived, down_term, out_parts, gate_term)
    grad_normed = back_own.astype(F32)
    for term in arrived:
        grad_normed = grad_normed + term.astype(F32)
    out_parts = after(out_parts, arrived)

    def over_planes(term):
        return lax.psum_scatter(term, "fsdp", scatter_dimension=0, tiled=True)

    gate_term, down_term = over_planes(gate_term), over_planes(down_term)

    grad_gain_two = jnp.sum(grad_normed * unit_two, axis=0)
    scaled_two = grad_normed * gain_two
    grad_residual = grad_out.astype(F32) + inverse_two * (
        scaled_two - unit_two * jnp.mean(scaled_two * unit_two, axis=1, keepdims=True)
    )
    grad_branch = grad_residual.astype(BF16)
    both_branch = jnp.concatenate([grad_branch, swap_core(grad_branch)], axis=0)
    grad_attn = contract_cols(both_branch, out_half).astype(BF16)
    branch_terms = contract_rows(attended, both_branch).astype(BF16)
    branch_terms = branch_terms.reshape(planes, part, model_dim)
    grad_attn = after(grad_attn, branch_terms)
    group = heads // 2

    def backward(grads, which, before=None):
        return attention_backward(
            scalars, order, turned, grads, attended, lse, cosine, sine_vals, slot_kv, blk, group, which, before
        )

    def deal_rows(terms):
        return lax.all_to_all(terms.reshape(places, planes * (depth // places), -1), ("chip", "core"), 0, 0, tiled=False)

    branch_dealt = lax.all_to_all(branch_terms, "chip", 0, 0, tiled=False)
    up_term = contract_rows(*after((dup_all, normed_all), branch_terms)).astype(BF16)
    if chips == 4:
        out_passing = exchange(out_parts[3], "chip", 1), exchange(out_parts[4], "chip", 2)
    else:
        out_passing = ()
    grad_query_a, kv_terms_a = backward(after(grad_attn, up_term), 0)
    grad_query_a, kv_terms_a, out_passing, branch_dealt = lax.optimization_barrier(
        (grad_query_a, kv_terms_a, out_passing, branch_dealt)
    )
    branch_sum = jnp.sum(branch_dealt.astype(F32), axis=0)
    query_terms_a = contract_rows(both_normed, grad_query_a).astype(BF16)
    if chips == 4:
        out_near = (add_half(out_parts[1], out_passing[1], 1), add_half(out_parts[2], out_passing[0], 0))
    else:
        out_near = tuple(out_parts[k] for k in range(1, chips))
    branch_sum = branch_sum.reshape(planes, part // planes, model_dim)
    grad_query_b, kv_mine, kv_other = backward(
        after(grad_attn, out_near, query_terms_a, branch_sum), 1, kv_terms_a
    )
    out_arrived = [exchange(term, "chip", k + 1) for k, term in enumerate(out_near)]
    grad_w_out = sum_planes(branch_sum, plane)
    query_sums_a = deal_rows(query_terms_a)
    ffn_terms = [gate_term, over_planes(up_term), down_term]
    grad_query_b, kv_mine, kv_other, out_arrived, grad_w_out, ffn_terms, query_sums_a = lax.optimization_barrier(
        (grad_query_b, kv_mine, kv_other, out_arrived, grad_w_out, ffn_terms, query_sums_a)
    )
    kv_parts = with_layout_constraint(add_cores(kv_mine, kv_other), Layout((0, 1)))
    kv_parts = kv_parts.reshape(chips, local_len, 2 * HD)
    kv_parts = [with_layout_constraint(at(kv_parts, chip ^ k), Layout((0, 1))) for k in range(chips)]
    kv_arrived = [exchange(kv_parts[k], "chip", k) for k in range(1, chips)]
    out_arrived, ffn_terms, grad_query_b, query_sums_a = after(
        (out_arrived, ffn_terms, grad_query_b, query_sums_a), kv_parts
    )
    query_terms_b = contract_rows(both_normed, grad_query_b).astype(BF16)
    kv_arrived = after(kv_arrived, query_terms_b)
    ffn_terms = pack_units(after(ffn_terms, query_sums_a), places)
    ffn_terms = lax.all_to_all(after(ffn_terms, kv_arrived), ("chip", "core"), 0, 0, tiled=False)
    kv_total = kv_parts[0].astype(F32)
    for term in kv_arrived:
        kv_total = kv_total + term.astype(F32)
    kv_total = kv_total + jnp.where(live_rows, kv_cotangent[0].astype(F32), 0.0)
    kv_low = kv_total.astype(BF16).astype(F32)
    grad_key = rotate(kv_low[:, :HD], own_cosine, -own_sine)
    grad_kv = jnp.concatenate([grad_key, kv_low[:, HD:]], axis=1).astype(BF16)
    both_grad_kv = jnp.concatenate([grad_kv, swap_core(grad_kv)], axis=0)
    kv_half = lax.dynamic_slice_in_dim(both_grad_kv, core * HD, HD, 1)
    kv_weight_half = lax.dynamic_slice_in_dim(kv_full, core * HD, HD, 1)
    rows = depth // places
    first_row = (own * planes + plane) * rows
    other_row = ((own ^ 1) * planes + plane) * rows
    kept_rows = lax.dynamic_slice_in_dim(query_half, first_row, rows, 0)
    sent_rows = swap_core(lax.dynamic_slice_in_dim(query_half, other_row, rows, 0))
    own_query_rows = jnp.where(
        core == 0, jnp.stack([kept_rows, sent_rows]), jnp.stack([sent_rows, kept_rows])
    )
    own_kv_rows = lax.dynamic_slice_in_dim(kv_full, first_row, rows, 0)
    both_query = jnp.concatenate([grad_query_a, grad_query_b], axis=1)

    def normed_one_term(rows):
        return contract_cols(both_query[rows], query_half) + contract_cols(kv_half[rows], kv_weight_half)

    gains = jnp.pad(grad_gain_two[:, None], ((0, 0), (0, HD - 1)))
    kv_grads = jnp.concatenate([contract_rows(both_normed, kv_half), gains], axis=1).astype(BF16)
    last_terms = jnp.concatenate([query_terms_b, kv_grads], axis=1)
    last_terms = with_layout_constraint(last_terms, Layout((0, 1)))
    last_dealt = deal_rows(after(last_terms, ffn_terms))
    first_planes = split_planes(after(query_sums_a, last_terms), plane, planes)
    first_arrived = [exchange(first_planes[k], "fsdp", k) for k in range(1, planes)]
    both_query = after(both_query, last_terms)
    other_one = swap_core(normed_one_term(slice(local_len, None)).astype(BF16))

    grad_normed_one = normed_one_term(slice(0, local_len)) + other_one.astype(F32)
    unit_one = tokens_flat * inverse_one
    scaled_one = grad_normed_one * gain_one
    grad_tokens = grad_residual + inverse_one * (
        scaled_one - unit_one * jnp.mean(scaled_one * unit_one, axis=1, keepdims=True)
    )
    grad_tokens = grad_tokens.astype(BF16)
    out_arrived = after(out_arrived, last_terms)
    ffn_out = out_parts[0].astype(F32)
    for term in out_arrived:
        ffn_out = ffn_out + term.astype(F32)
    output = jnp.where(live_rows, residual + ffn_out, 0.0).astype(BF16)

    ffn_grads = turn_units(after(ffn_terms, last_terms))
    last_dealt = after(last_dealt, grad_tokens, output, ffn_grads)
    last_planes = split_planes(last_dealt, plane, planes)
    last_arrived = [exchange(last_planes[k], "fsdp", k) for k in range(1, planes)]
    query_sums_a = first_planes[0].astype(F32)
    for term in after(first_arrived, last_planes[0]):
        query_sums_a = query_sums_a + term.astype(F32)
    last_sums = last_planes[0].astype(F32)
    for term in last_arrived:
        last_sums = last_sums + term.astype(F32)
    query_sums = jnp.concatenate([query_sums_a, last_sums[:, :, : -2 * HD]], axis=2)
    kv_sums = last_sums[:, :, -2 * HD :]

    own_gain = lax.dynamic_slice_in_dim(gain_one, first_row, rows, 0)
    grad_gain_one = (
        jnp.sum(own_query_rows.astype(F32) * query_sums, axis=(0, 2))
        + jnp.sum(own_kv_rows.astype(F32) * jnp.concatenate([kv_sums[0, :, :HD], kv_sums[1, :, :HD]], axis=1), axis=1)
    ) / own_gain
    grad_gain_two = kv_sums[0, :, HD] + kv_sums[1, :, HD]
    grad_w_query = alternate(query_sums[0], query_sums[1], part)
    grad_w_kv = jnp.concatenate([kv_sums[0, :, :HD], kv_sums[1, :, :HD]], axis=1)
    return (
        output[None],
        grad_tokens.astype(BF16)[None],
        grad_w_query,
        grad_w_kv,
        grad_w_out,
        grad_gain_one,
        grad_gain_two,
        ffn_grads[0],
        ffn_grads[1],
        ffn_grads[2],
    )


def solution(mesh):
    ctx, planes = mesh.shape["ctx"], mesh.shape["fsdp"]
    split = Mesh(mesh.devices.reshape(ctx // 2, 2, planes), ("chip", "core", "fsdp"))
    ctx_axes = ("chip", "core")
    return jax.shard_map(
        shards,
        mesh=split,
        in_specs=(
            P("fsdp", ctx_axes, None),
            P("fsdp", ctx_axes, None),
            P("fsdp", ctx_axes, None),
            P("fsdp"),
            P("fsdp", None),
            P("fsdp", None),
            P("fsdp", None),
            P("fsdp", None),
            P("fsdp"),
            P("fsdp"),
            P(None, "fsdp"),
            P(None, "fsdp"),
            P(None, "fsdp"),
        ),
        out_specs=(
            P("fsdp", ctx_axes, None),
            P("fsdp", ctx_axes, None),
            P(("chip", "core", "fsdp"), None),
            P(("chip", "core", "fsdp"), None),
            P(("chip", "core", "fsdp"), None),
            P(("chip", "core", "fsdp")),
            P(("chip", "core", "fsdp")),
            P(ctx_axes, "fsdp"),
            P(ctx_axes, "fsdp"),
            P(ctx_axes, "fsdp"),
        ),
        check_vma=False,
    )
```
